32 devices in a mesh: dp: 8 (over z, y), mp: 4 (over x, core).
Axes of the slice: x: 2, y: 2, z: 4, core: 2. Of those that a mesh axis runs over, the one named last changes fastest.
Arguments:
- tokens: bfloat16 [16384, 768], P(('dp', 'mp')), may hold values from -6 to 6
- w_query: bfloat16 [768, 768], P('dp', 'mp'), may hold values from -0.109375 to 0.109375
- w_key: bfloat16 [768, 768], P('dp', 'mp'), may hold values from -0.109375 to 0.109375
- w_value: bfloat16 [768, 768], P('dp', 'mp'), may hold values from -0.21875 to 0.21875
- w_out: bfloat16 [768, 768], P('dp', 'mp'), may hold values from -0.625 to 0.625
- w_gate: bfloat16 [768, 2048], P('dp', 'mp'), may hold values from -0.21875 to 0.21875
- w_up: bfloat16 [768, 2048], P('dp', 'mp'), may hold values from -0.21875 to 0.21875
- w_down: bfloat16 [768, 2048], P('dp', 'mp'), may hold values from -0.125 to 0.125
- norm_attn: float32 [768], replicated, may hold values from 0.5 to 1.5
- norm_mlp: float32 [768], replicated, may hold values from 0.5 to 1.5
- valid_counts: int32 [8], P('dp'), may hold values from 512 to 2048
- group_ids: int32 [8, 2048], P('dp'), may hold values from 0 to 3, never falling along the last dimension, each value on 1 to 1024 neighbouring positions
- cotangent: bfloat16 [16384, 768], P(('dp', 'mp')), may hold values from -6 to 6
Outputs:
- output: bfloat16 [16384, 768], P(('dp', 'mp'))
- grad_tokens: bfloat16 [16384, 768], P(('dp', 'mp'))
- grad_query: float32 [768, 768], P('dp', 'mp')
- grad_key: float32 [768, 768], P('dp', 'mp')
- grad_value: float32 [768, 768], P('dp', 'mp')
- grad_out: float32 [768, 768], P('dp', 'mp')
- grad_gate: float32 [768, 2048], P('dp', 'mp')
- grad_up: float32 [768, 2048], P('dp', 'mp')
- grad_down: float32 [768, 2048], P('dp', 'mp')
- grad_norm_attn: float32 [768], replicated
- grad_norm_mlp: float32 [768], replicated
The draws below stay inside these ranges and needn't reach their ends.
Inputs may be any that keep to these rules, and one draw needn't show every extreme that they name: `group_ids`: in each image the ids never fall, start at 0 and reach 3; each group has 1 to 1024 patches.
All inputs are finite; a program needn't handle non-finite values.
Results may differ from the reference program's by a relative error of at most 0.02.
Values may be sent and summed in bfloat16 or wider, within the bound.
No kernel may reach another device: no remote copies, remote signals or barrier semaphores. Data moves between devices by JAX's collectives and lax.ppermute only.
A program may use at most 128 MiB of HBM per device.

```python
import math
import jax
import jax.numpy as jnp
import numpy as np
from jax import lax

D = 768
HEAD = 64
FF = 2048
PATCHES = 2048
BLOCK = 512
GROUPS = 4
SEQS = 8
TOKENS = 16384
N_MP = 4


def touch_ends(entries, own_key, least, largest):
    longest = entries.shape.index(max(entries.shape))
    spots = []
    for shift in (0, 1):
        where = [jax.random.randint(jax.random.fold_in(own_key, axis), (), 0, length) for axis, length in enumerate(entries.shape)]
        where[longest] = (where[longest] + shift) % entries.shape[longest]
        spots.append(tuple(where))
    return entries.at[spots[0]].set(least).at[spots[1]].set(largest)


def shard_levels(own_key, shape, split, smallest, top_value):
    def one(axis_at, blocks):
        steps = jax.random.uniform(jax.random.fold_in(jax.random.fold_in(own_key, 6), axis_at), (blocks,), jnp.float32, smallest / len(split), top_value / len(split))
        return jnp.repeat(jnp.exp(steps), shape[axis_at] // blocks).reshape((-1,) + (1,) * (len(shape) - axis_at - 1))

    level = one(*split[0])
    for cut in split[1:]:
        level = level * one(*cut)
    return level


def profile(amount, total, limit, skew):
    weights = [(1 << 20) // math.isqrt(standing ** skew) + 1 for standing in range(2, amount + 1)]
    surplus, holding = total - limit - (amount - 1), [1] * (amount - 1)
    while surplus > 0:
        movable = [i for i in range(amount - 1) if holding[i] < limit]
        whole, left = sum([weights[i] for i in movable]), surplus
        for i in movable:
            more = min(limit - holding[i], max(1, left * weights[i] // whole), surplus)
            holding[i] = holding[i] + more
            surplus = surplus - more
    return np.array([limit] + holding)


def ragged(rng, number_of, total, limit, lean):
    if number_of == 2:
        one = jax.random.randint(rng, (), max(1, total - limit), min(limit, total - 1) + 1)
        return jnp.stack([one, total - one])
    lengths = jnp.asarray(profile(number_of, total, limit, lean), jnp.int32)
    twos = (number_of - 1) // 2
    source_of, receiver = lengths[1:1 + 2 * twos:2], lengths[2:2 + 2 * twos:2]
    margin = jnp.minimum(source_of - 1, limit - receiver)
    moved = jax.random.randint(jax.random.fold_in(rng, 1), (twos,), 0, 1 << 20) % (margin + 1)
    lengths = lengths.at[1:1 + 2 * twos:2].set(source_of - moved).at[2:2 + 2 * twos:2].set(receiver + moved)
    return lengths[jax.random.permutation(jax.random.fold_in(rng, 2), number_of)]


def normal_values(key, extent, scale, most, cuts=(), kind=jnp.bfloat16):
    entries = scale * jax.random.normal(key, extent, jnp.float32)
    if cuts:
        entries = entries * shard_levels(key, extent, cuts, -0.22, 0.18)
    return jnp.clip(entries, -most, most).astype(kind)


def setup_inputs(seed: int = 0) -> dict:
    key_list = jax.random.split(jax.random.key(seed), 14)
    tokens = normal_values(key_list[0], (TOKENS, D), 1.0, 6.0, ((0, 32),))
    w_query = normal_values(key_list[1], (D, D), (4 * D) ** -0.5, 0.109375, ((0, 8), (1, 4)))
    w_key = normal_values(key_list[2], (D, D), (4 * D) ** -0.5, 0.109375, ((0, 8), (1, 4)))
    w_value = normal_values(key_list[3], (D, D), D ** -0.5, 0.21875, ((0, 8), (1, 4)))
    w_out = normal_values(key_list[4], (D, D), (D // 8) ** -0.5, 0.625, ((0, 8), (1, 4)))
    w_gate = normal_values(key_list[5], (D, FF), D ** -0.5, 0.21875, ((0, 8), (1, 4)))
    w_up = normal_values(key_list[6], (D, FF), D ** -0.5, 0.21875, ((0, 8), (1, 4)))
    w_down = normal_values(key_list[7], (D, FF), FF ** -0.5, 0.125, ((0, 8), (1, 4)))
    norm_attn = jnp.clip(1.0 + 0.1 * jax.random.normal(key_list[8], (D,), jnp.float32), 0.5, 1.5)
    norm_mlp = jnp.clip(1.0 + 0.1 * jax.random.normal(key_list[9], (D,), jnp.float32), 0.5, 1.5)
    valid_counts = touch_ends(jax.random.randint(key_list[10], (SEQS,), PATCHES // 4, PATCHES + 1), jax.random.fold_in(key_list[10], 1), PATCHES // 4, PATCHES).astype(jnp.int32)
    group_ids = jax.vmap(lambda own: jnp.searchsorted(jnp.cumsum(ragged(own, GROUPS, PATCHES, PATCHES // 2, 1)), jnp.arange(PATCHES), side="right"))(jax.random.split(key_list[11], SEQS)).reshape((SEQS, PATCHES)).astype(jnp.int32)
    cotangent = normal_values(key_list[12], (TOKENS, D), 1.0, 6.0, ((0, 32),))
    return {"tokens": tokens, "w_query": w_query, "w_key": w_key, "w_value": w_value, "w_out": w_out, "w_gate": w_gate, "w_up": w_up, "w_down": w_down, "norm_attn": norm_attn, "norm_mlp": norm_mlp, "valid_counts": valid_counts, "group_ids": group_ids, "cotangent": cotangent}


eps_norm = 1e-06
neg_large = -1e+30
highest = lax.Precision.HIGHEST

@jax.custom_vjp
def low(v):
    return lax.optimization_barrier(v.astype(jnp.bfloat16)).astype(jnp.float32)

@jax.custom_vjp
def low_back(v):
    return v

def low_keep(v):
    return (low(v), None)

def low_pass(kept, grad):
    return (grad,)

def back_keep(v):
    return (v, None)

def back_low(kept, grad):
    return (low(grad),)
low.defvjp(low_keep, low_pass)
low_back.defvjp(back_keep, back_low)

def rms_scale(values):
    return lax.rsqrt(lax.optimization_barrier(jnp.mean(values * values, axis=-1, keepdims=True)) + eps_norm)

def matmul_plain(matrix_one, matrix_two):
    return jnp.dot(matrix_one, matrix_two, precision=highest)

def matmul_trans(matrix_one, matrix_two):
    return jnp.dot(matrix_one, matrix_two.T, precision=highest)

def allowed_mask(first_row, row_count, groups, valid_count):
    key_index = jnp.arange(groups.shape[0], dtype=jnp.int32)
    row_index = first_row + jnp.arange(row_count, dtype=jnp.int32)
    row_groups = lax.dynamic_slice_in_dim(groups, first_row, row_count)
    same_group = row_groups[:, None] == groups[None, :]
    usable = (key_index < valid_count)[None, :] | (row_index[:, None] == key_index[None, :])
    return same_group & usable

def attend(queries, keys_all, values_all, groups, valid_count):
    length = queries.shape[0]
    head_count = queries.shape[1] // HEAD
    key_heads = keys_all.reshape(length, head_count, HEAD)
    value_heads = values_all.reshape(length, head_count, HEAD)
    blocks = length // BLOCK
    query_blocks = queries.reshape(blocks, BLOCK, head_count, HEAD)
    starts = jnp.arange(blocks, dtype=jnp.int32) * BLOCK

    def one_block(block_items):
        query_blk, first_row = block_items
        scores = low_back(jnp.einsum('qhd,khd->hqk', query_blk, key_heads, precision=highest))
        allowed = allowed_mask(first_row, BLOCK, groups, valid_count)
        scores = jnp.where(allowed[None], scores, neg_large)
        weights_p = jax.nn.softmax(scores, axis=-1)
        return jnp.einsum('hqk,khd->qhd', low(weights_p), value_heads, precision=highest)
    outputs = lax.map(jax.checkpoint(one_block), (query_blocks, starts))
    return outputs.reshape(length, head_count * HEAD)

def image_layer(inputs, valid_count, groups, params):
    w_query, w_key, w_value, w_out, w_gate, w_up, w_down, norm_attn, norm_mlp = params
    normed_one = low(inputs * rms_scale(inputs) * norm_attn)
    head_cols = w_query.shape[1] // N_MP
    unit_cols = w_gate.shape[1] // N_MP
    summed = jnp.zeros(inputs.shape, jnp.float32)
    for portion in range(N_MP):
        normed = low_back(normed_one)
        first_col = portion * head_cols
        queries = low(low_back(matmul_plain(normed, w_query[:, first_col:first_col + head_cols])))
        keys_all = low(low_back(matmul_plain(normed, w_key[:, first_col:first_col + head_cols])))
        values_all = low(low_back(matmul_plain(normed, w_value[:, first_col:first_col + head_cols])))
        mixed_out = low(low_back(attend(queries, keys_all, values_all, groups, valid_count)))
        summed = summed + low(matmul_trans(mixed_out, w_out[:, first_col:first_col + head_cols]))
    middle = inputs + low_back(summed)
    normed_two = low(middle * rms_scale(middle) * norm_mlp)
    summed_mlp = jnp.zeros(inputs.shape, jnp.float32)
    for portion in range(N_MP):
        normed = low_back(normed_two)
        first_col = portion * unit_cols
        gate_part = low_back(matmul_plain(normed, w_gate[:, first_col:first_col + unit_cols]))
        up_part = low_back(matmul_plain(normed, w_up[:, first_col:first_col + unit_cols]))
        hidden = low(jax.nn.gelu(gate_part, approximate=True) * up_part)
        summed_mlp = summed_mlp + low(matmul_trans(hidden, w_down[:, first_col:first_col + unit_cols]))
    return middle + low_back(summed_mlp)

def reference(tokens, w_query, w_key, w_value, w_out, w_gate, w_up, w_down, norm_attn, norm_mlp, valid_counts, group_ids, cotangent):
    images = valid_counts.shape[0]
    inputs = tokens.astype(jnp.float32).reshape(images, PATCHES, D)
    params = (w_query.astype(jnp.float32), w_key.astype(jnp.float32), w_value.astype(jnp.float32), w_out.astype(jnp.float32), w_gate.astype(jnp.float32), w_up.astype(jnp.float32), w_down.astype(jnp.float32), norm_attn.astype(jnp.float32), norm_mlp.astype(jnp.float32))

    def forward(layer_in, layer_params):

        def step(carry, image_items):
            image, valid_count, groups = image_items
            return (carry, jax.checkpoint(image_layer)(image, valid_count, groups, layer_params))
        carry, outputs = lax.scan(step, jnp.zeros((), jnp.float32), (layer_in, valid_counts, group_ids))
        return outputs
    outputs, pullback = jax.vjp(forward, inputs, params)
    grad_inputs, grad_params = pullback(cotangent.astype(jnp.float32).reshape(images, PATCHES, D))
    return (outputs.reshape(-1, D).astype(jnp.bfloat16), grad_inputs.reshape(-1, D).astype(jnp.bfloat16), grad_params[0], grad_params[1], grad_params[2], grad_params[3], grad_params[4], grad_params[5], grad_params[6], grad_params[7], grad_params[8])
```

```python
import functools

import jax
import jax.numpy as jnp
from jax import lax
from jax.experimental import pallas as pl
from jax.experimental.pallas import tpu as pltpu
from jax.sharding import PartitionSpec as P

HEAD = 64
BLK = 256
DIRECT = 8
eps_norm = 1e-06
neg_large = -1e30
F32 = jnp.float32
BF16 = jnp.bfloat16


def nn(a, b):
    return lax.dot_general(a, b, (((1,), (0,)), ((), ())), preferred_element_type=F32)


def nt(a, b):
    return lax.dot_general(a, b, (((1,), (1,)), ((), ())), preferred_element_type=F32)


def tn(a, b):
    return lax.dot_general(a, b, (((0,), (0,)), ((), ())), preferred_element_type=F32)


def shape(dims, kind):
    return jax.ShapeDtypeStruct(dims, kind)


def whole(dims):
    return pl.BlockSpec(dims, lambda *_: (0,) * len(dims))


SMEM = pl.BlockSpec(memory_space=pltpu.SMEM)


def qkv_kernel(pieces, sc, t0, t1, t2, t3, gain, *rest):
    w_refs, (n1_o, qkvt_o, kn_o, vn_o, wt_o, xs, ws) = rest[:pieces], rest[pieces:]
    step = pl.program_id(0)
    cols = kn_o.shape[1]

    @pl.when(step == 0)
    def _():
        if pieces == 1:
            ws[...] = w_refs[0][...]
        else:
            depth = w_refs[0].shape[0]
            for j in range(pieces):
                at = pl.multiple_of((sc[1] ^ j) * depth, 16)
                ws[pl.ds(at, depth), :] = w_refs[j][...]
        wt_o[...] = ws[...].T

    for j, ref in enumerate((t0, t1, t2, t3)):

        @pl.when(step == j)
        def _(ref=ref):
            xs[...] = ref[...]

    x = xs[...].astype(F32)
    scale = lax.rsqrt(jnp.mean(x * x, axis=-1, keepdims=True) + eps_norm)
    n1 = (x * scale * gain[...]).astype(BF16)
    n1_o[...] = n1
    qkvt_o[...] = nt(wt_o[0 : 3 * cols, :], n1).astype(BF16)
    kn_o[...] = nn(n1, ws[:, 0:cols]).astype(BF16)
    vn_o[...] = nn(n1, ws[:, 2 * cols : 3 * cols]).astype(BF16)


def qkv(sc, shards, gain, pieces, cols):
    rows, width = shards[0].shape
    total = rows * len(shards)
    return pl.pallas_call(
        functools.partial(qkv_kernel, len(pieces)),
        grid=(len(shards),),
        in_specs=[SMEM]
        + [whole((rows, width))] * 4
        + [whole((1, width))]
        + [whole(p.shape) for p in pieces],
        out_specs=[
            pl.BlockSpec((rows, width), lambda i: (i, 0)),
            pl.BlockSpec((3 * cols, rows), lambda i: (0, i)),
            pl.BlockSpec((rows, cols), lambda i: (i, 0)),
            pl.BlockSpec((rows, cols), lambda i: (i, 0)),
            whole((4 * cols, width)),
        ],
        out_shape=[
            shape((total, width), BF16),
            shape((3 * cols, total), BF16),
            shape((total, cols), BF16),
            shape((total, cols), BF16),
            shape((4 * cols, width), BF16),
        ],
        scratch_shapes=[pltpu.VMEM((rows, width), BF16), pltpu.VMEM((width, 4 * cols), BF16)],
        name="qkv",
    )(sc, *shards, gain, *pieces)


def spread(rows, z_ref):
    heads = rows.shape[0] // HEAD
    z_ref[...] = jnp.zeros(z_ref.shape, z_ref.dtype)
    for h in range(heads):
        z_ref[h, h * HEAD : (h + 1) * HEAD, :] = rows[h * HEAD : (h + 1) * HEAD, :]


def placed(block, me, per):
    return ((block // per) ^ me) * per + lax.rem(block, per)


def span(sc, half, per, blocks):
    me = sc[0]
    stored = half * blocks + pl.program_id(0)
    place = placed(stored, me, per)
    low, high = sc[8 + place], sc[16 + place]
    has_own = jnp.logical_and(low <= place, place < high)
    count = jnp.maximum(high - low, 0) - has_own.astype(jnp.int32)

    def at(t):
        block = low + t
        block = block + (block >= place).astype(jnp.int32)
        return placed(block, me, per)

    return stored, count, at


def allowed(gkv, gq, start, own):
    keys = gkv[pl.ds(start, BLK), :]
    mask = jnp.concatenate([keys] * (BLK // 128), axis=1) == gq[...]
    if own:
        mask = mask | (
            lax.broadcasted_iota(jnp.int32, (BLK, BLK), 0)
            == lax.broadcasted_iota(jnp.int32, (BLK, BLK), 1)
        )
    return mask


def forward_kernel(half, per, sc, qt, kn, vt, gq, gkv, ot, lse, zq):
    heads = qt.shape[0] // HEAD
    stored, count, at = span(sc, half, per, pl.num_programs(0))
    spread(qt, zq)

    def scores(start, own):
        mask = allowed(gkv, gq, start, own)
        keys = kn[pl.ds(start, BLK), :]
        return [jnp.where(mask, nn(keys, zq[h]), neg_large) for h in range(heads)]

    def mixed(h, start, p):
        return nn(vt[h * HEAD : (h + 1) * HEAD, pl.ds(start, BLK)], p.astype(BF16))

    start = pl.multiple_of(stored * BLK, BLK)
    carry = []
    for h, s in enumerate(scores(start, True)):
        top = jnp.max(s, axis=0, keepdims=True)
        p = jnp.exp(s - top)
        carry.append((top, jnp.sum(p, axis=0, keepdims=True), mixed(h, start, p)))

    def body(t, carry):
        start = pl.multiple_of(at(t) * BLK, BLK)
        out = []
        for h, s in enumerate(scores(start, False)):
            top, total, acc = carry[h]
            higher = jnp.maximum(top, jnp.max(s, axis=0, keepdims=True))
            p = jnp.exp(s - higher)
            fade = jnp.exp(top - higher)
            out.append(
                (
                    higher,
                    fade * total + jnp.sum(p, axis=0, keepdims=True),
                    fade * acc + mixed(h, start, p),
                )
            )
        return tuple(out)

    carry = lax.fori_loop(0, count, body, tuple(carry))
    for h, (top, total, acc) in enumerate(carry):
        ot[h * HEAD : (h + 1) * HEAD, :] = (acc / total).astype(BF16)
        lse[h : h + 1, :] = top + jnp.log(total)


def attention(half, sc, qkvt, kn, gq, gkv):
    cols3, total = qkvt.shape
    cols = cols3 // 3
    blocks = total // BLK // 2
    per = total // 4 // BLK
    return pl.pallas_call(
        functools.partial(forward_kernel, half, per),
        grid=(blocks,),
        in_specs=[
            SMEM,
            pl.BlockSpec((cols, BLK), lambda i: (1, half * blocks + i)),
            whole((total, cols)),
            pl.BlockSpec((cols, total), lambda i: (2, 0)),
            pl.BlockSpec((1, BLK), lambda i: (0, half * blocks + i)),
            whole((total, 128)),
        ],
        out_specs=[
            pl.BlockSpec((cols, BLK), lambda i: (0, i)),
            pl.BlockSpec((8, BLK), lambda i: (0, i)),
        ],
        out_shape=[shape((cols, blocks * BLK), BF16), shape((8, blocks * BLK), F32)],
        scratch_shapes=[pltpu.VMEM((cols // HEAD, cols, BLK), BF16)],
        name="attention",
    )(sc, qkvt, kn, qkvt, gq, gkv)


def backward_kernel(
    half, per, first, sc, qt, kn, kt, vn, dot_, ot, lse, gq, gkv, *rest
):
    if first:
        dqt, dk_o, dv_o, dk, dv, zq, zd = rest
    else:
        dk_i, dv_i, dqt, dk_o, dv_o, dk, dv, zq, zd = rest
    heads = qt.shape[0] // HEAD
    step = pl.program_id(0)
    stored, count, at = span(sc, half, per, pl.num_programs(0))

    @pl.when(step == 0)
    def _():
        if first:
            dk[...] = jnp.zeros(dk.shape, F32)
            dv[...] = jnp.zeros(dv.shape, F32)
        else:
            dk[...] = dk_i[...]
            dv[...] = dv_i[...]

    spread(qt, zq)
    spread(dot_, zd)
    deltas = []
    for h in range(heads):
        part = slice(h * HEAD, (h + 1) * HEAD)
        deltas.append(
            jnp.sum(dot_[part, :].astype(F32) * ot[part, :].astype(F32), axis=0, keepdims=True)
        )

    def one(start, own):
        mask = allowed(gkv, gq, start, own)
        keys, values = kn[pl.ds(start, BLK), :], vn[pl.ds(start, BLK), :]
        out = []
        for h in range(heads):
            part = slice(h * HEAD, (h + 1) * HEAD)
            s = jnp.where(mask, nn(keys, zq[h]), neg_large)
            p = jnp.exp(s - lse[h : h + 1, :])
            ds = (p * (nn(values, zd[h]) - deltas[h])).astype(BF16)
            at_keys = pl.ds(start, BLK)
            dv[part, at_keys] += nt(dot_[part, :], p.astype(BF16))
            dk[part, at_keys] += nt(qt[part, :], ds)
            out.append(nn(kt[part, at_keys], ds))
        return out

    carry = one(pl.multiple_of(stored * BLK, BLK), True)

    def body(t, carry):
        new = one(pl.multiple_of(at(t) * BLK, BLK), False)
        return tuple(c + n for c, n in zip(carry, new))

    carry = lax.fori_loop(0, count, body, tuple(carry))
    for h in range(heads):
        dqt[h * HEAD : (h + 1) * HEAD, :] = carry[h].astype(BF16)

    @pl.when(step == pl.num_programs(0) - 1)
    def _():
        dk_o[...] = dk[...].astype(dk_o.dtype)
        dv_o[...] = dv[...].astype(dv_o.dtype)


def attention_back(half, first, sc, qkvt, kn, vn, dout, out, lse, gq, gkv, sums=()):
    cols3, total = qkvt.shape
    cols = cols3 // 3
    blocks = total // BLK // 2
    per = total // 4 // BLK
    kind = F32 if first else BF16
    return pl.pallas_call(
        functools.partial(backward_kernel, half, per, first),
        grid=(blocks,),
        in_specs=[
            SMEM,
            pl.BlockSpec((cols, BLK), lambda i: (1, half * blocks + i)),
            whole((total, cols)),
            pl.BlockSpec((cols, total), lambda i: (0, 0)),
            whole((total, cols)),
            pl.BlockSpec((cols, BLK), lambda i: (0, i)),
            pl.BlockSpec((cols, BLK), lambda i: (0, i)),
            pl.BlockSpec((8, BLK), lambda i: (0, i)),
            pl.BlockSpec((1, BLK), lambda i: (0, half * blocks + i)),
            whole((total, 128)),
        ]
        + [whole((cols, total))] * len(sums),
        out_specs=[
            pl.BlockSpec((cols, BLK), lambda i: (0, i)),
            whole((cols, total)),
            whole((cols, total)),
        ],
        out_shape=[
            shape((cols, blocks * BLK), BF16),
            shape((cols, total), kind),
            shape((cols, total), kind),
        ],
        scratch_shapes=[
            pltpu.VMEM((cols, total), F32),
            pltpu.VMEM((cols, total), F32),
            pltpu.VMEM((cols // HEAD, cols, BLK), BF16),
            pltpu.VMEM((cols // HEAD, cols, BLK), BF16),
        ],
        name="attention_back",
    )(sc, qkvt, kn, qkvt, vn, dout, out, lse, gq, gkv, *sums)


def out_kernel(om, ox, wm, wx, own, other):
    rows = own.shape[0]
    part = nn(om[...].T, wm[...]) + nn(ox[...].T, wx[...])
    own[...] = part[:rows]
    other[...] = part[rows:].astype(BF16)


def out_projection(om, ox, wm, wx):
    cols, both = om.shape
    width = wm.shape[1]
    return pl.pallas_call(
        out_kernel,
        out_shape=[shape((both // 2, width), F32), shape((both // 2, width), BF16)],
        name="out_projection",
    )(om, ox, wm, wx)


def middle_kernel(tokens, own, got, gain, h1_o, n2_o):
    h1 = tokens[...].astype(F32) + (own[...] + got[...].astype(F32))
    scale = lax.rsqrt(jnp.mean(h1 * h1, axis=-1, keepdims=True) + eps_norm)
    h1_o[...] = h1
    n2_o[...] = (h1 * scale * gain[...]).astype(BF16)


def middle(tokens, own, got, gain):
    rows, width = tokens.shape
    tile = pl.BlockSpec((rows // 4, width), lambda i: (i, 0))
    return pl.pallas_call(
        middle_kernel,
        grid=(4,),
        in_specs=[tile, tile, tile, whole((1, width))],
        out_specs=[tile, tile],
        out_shape=[shape((rows, width), F32), shape((rows, width), BF16)],
        name="middle",
    )(tokens, own, got, gain)


def mlp_kernel(na, nb, ya, yb, wg, wu, wd, ma, mb, da, db, hid_o, dgu_o):
    step = pl.program_id(0)
    lower = step < pl.num_programs(0) // 2
    n2 = jnp.where(lower, na[...], nb[...])
    dy = jnp.where(lower, ya[...], yb[...])
    gate, up = nn(n2, wg[...]), nn(n2, wu[...])
    inner = 0.7978845608028654 * (gate + 0.044715 * gate * gate * gate)
    t = jnp.tanh(inner)
    value = 0.5 * gate * (1.0 + t)
    hidden = (value * up).astype(BF16)
    hid_o[...] = hidden
    dhid = nn(dy, wd[...])
    slope = 0.5 * (1.0 + t) + 0.5 * gate * (1.0 - t * t) * 0.7978845608028654 * (
        1.0 + 3.0 * 0.044715 * gate * gate
    )
    units = wg.shape[1]
    dgate = (dhid * up * slope).astype(BF16)
    dup = (dhid * value).astype(BF16)
    dgu_o[:, 0:units] = dgate
    dgu_o[:, units : 2 * units] = dup
    dn2 = (nt(dgate, wg[...]) + nt(dup, wu[...])).astype(BF16)
    mlp = nt(hidden, wd[...]).astype(BF16)

    @pl.when(lower)
    def _():
        da[...] = dn2
        ma[...] = mlp

    @pl.when(jnp.logical_not(lower))
    def _():
        db[...] = dn2
        mb[...] = mlp


def mlp_both(na, nb, ya, yb, weights):
    rows, width = na.shape
    units = weights.shape[1] // 3
    tile = 256
    per = rows // tile
    first = pl.BlockSpec((tile, width), lambda i: (jnp.minimum(i, per - 1), 0))
    second = pl.BlockSpec((tile, width), lambda i: (jnp.maximum(i - per, 0), 0))
    part = [pl.BlockSpec((width, units), functools.partial(lambda j, i: (0, j), j)) for j in range(3)]
    return pl.pallas_call(
        mlp_kernel,
        grid=(2 * per,),
        in_specs=[first, second, first, second, *part],
        out_specs=[
            first,
            second,
            first,
            second,
            pl.BlockSpec((tile, units), lambda i: (i, 0)),
            pl.BlockSpec((tile, 2 * units), lambda i: (i, 0)),
        ],
        out_shape=[shape((rows, width), BF16)] * 4
        + [shape((2 * rows, units), BF16), shape((2 * rows, 2 * units), BF16)],
        name="mlp",
    )(na, nb, ya, yb, weights, weights, weights)


def middle_back_kernel(dy, h1_r, a, b, c, gain, dh1_o, da_o, gain_o):
    dn2 = a[...].astype(F32) + b[...].astype(F32) + c[...].astype(F32)
    h1 = h1_r[...]
    scale = lax.rsqrt(jnp.mean(h1 * h1, axis=-1, keepdims=True) + eps_norm)
    hat = dn2 * gain[...]
    dh1 = (
        dy[...].astype(F32)
        + scale * hat
        - h1 * (scale * scale * scale) * jnp.mean(hat * h1, axis=-1, keepdims=True)
    )
    dh1_o[...] = dh1
    da_o[...] = dh1.astype(BF16)

    @pl.when(pl.program_id(0) == 0)
    def _():
        gain_o[...] = jnp.zeros(gain_o.shape, F32)

    gain_o[...] += jnp.sum(dn2 * h1 * scale, axis=0, keepdims=True)


def middle_back(dy, h1, a, b, c, gain):
    rows, width = h1.shape
    tile = pl.BlockSpec((rows // 4, width), lambda i: (i, 0))
    return pl.pallas_call(
        middle_back_kernel,
        grid=(4,),
        in_specs=[tile] * 5 + [whole((1, width))],
        out_specs=[tile, tile, whole((1, width))],
        out_shape=[shape((rows, width), F32), shape((rows, width), BF16), shape((1, width), F32)],
        name="middle_back",
    )(dy, h1, a, b, c, gain)


def out_back_kernel(own, other, wm, wx, om, ox, dm_o, dx_o, gm_o, gx_o):
    rows = own.shape[0]
    for at, ref in ((0, own), (rows, other)):
        dm_o[:, at : at + rows] = nt(wm[...], ref[...]).astype(BF16)
        dx_o[:, at : at + rows] = nt(wx[...], ref[...]).astype(BF16)
    gm_o[...] = nn(om[:, :rows], own[...]) + nn(om[:, rows:], other[...])
    gx_o[...] = (nn(ox[:, :rows], own[...]) + nn(ox[:, rows:], other[...])).astype(BF16)


def out_back(own, other, wm, wx, om, ox):
    cols, both = om.shape
    width = own.shape[1]
    return pl.pallas_call(
        out_back_kernel,
        out_shape=[
            shape((cols, both), BF16),
            shape((cols, both), BF16),
            shape((cols, width), F32),
            shape((cols, width), BF16),
        ],
        name="out_back",
    )(own, other, wm, wx, om, ox)


def rows_back_kernel(dk, dq, dv, wt, a_o, b_o):
    rows = a_o.shape[0]
    grads = jnp.concatenate([dk[...], dq[...], dv[...]], axis=0)
    part = nn(grads.T, wt[0 : grads.shape[0], :]).astype(BF16)
    a_o[...] = part[:rows]
    b_o[...] = part[rows:]


def rows_back(half, dk, dq, dv, wt):
    cols, both = dq.shape
    width = wt.shape[1]
    side = pl.BlockSpec((cols, both), lambda i: (0, half))
    return pl.pallas_call(
        rows_back_kernel,
        grid=(1,),
        in_specs=[side, whole((cols, both)), side, whole(wt.shape)],
        out_specs=[whole((both // 2, width))] * 2,
        out_shape=[shape((both // 2, width), BF16)] * 2,
        name="rows_back",
    )(dk, dq, dv, wt)


def weights_back_kernel(pieces, sc, dk, dqa, dqb, dv, n1, wt, gain, gain_o, *rest):
    outs, gs = rest[:pieces], rest[pieces]
    cols, half = dqa.shape
    gt = [
        nn(dk[...], n1[...]),
        nn(dqa[...], n1[:half, :]) + nn(dqb[...], n1[half:, :]),
        nn(dv[...], n1[...]),
    ]
    total = jnp.zeros(gain.shape, F32)
    for j in range(3):
        at = slice(j * cols, (j + 1) * cols)
        total += jnp.sum(gt[j] * wt[at, :].astype(F32), axis=0, keepdims=True)
    gain_o[...] = total / gain[...]
    gs[...] = jnp.concatenate(gt, axis=0).T.astype(BF16)
    if pieces == 1:
        outs[0][...] = gs[...]
    else:
        depth = outs[0].shape[0]
        for j in range(pieces):
            outs[j][...] = gs[pl.ds(pl.multiple_of((sc[1] ^ j) * depth, 16), depth), :]


def weights_back(pieces, sc, dk, dqa, dqb, dv, n1, wt, gain):
    cols, total = dk.shape
    width = n1.shape[1]
    return pl.pallas_call(
        functools.partial(weights_back_kernel, pieces),
        in_specs=[SMEM] + [pl.BlockSpec(memory_space=pltpu.VMEM)] * 7,
        out_shape=[shape((1, width), F32)]
        + [shape((width // pieces, 3 * cols), BF16)] * pieces,
        scratch_shapes=[pltpu.VMEM((width, 3 * cols), BF16)],
        name="weights_back",
    )(sc, dk, dqa, dqb, dv, n1, wt, gain)


def last_kernel(tokens, dh1, a, b, c, gain, out):
    x = tokens[...].astype(F32)
    dn1 = a[...].astype(F32) + b[...].astype(F32) + c[...].astype(F32)
    scale = lax.rsqrt(jnp.mean(x * x, axis=-1, keepdims=True) + eps_norm)
    hat = dn1 * gain[...]
    out[...] = (
        dh1[...]
        + scale * hat
        - x * (scale * scale * scale) * jnp.mean(hat * x, axis=-1, keepdims=True)
    ).astype(BF16)


def last(tokens, dh1, a, b, c, gain):
    rows, width = tokens.shape
    tile = pl.BlockSpec((rows // 4, width), lambda i: (i, 0))
    return pl.pallas_call(
        last_kernel,
        grid=(4,),
        in_specs=[tile] * 5 + [whole((1, width))],
        out_specs=tile,
        out_shape=shape((rows, width), BF16),
        name="last",
    )(tokens, dh1, a, b, c, gain)


def local(
    dp,
    mp,
    tokens,
    w_query,
    w_key,
    w_value,
    w_out,
    w_gate,
    w_up,
    w_down,
    norm_attn,
    norm_mlp,
    valid_counts,
    group_ids,
    cotangent,
):
    me, row = lax.axis_index("mp"), lax.axis_index("dp")
    cols = w_query.shape[1]
    length = group_ids.shape[1]

    def core(v):
        return lax.ppermute(v, "mp", [(i, i ^ 1) for i in range(mp)])

    def across(v):
        return lax.ppermute(v, "mp", [(i, i ^ 2) for i in range(mp)])

    def far(v, k):
        return lax.ppermute(v, "dp", [(i, i ^ k) for i in range(dp)])

    def after(v, *others):
        return lax.optimization_barrier((v, *others))[0]

    direct = dp <= DIRECT
    gain_a, gain_m = norm_attn[None], norm_mlp[None]

    tok2 = across(tokens)
    tok1 = core(tokens)
    w_attn = jnp.concatenate([w_key, w_query, w_value, w_out], axis=1)
    if direct:
        w_pieces = [w_attn] + [far(w_attn, k) for k in range(1, dp)]
    else:
        w_pieces = [lax.all_gather(w_attn, "dp", axis=0, tiled=True)]
    w_mlp = lax.all_gather(
        jnp.concatenate([w_gate, w_up, w_down], axis=1), "dp", axis=0, tiled=True
    )
    tok3 = core(tok2)

    ids = group_ids.reshape(4, length // 4)
    valid = valid_counts[0]
    flat = ids.reshape(-1)
    tiles = flat.reshape(length // BLK, BLK)
    low = jnp.sum(flat[None, :] < tiles[:, :1], axis=1) // BLK
    high = jnp.minimum(jnp.sum(flat[None, :] <= tiles[:, -1:], axis=1), valid)
    high = (high + BLK - 1) // BLK
    head = jnp.stack([me, row, valid, valid, valid, valid, valid, valid])
    sc = jnp.concatenate([head, low, high]).astype(jnp.int32)
    place = jnp.arange(length, dtype=jnp.int32).reshape(4, length // 4)
    keyed = jnp.where(place < valid, ids, -1)

    def relative(v):
        v = jnp.where(me % 2 == 1, v[jnp.array([1, 0, 3, 2])], v)
        return jnp.where(me >= 2, v[jnp.array([2, 3, 0, 1])], v)

    gq = relative(ids).reshape(1, length)
    gkv = jnp.broadcast_to(relative(keyed).reshape(length, 1), (length, 128))

    n1, qkvt, kn, vn, wt = qkv(sc, (tokens, tok1, tok2, tok3), gain_a, w_pieces, cols)
    wo = wt[3 * cols :]
    wo_x = across(wo)
    dy0 = cotangent
    dy2 = across(after(cotangent, wo))
    dy1 = core(after(cotangent, wo))
    dy3 = core(dy2)

    o_far, lse_far = attention(1, sc, qkvt, kn, gq, gkv)
    o_x = across(o_far)
    o_own, lse_own = attention(0, after(sc, o_far), qkvt, kn, gq, gkv)
    p_own, p_other = out_projection(o_own, o_x, wo, wo_x)
    h1, n2 = middle(tokens, p_own, core(p_other), gain_m)

    n2_2 = across(n2)
    n2_1 = core(n2)
    n2_3 = core(n2_2)
    m0, m1, d0, d1, hid_a, dgu_a = mlp_both(n2, n2_1, dy0, dy1, w_mlp)
    m2, m3, d2, d3, hid_b, dgu_b = mlp_both(n2_2, n2_3, dy2, dy3, w_mlp)

    def summed(a, b):
        return (a.astype(F32) + b.astype(F32)).astype(BF16)

    d_x = across(summed(d2, core(d3)))
    dh1, da, gain_m_part = middle_back(dy0, h1, d0, core(d1), d_x, gain_m)
    m_x = across(summed(after(m2, d_x), core(after(m3, d_x))))
    output = (
        h1 + (m0.astype(F32) + core(m1).astype(F32) + m_x.astype(F32))
    ).astype(BF16)
    n2_a = jnp.concatenate([n2, n2_1], axis=0)
    n2_b = jnp.concatenate([n2_2, n2_3], axis=0)
    dy_a = jnp.concatenate([dy0, dy1], axis=0)
    dy_b = jnp.concatenate([dy2, dy3], axis=0)
    grad_gu = tn(n2_a, dgu_a) + tn(n2_b, dgu_b)
    grad_d = tn(dy_a, hid_a) + tn(dy_b, hid_b)

    do_own, do_send, go, go_send = out_back(da, core(da), wo, wo_x, o_own, o_x)
    do_far = across(do_send)
    grad_o = (go + across(go_send).astype(F32)).T
    mlp_grads = lax.psum_scatter(
        jnp.concatenate([grad_gu.astype(BF16), grad_d.astype(BF16), grad_o.astype(BF16)], axis=1),
        "dp",
        scatter_dimension=0,
        tiled=True,
    ).astype(F32)

    dq_own, dk, dv = attention_back(
        0, True, sc, qkvt, kn, vn, do_own, o_own, lse_own, gq, gkv
    )
    dq_far, dk, dv = attention_back(
        1, False, sc, qkvt, kn, vn, do_far, o_far, lse_far, gq, gkv, (dk, dv)
    )
    r2, r3 = rows_back(1, dk, dq_far, dv, wt)
    r_x = across(summed(r2, core(r3)))
    if direct:
        pieces = dp
    else:
        pieces = 1
    gain_a_part, *grads = weights_back(
        pieces, sc, after(dk, r2), dq_own, dq_far, dv, n1, wt, gain_a
    )
    if direct:
        attn_grads = grads[0].astype(F32)
        for k in range(1, dp):
            attn_grads = attn_grads + far(grads[k], k).astype(F32)
    else:
        attn_grads = lax.psum_scatter(
            grads[0], "dp", scatter_dimension=0, tiled=True
        ).astype(F32)
    r0, r1 = rows_back(0, dk, dq_own, dv, wt)
    grad_tokens = last(tokens, dh1, r0, core(r1), r_x, gain_a)

    gains = jnp.concatenate([gain_a_part, gain_m_part], axis=0)
    if direct:
        gains = gains + core(gains)
        gains = gains + across(gains)
        k = 1
        while k < dp:
            gains = gains + far(gains, k)
            k *= 2
    else:
        gains = lax.psum(gains, ("dp", "mp"))

    units = w_gate.shape[1]
    return (
        output,
        grad_tokens,
        attn_grads[:, cols : 2 * cols],
        attn_grads[:, :cols],
        attn_grads[:, 2 * cols :],
        mlp_grads[:, 3 * units :],
        mlp_grads[:, :units],
        mlp_grads[:, units : 2 * units],
        mlp_grads[:, 2 * units : 3 * units],
        gains[0],
        gains[1],
    )


def solution(mesh):
    rows, weight = P(("dp", "mp"), None), P("dp", "mp")
    return jax.shard_map(
        functools.partial(local, mesh.shape["dp"], mesh.shape["mp"]),
        mesh=mesh,
        in_specs=(rows,) + (weight,) * 7 + (P(), P(), P("dp"), P("dp", None), rows),
        out_specs=(rows, rows) + (weight,) * 7 + (P(), P()),
        check_vma=False,
    )
```

```python
import functools

import jax
import jax.numpy as jnp
from jax import lax
from jax.experimental import pallas as pl
from jax.experimental.pallas import tpu as pltpu
from jax.sharding import PartitionSpec as P

HEAD = 64
BLK = 256
DIRECT = 8
FOLD = 32
EXTRA = 8
eps_norm = 1e-06
neg_large = -1e30
F32 = jnp.float32
BF16 = jnp.bfloat16


def nn(a, b):
    return lax.dot_general(a, b, (((1,), (0,)), ((), ())), preferred_element_type=F32)


def nt(a, b):
    return lax.dot_general(a, b, (((1,), (1,)), ((), ())), preferred_element_type=F32)


def tn(a, b):
    return lax.dot_general(a, b, (((0,), (0,)), ((), ())), preferred_element_type=F32)


def shape(dims, kind):
    return jax.ShapeDtypeStruct(dims, kind)


def whole(dims):
    return pl.BlockSpec(dims, lambda *_: (0,) * len(dims))


SMEM = pl.BlockSpec(memory_space=pltpu.SMEM)


def qkv_kernel(pieces, sc, t0, t1, t2, t3, gain, *rest):
    w_refs, (n1_o, qkvt_o, kn_o, vn_o, wt_o, xs, ws) = rest[:pieces], rest[pieces:]
    step = pl.program_id(0)
    cols = kn_o.shape[1]

    @pl.when(step == 0)
    def _():
        if pieces == 1:
            ws[...] = w_refs[0][...]
        else:
            depth = w_refs[0].shape[0]
            for j in range(pieces):
                at = pl.multiple_of((sc[1] ^ j) * depth, 16)
                ws[pl.ds(at, depth), :] = w_refs[j][...]
        wt_o[...] = ws[...].T

    for j, ref in enumerate((t0, t1, t2, t3)):

        @pl.when(step == j)
        def _(ref=ref):
            xs[...] = ref[...]

    x = xs[...].astype(F32)
    scale = lax.rsqrt(jnp.mean(x * x, axis=-1, keepdims=True) + eps_norm)
    n1 = (x * scale * gain[...]).astype(BF16)
    n1_o[...] = n1
    qkvt_o[...] = nt(wt_o[0 : 3 * cols, :], n1).astype(BF16)
    kn_o[...] = nn(n1, ws[:, 0:cols]).astype(BF16)
    vn_o[...] = nn(n1, ws[:, 2 * cols : 3 * cols]).astype(BF16)


def qkv(sc, shards, gain, pieces, cols):
    rows, width = shards[0].shape
    total = rows * len(shards)
    return pl.pallas_call(
        functools.partial(qkv_kernel, len(pieces)),
        grid=(len(shards),),
        in_specs=[SMEM]
        + [whole((rows, width))] * 4
        + [whole((1, width))]
        + [whole(p.shape) for p in pieces],
        out_specs=[
            pl.BlockSpec((rows, width), lambda i: (i, 0)),
            pl.BlockSpec((3 * cols, rows), lambda i: (0, i)),
            pl.BlockSpec((rows, cols), lambda i: (i, 0)),
            pl.BlockSpec((rows, cols), lambda i: (i, 0)),
            whole((4 * cols, width)),
        ],
        out_shape=[
            shape((total, width), BF16),
            shape((3 * cols, total), BF16),
            shape((total, cols), BF16),
            shape((total, cols), BF16),
            shape((4 * cols, width), BF16),
        ],
        scratch_shapes=[pltpu.VMEM((rows, width), BF16), pltpu.VMEM((width, 4 * cols), BF16)],
        name="qkv",
        cost_estimate=cost(0.01),
    )(sc, *shards, gain, *pieces)


def spread(rows, z_ref):
    heads = rows.shape[0] // HEAD
    z_ref[...] = jnp.zeros(z_ref.shape, z_ref.dtype)
    for h in range(heads):
        z_ref[h, h * HEAD : (h + 1) * HEAD, :] = rows[h * HEAD : (h + 1) * HEAD, :]


def placed(block, me, per):
    return ((block // per) ^ me) * per + lax.rem(block, per)


def cost(us):
    return pl.CostEstimate(flops=int(us * 1e9), transcendentals=0, bytes_accessed=1024)


def span(sc, half, per, blocks):
    me = sc[0]
    stored = half * blocks + pl.program_id(0)
    place = placed(stored, me, per)
    low, high = sc[8 + place], sc[16 + place]
    has_own = jnp.logical_and(low <= place, place < high)
    count = jnp.maximum(high - low, 0) - has_own.astype(jnp.int32)

    def at(t):
        block = low + t
        block = block + (block >= place).astype(jnp.int32)
        return block, pl.multiple_of(placed(block, me, per) * BLK, BLK)

    return stored, place, count, at


def allowed(gkv, queries, block, own):
    keys = gkv[pl.ds(pl.multiple_of(block * BLK, BLK), BLK), :]
    mask = jnp.concatenate([keys] * (BLK // 128), axis=1) == queries
    if own:
        mask = mask | (
            lax.broadcasted_iota(jnp.int32, (BLK, BLK), 0)
            == lax.broadcasted_iota(jnp.int32, (BLK, BLK), 1)
        )
    return mask


def forward_kernel(half, per, sc, qt, kn, vt, gq, gkv, ot, lse, zq):
    heads = qt.shape[0] // HEAD
    stored, place, count, at = span(sc, half, per, pl.num_programs(0))
    spread(qt, zq)
    queries = gq[:, pl.ds(pl.multiple_of(place * BLK, BLK), BLK)]

    def scores(block, start, own):
        mask = allowed(gkv, queries, block, own)
        keys = kn[pl.ds(start, BLK), :]
        return [jnp.where(mask, nn(keys, zq[h]), neg_large) for h in range(heads)]

    def mixed(h, start, p):
        return nn(vt[h * HEAD : (h + 1) * HEAD, pl.ds(start, BLK)], p.astype(BF16))

    start = pl.multiple_of(stored * BLK, BLK)
    carry = []
    for h, s in enumerate(scores(place, start, True)):
        top = jnp.max(s, axis=0, keepdims=True)
        p = jnp.exp(s - top)
        carry.append((top, jnp.sum(p, axis=0, keepdims=True), mixed(h, start, p)))

    def body(t, carry):
        block, start = at(t)
        out = []
        for h, s in enumerate(scores(block, start, False)):
            top, total, acc = carry[h]
            higher = jnp.maximum(top, jnp.max(s, axis=0, keepdims=True))
            p = jnp.exp(s - higher)
            fade = jnp.exp(top - higher)
            out.append(
                (
                    higher,
                    fade * total + jnp.sum(p, axis=0, keepdims=True),
                    fade * acc + mixed(h, start, p),
                )
            )
        return tuple(out)

    carry = lax.fori_loop(0, count, body, tuple(carry))
    for h, (top, total, acc) in enumerate(carry):
        ot[h * HEAD : (h + 1) * HEAD, :] = (acc / total).astype(BF16)
        lse[h : h + 1, :] = top + jnp.log(total)


def attention(half, sc, qkvt, kn, gq, gkv):
    cols3, total = qkvt.shape
    cols = cols3 // 3
    blocks = total // BLK // 2
    per = total // 4 // BLK
    return pl.pallas_call(
        functools.partial(forward_kernel, half, per),
        grid=(blocks,),
        in_specs=[
            SMEM,
            pl.BlockSpec((cols, BLK), lambda i: (1, half * blocks + i)),
            whole((total, cols)),
            pl.BlockSpec((cols, total), lambda i: (2, 0)),
            whole((1, total)),
            whole((total, 128)),
        ],
        out_specs=[
            pl.BlockSpec((cols, BLK), lambda i: (0, i)),
            pl.BlockSpec((8, BLK), lambda i: (0, i)),
        ],
        out_shape=[shape((cols, blocks * BLK), BF16), shape((8, blocks * BLK), F32)],
        scratch_shapes=[pltpu.VMEM((cols // HEAD, cols, BLK), BF16)],
        name="attention",
        cost_estimate=cost(12),
    )(sc, qkvt, kn, qkvt, gq, gkv)


def backward_block(
    half, per, sc, qt, kn, kt, vn, dot_, ot, lse, gq, gkv, dk, dv, zq, zd
):
    heads = qt.shape[0] // HEAD
    stored, place, count, at = span(sc, half, per, pl.num_programs(0))
    queries = gq[:, pl.ds(pl.multiple_of(place * BLK, BLK), BLK)]
    spread(qt, zq)
    spread(dot_, zd)
    deltas = []
    for h in range(heads):
        part = slice(h * HEAD, (h + 1) * HEAD)
        deltas.append(
            jnp.sum(dot_[part, :].astype(F32) * ot[part, :].astype(F32), axis=0, keepdims=True)
        )

    def one(block, start, own):
        mask = allowed(gkv, queries, block, own)
        keys, values = kn[pl.ds(start, BLK), :], vn[pl.ds(start, BLK), :]
        out = []
        for h in range(heads):
            part = slice(h * HEAD, (h + 1) * HEAD)
            s = jnp.where(mask, nn(keys, zq[h]), neg_large)
            p = jnp.exp(s - lse[h : h + 1, :])
            ds = (p * (nn(values, zd[h]) - deltas[h])).astype(BF16)
            at_keys = pl.ds(start, BLK)
            dv[part, at_keys] += nt(dot_[part, :], p.astype(BF16))
            dk[part, at_keys] += nt(qt[part, :], ds)
            out.append(nn(kt[part, at_keys], ds))
        return out

    carry = one(place, pl.multiple_of(stored * BLK, BLK), True)

    def body(t, carry):
        new = one(*at(t), False)
        return tuple(c + n for c, n in zip(carry, new))

    return lax.fori_loop(0, count, body, tuple(carry))


def first_back_kernel(per, sc, qt, kn, kt, vn, dot_, ot, lse, gq, gkv, dqt, dk_o, dv_o, dk, dv, zq, zd):
    step = pl.program_id(0)

    @pl.when(step == 0)
    def _():
        dk[...] = jnp.zeros(dk.shape, F32)
        dv[...] = jnp.zeros(dv.shape, F32)

    dq = backward_block(0, per, sc, qt, kn, kt, vn, dot_, ot, lse, gq, gkv, dk, dv, zq, zd)
    for h, part in enumerate(dq):
        dqt[h * HEAD : (h + 1) * HEAD, :] = part.astype(BF16)

    @pl.when(step == pl.num_programs(0) - 1)
    def _():
        dk_o[...] = dk[...]
        dv_o[...] = dv[...]


def folded(v):
    return sum(v[at : at + FOLD, :] for at in range(0, v.shape[0], FOLD))


def halves(row):
    high = row.astype(BF16)
    return [high, (row - high.astype(F32)).astype(BF16)]


def second_back_kernel(
    per, pieces, sc, qt, kn, kt, vn, dot_, ot, lse, gq, gkv,
    dk_i, dv_i, dqa, go, gox, gain, gain_m, n1_h, wt_h, *rest
):
    r2, r3, dk_o, dv_o = rest[:4]
    outs = rest[4 : 4 + pieces]
    dk, dv, dqb, zq, zd, n1, wt, gs, sems = rest[4 + pieces :]
    step = pl.program_id(0)
    cols = dk.shape[0]
    copies = [
        pltpu.make_async_copy(n1_h, n1, sems.at[0]),
        pltpu.make_async_copy(wt_h, wt, sems.at[1]),
    ]

    @pl.when(step == 0)
    def _():
        for copy in copies:
            copy.start()
        dk[...] = dk_i[...]
        dv[...] = dv_i[...]

    dq = backward_block(1, per, sc, qt, kn, kt, vn, dot_, ot, lse, gq, gkv, dk, dv, zq, zd)
    at = pl.multiple_of(step * BLK, BLK)
    for h, part in enumerate(dq):
        dqb[h * HEAD : (h + 1) * HEAD, pl.ds(at, BLK)] = part.astype(BF16)

    @pl.when(step == pl.num_programs(0) - 1)
    def _():
        for copy in copies:
            copy.wait()
        both = dqb.shape[1]
        dkb, dvb = dk[...].astype(BF16), dv[...].astype(BF16)
        dk_o[...] = dkb[:, :both]
        dv_o[...] = dvb[:, :both]
        grads = jnp.concatenate([dkb[:, both:], dqb[...], dvb[:, both:]], axis=0)
        part = nn(grads.T, wt[0 : 3 * cols, :]).astype(BF16)
        r2[...] = part[: both // 2]
        r3[...] = part[both // 2 :]
        gt = [
            nn(dkb, n1[...]),
            nn(dqa[...], n1[:both, :]) + nn(dqb[...], n1[both:, :]),
            nn(dvb, n1[...]),
        ]
        total = jnp.zeros((FOLD, gain.shape[1]), F32)
        for j in range(3):
            total += folded(gt[j] * wt[j * cols : (j + 1) * cols, :].astype(F32))
        gain_a = jnp.sum(total, axis=0, keepdims=True) / gain[...]
        gt.append(go[...] + gox[...].astype(F32))
        gs[...] = jnp.concatenate(gt, axis=0).T.astype(BF16)
        depth = gs.shape[0] // pieces
        extra = halves(gain_a) + halves(jnp.sum(gain_m[...], axis=0, keepdims=True))
        extra.append(jnp.zeros((EXTRA - len(extra), gain.shape[1]), BF16))
        extra = jnp.concatenate(extra, axis=0)
        for j, out in enumerate(outs):
            start = pl.multiple_of((sc[1] ^ j) * depth, 16) if pieces > 1 else 0
            out[0:depth, :] = gs[pl.ds(start, depth), :]
            out[depth : depth + EXTRA, :] = extra


def back_specs(half, total, cols):
    blocks = total // BLK // 2
    return [
        SMEM,
        pl.BlockSpec((cols, BLK), lambda i: (1, half * blocks + i)),
        whole((total, cols)),
        pl.BlockSpec((cols, total), lambda i: (0, 0)),
        whole((total, cols)),
        pl.BlockSpec((cols, BLK), lambda i: (0, i)),
        pl.BlockSpec((cols, BLK), lambda i: (0, i)),
        pl.BlockSpec((8, BLK), lambda i: (0, i)),
        whole((1, total)),
        whole((total, 128)),
    ]


def spread_scratch(cols):
    return [pltpu.VMEM((cols // HEAD, cols, BLK), BF16)] * 2


def first_back(sc, qkvt, kn, vn, dout, out, lse, gq, gkv):
    total, cols = kn.shape
    blocks = total // BLK // 2
    return pl.pallas_call(
        functools.partial(first_back_kernel, total // 4 // BLK),
        grid=(blocks,),
        in_specs=back_specs(0, total, cols),
        out_specs=[
            pl.BlockSpec((cols, BLK), lambda i: (0, i)),
            whole((cols, total)),
            whole((cols, total)),
        ],
        out_shape=[
            shape((cols, blocks * BLK), BF16),
            shape((cols, total), F32),
            shape((cols, total), F32),
        ],
        scratch_shapes=[pltpu.VMEM((cols, total), F32)] * 2 + spread_scratch(cols),
        name="attention_back",
        cost_estimate=cost(20),
    )(sc, qkvt, kn, qkvt, vn, dout, out, lse, gq, gkv)


def second_back(pieces, sc, qkvt, kn, vn, dout, out, lse, gq, gkv, dk, dv, dqa, go, gox, gain, gain_m, n1, wt):
    total, cols = kn.shape
    blocks = total // BLK // 2
    both = blocks * BLK
    width = n1.shape[1]
    piece = (width // pieces + EXTRA, 4 * cols)
    return pl.pallas_call(
        functools.partial(second_back_kernel, total // 4 // BLK, pieces),
        grid=(blocks,),
        in_specs=back_specs(1, total, cols)
        + [whole((cols, total))] * 2
        + [whole((cols, both))]
        + [whole((cols, width))] * 2
        + [whole((1, width)), whole(gain_m.shape)]
        + [pl.BlockSpec(memory_space=pl.ANY)] * 2,
        out_specs=[whole((both // 2, width))] * 2
        + [whole((cols, both))] * 2
        + [whole(piece)] * pieces,
        out_shape=[shape((both // 2, width), BF16)] * 2
        + [shape((cols, both), BF16)] * 2
        + [shape(piece, BF16)] * pieces,
        scratch_shapes=[pltpu.VMEM((cols, total), F32)] * 2
        + [pltpu.VMEM((cols, both), BF16)]
        + spread_scratch(cols)
        + [
            pltpu.VMEM(n1.shape, BF16),
            pltpu.VMEM(wt.shape, BF16),
            pltpu.VMEM((width, 4 * cols), BF16),
            pltpu.SemaphoreType.DMA((2,)),
        ],
        name="attention_back_end",
        cost_estimate=cost(20),
    )(sc, qkvt, kn, qkvt, vn, dout, out, lse, gq, gkv, dk, dv, dqa, go, gox, gain, gain_m, n1, wt)


def out_kernel(om, ox, wm, wx, own, other):
    rows = own.shape[0]
    part = nn(om[...].T, wm[...]) + nn(ox[...].T, wx[...])
    own[...] = part[:rows]
    other[...] = part[rows:].astype(BF16)


def out_projection(om, ox, wm, wx):
    cols, both = om.shape
    width = wm.shape[1]
    return pl.pallas_call(
        out_kernel,
        out_shape=[shape((both // 2, width), F32), shape((both // 2, width), BF16)],
        name="out_projection",
        cost_estimate=cost(0.01),
    )(om, ox, wm, wx)


def middle_kernel(tokens, own, got, gain, h1_o, n2_o):
    h1 = tokens[...].astype(F32) + (own[...] + got[...].astype(F32))
    scale = lax.rsqrt(jnp.mean(h1 * h1, axis=-1, keepdims=True) + eps_norm)
    h1_o[...] = h1
    n2_o[...] = (h1 * scale * gain[...]).astype(BF16)


def middle(tokens, own, got, gain):
    rows, width = tokens.shape
    tile = pl.BlockSpec((rows // 4, width), lambda i: (i, 0))
    return pl.pallas_call(
        middle_kernel,
        grid=(4,),
        in_specs=[tile, tile, tile, whole((1, width))],
        out_specs=[tile, tile],
        out_shape=[shape((rows, width), F32), shape((rows, width), BF16)],
        name="middle",
        cost_estimate=cost(0.01),
    )(tokens, own, got, gain)


def mlp_kernel(na, nb, ya, yb, wg, wu, wd, ma, mb, da, db, hid_o, dgu_o):
    step = pl.program_id(0)
    lower = step < pl.num_programs(0) // 2
    n2 = jnp.where(lower, na[...], nb[...])
    dy = jnp.where(lower, ya[...], yb[...])
    gate, up = nn(n2, wg[...]), nn(n2, wu[...])
    inner = 0.7978845608028654 * (gate + 0.044715 * gate * gate * gate)
    t = jnp.tanh(inner)
    value = 0.5 * gate * (1.0 + t)
    hidden = (value * up).astype(BF16)
    hid_o[...] = hidden
    dhid = nn(dy, wd[...])
    slope = 0.5 * (1.0 + t) + 0.5 * gate * (1.0 - t * t) * 0.7978845608028654 * (
        1.0 + 3.0 * 0.044715 * gate * gate
    )
    units = wg.shape[1]
    dgate = (dhid * up * slope).astype(BF16)
    dup = (dhid * value).astype(BF16)
    dgu_o[:, 0:units] = dgate
    dgu_o[:, units : 2 * units] = dup
    dn2 = (nt(dgate, wg[...]) + nt(dup, wu[...])).astype(BF16)
    mlp = nt(hidden, wd[...]).astype(BF16)

    @pl.when(lower)
    def _():
        da[...] = dn2
        ma[...] = mlp

    @pl.when(jnp.logical_not(lower))
    def _():
        db[...] = dn2
        mb[...] = mlp


def mlp_both(na, nb, ya, yb, weights):
    rows, width = na.shape
    units = weights.shape[1] // 3
    tile = 256
    per = rows // tile
    first = pl.BlockSpec((tile, width), lambda i: (jnp.minimum(i, per - 1), 0))
    second = pl.BlockSpec((tile, width), lambda i: (jnp.maximum(i - per, 0), 0))
    part = [pl.BlockSpec((width, units), functools.partial(lambda j, i: (0, j), j)) for j in range(3)]
    return pl.pallas_call(
        mlp_kernel,
        grid=(2 * per,),
        in_specs=[first, second, first, second, *part],
        out_specs=[
            first,
            second,
            first,
            second,
            pl.BlockSpec((tile, units), lambda i: (i, 0)),
            pl.BlockSpec((tile, 2 * units), lambda i: (i, 0)),
        ],
        out_shape=[shape((rows, width), BF16)] * 4
        + [shape((2 * rows, units), BF16), shape((2 * rows, 2 * units), BF16)],
        name="mlp",
        cost_estimate=cost(0.01),
    )(na, nb, ya, yb, weights, weights, weights)


def middle_back_kernel(dy, h1_r, a, b, c, gain, dh1_o, da_o, gain_o):
    dn2 = a[...].astype(F32) + b[...].astype(F32) + c[...].astype(F32)
    h1 = h1_r[...]
    scale = lax.rsqrt(jnp.mean(h1 * h1, axis=-1, keepdims=True) + eps_norm)
    hat = dn2 * gain[...]
    dh1 = (
        dy[...].astype(F32)
        + scale * hat
        - h1 * (scale * scale * scale) * jnp.mean(hat * h1, axis=-1, keepdims=True)
    )
    dh1_o[...] = dh1
    da_o[...] = dh1.astype(BF16)

    @pl.when(pl.program_id(0) == 0)
    def _():
        gain_o[...] = jnp.zeros(gain_o.shape, F32)

    gain_o[...] += folded(dn2 * h1 * scale)


def middle_back(dy, h1, a, b, c, gain):
    rows, width = h1.shape
    tile = pl.BlockSpec((rows // 4, width), lambda i: (i, 0))
    return pl.pallas_call(
        middle_back_kernel,
        grid=(4,),
        in_specs=[tile] * 5 + [whole((1, width))],
        out_specs=[tile, tile, whole((FOLD, width))],
        out_shape=[shape((rows, width), F32), shape((rows, width), BF16), shape((FOLD, width), F32)],
        name="middle_back",
        cost_estimate=cost(0.01),
    )(dy, h1, a, b, c, gain)


def out_back_kernel(own, other, wm, wx, om, ox, dm_o, dx_o, gm_o, gx_o):
    rows = own.shape[0]
    for at, ref in ((0, own), (rows, other)):
        dm_o[:, at : at + rows] = nt(wm[...], ref[...]).astype(BF16)
        dx_o[:, at : at + rows] = nt(wx[...], ref[...]).astype(BF16)
    gm_o[...] = nn(om[:, :rows], own[...]) + nn(om[:, rows:], other[...])
    gx_o[...] = (nn(ox[:, :rows], own[...]) + nn(ox[:, rows:], other[...])).astype(BF16)


def out_back(own, other, wm, wx, om, ox):
    cols, both = om.shape
    width = own.shape[1]
    return pl.pallas_call(
        out_back_kernel,
        out_shape=[
            shape((cols, both), BF16),
            shape((cols, both), BF16),
            shape((cols, width), F32),
            shape((cols, width), BF16),
        ],
        name="out_back",
        cost_estimate=cost(0.01),
    )(own, other, wm, wx, om, ox)


def rows_back_kernel(dk, dq, dv, wt, a_o, b_o):
    rows = a_o.shape[0]
    grads = jnp.concatenate([dk[...], dq[...], dv[...]], axis=0)
    part = nn(grads.T, wt[0 : grads.shape[0], :]).astype(BF16)
    a_o[...] = part[:rows]
    b_o[...] = part[rows:]


def rows_back(dk, dq, dv, wt):
    cols, both = dq.shape
    width = wt.shape[1]
    return pl.pallas_call(
        rows_back_kernel,
        out_shape=[shape((both // 2, width), BF16)] * 2,
        name="rows_back",
        cost_estimate=cost(0.01),
    )(dk, dq, dv, wt)


def last_kernel(tokens, dh1, a, b, c, gain, out):
    x = tokens[...].astype(F32)
    dn1 = a[...].astype(F32) + b[...].astype(F32) + c[...].astype(F32)
    scale = lax.rsqrt(jnp.mean(x * x, axis=-1, keepdims=True) + eps_norm)
    hat = dn1 * gain[...]
    out[...] = (
        dh1[...]
        + scale * hat
        - x * (scale * scale * scale) * jnp.mean(hat * x, axis=-1, keepdims=True)
    ).astype(BF16)


def last(tokens, dh1, a, b, c, gain):
    rows, width = tokens.shape
    tile = pl.BlockSpec((rows // 4, width), lambda i: (i, 0))
    return pl.pallas_call(
        last_kernel,
        grid=(4,),
        in_specs=[tile] * 5 + [whole((1, width))],
        out_specs=tile,
        out_shape=shape((rows, width), BF16),
        name="last",
        cost_estimate=cost(0.01),
    )(tokens, dh1, a, b, c, gain)


def grads_sum_kernel(count, *refs):
    ins, outs, gains_o = refs[:count], refs[count:-1], refs[-1]
    rows, cols = outs[0].shape
    total = ins[0][0:rows, :].astype(F32)
    for ref in ins[1:]:
        total = total + ref[0:rows, :].astype(F32)
    for j, ref in enumerate(outs):
        ref[...] = total[:, j * cols : (j + 1) * cols]
    tail = [ref[rows : rows + EXTRA, :].astype(F32) for ref in ins]
    gains = tail[0]
    for part in tail[1:]:
        gains = gains + part
    gains = gains[0:4, :] + gains[4:8, :]
    gains_o[...] = jnp.concatenate(
        [gains[0:1, :] + gains[1:2, :], gains[2:3, :] + gains[3:4, :]], axis=0
    )


def grads_sum(parts):
    rows, width = parts[0].shape
    rows -= EXTRA
    return pl.pallas_call(
        functools.partial(grads_sum_kernel, len(parts)),
        out_shape=[shape((rows, width // 4), F32)] * 4 + [shape((2, width), F32)],
        name="grads_sum",
        cost_estimate=cost(0.01),
    )(*parts)


def local(
    dp,
    mp,
    tokens,
    w_query,
    w_key,
    w_value,
    w_out,
    w_gate,
    w_up,
    w_down,
    norm_attn,
    norm_mlp,
    valid_counts,
    group_ids,
    cotangent,
):
    me, row = lax.axis_index("mp"), lax.axis_index("dp")
    cols = w_query.shape[1]
    length = group_ids.shape[1]

    def core(v):
        return lax.ppermute(v, "mp", [(i, i ^ 1) for i in range(mp)])

    def across(v):
        return lax.ppermute(v, "mp", [(i, i ^ 2) for i in range(mp)])

    def far(v, k):
        return lax.ppermute(v, "dp", [(i, i ^ k) for i in range(dp)])

    def after(v, *others):
        return lax.optimization_barrier((v, *others))[0]

    direct = dp <= DIRECT
    gain_a, gain_m = norm_attn[None], norm_mlp[None]

    tok2 = across(tokens)
    w_attn = jnp.concatenate([w_key, w_query, w_value, w_out], axis=1)
    if direct:
        near = [w_attn] + [far(w_attn, k) for k in range(2, dp, 2)]
        w_pieces = [p for v in near for p in (v, far(v, 1))]
        tok1 = core(after(tokens, w_pieces[1]))
    else:
        w_pieces = [lax.all_gather(w_attn, "dp", axis=0, tiled=True)]
        tok1 = core(tokens)
    w_mlp = lax.all_gather(
        jnp.concatenate([w_gate, w_up, w_down], axis=1), "dp", axis=0, tiled=True
    )
    tok3 = core(after(tok2, *w_pieces[1::2]))

    gq = group_ids
    flat = group_ids[0]
    valid = valid_counts[0]
    tiles = flat.reshape(length // BLK, BLK)
    low = jnp.sum(flat[None, :] < tiles[:, :1], axis=1) // BLK
    high = jnp.minimum(jnp.sum(flat[None, :] <= tiles[:, -1:], axis=1), valid)
    high = (high + BLK - 1) // BLK
    head = jnp.stack([me, row, valid, valid, valid, valid, valid, valid])
    sc = jnp.concatenate([head, low, high]).astype(jnp.int32)
    keyed = jnp.where(jnp.arange(length, dtype=jnp.int32) < valid, flat, -1)
    gkv = jnp.broadcast_to(keyed[:, None], (length, 128))

    n1, qkvt, kn, vn, wt = qkv(sc, (tokens, tok1, tok2, tok3), gain_a, w_pieces, cols)
    wo = wt[3 * cols :]
    wo_x = across(wo)
    dy0 = cotangent
    dy2 = across(after(cotangent, tok2))
    dy1 = core(after(cotangent, tok3))

    o_far, lse_far = attention(1, sc, qkvt, kn, gq, gkv)
    o_x = across(after(o_far, dy2))
    dy3 = core(after(dy2, o_far))
    o_own, lse_own = attention(0, after(sc, o_far), qkvt, kn, gq, gkv)
    p_own, p_other = out_projection(o_own, o_x, wo, wo_x)
    h1, n2 = middle(tokens, p_own, core(p_other), gain_m)

    n2_2 = across(n2)
    n2_1 = core(n2)
    m0, m1, d0, d1, hid_a, dgu_a = mlp_both(n2, n2_1, dy0, dy1, w_mlp)
    n2_a = jnp.concatenate([n2, n2_1], axis=0)
    gu_a = tn(n2_a, dgu_a)
    n2_3 = core(after(n2_2, gu_a))
    m2, m3, d2, d3, hid_b, dgu_b = mlp_both(n2_2, n2_3, dy2, dy3, w_mlp)

    def summed(a, b):
        return (a.astype(F32) + b.astype(F32)).astype(BF16)

    d_sum = summed(d2, core(d3))
    d_x = across(d_sum)
    dgu_b, hid_a, hid_b = after((dgu_b, hid_a, hid_b), d_sum)
    d_core = core(d1)
    m_sum, m_core = summed(m2, core(m3)), core(m1)
    n2_b = jnp.concatenate([n2_2, n2_3], axis=0)
    dy_a = jnp.concatenate([dy0, dy1], axis=0)
    dy_b = jnp.concatenate([dy2, dy3], axis=0)
    grad_gu = gu_a + tn(n2_b, dgu_b)
    grad_d = tn(dy_a, hid_a) + tn(dy_b, hid_b)
    mlp_all = jnp.concatenate([grad_gu.astype(BF16), grad_d.astype(BF16)], axis=1)
    mlp_grads = lax.psum_scatter(mlp_all, "dp", scatter_dimension=0, tiled=True)
    dh1, da, gain_m_part = middle_back(dy0, h1, d0, d_core, after(d_x, mlp_all, m_sum, m_core), gain_m)

    do_own, do_send, go, go_send = out_back(da, core(da), wo, wo_x, o_own, o_x)
    do_far = across(do_send)
    go_x = across(go_send)
    dq_own, dk, dv = first_back(sc, qkvt, kn, vn, do_own, o_own, lse_own, gq, gkv)
    m_x = across(after(m_sum, do_far, go_x))
    r2, r3, dk_own, dv_own, *grads = second_back(
        dp if direct else 1,
        sc, qkvt, kn, vn, do_far, o_far, lse_far, gq, gkv,
        dk, dv, dq_own, go, go_x, gain_a, gain_m_part, n1, wt,
    )
    r_sum = summed(r2, core(after(r3, m_x)))
    r_x = across(r_sum)
    r0, r1 = rows_back(after(dk_own, r_sum), dq_own, dv_own, wt)
    grad_tokens = last(tokens, dh1, r0, core(r1), r_x, gain_a)
    output = (
        h1 + (m0.astype(F32) + m_core.astype(F32) + after(m_x, r_sum).astype(F32))
    ).astype(BF16)
    depth = w_query.shape[0]
    if direct:
        parts = []
        for k in range(0, dp, 2):
            near, other = grads[k], after(far(grads[k + 1], 1), r_sum)
            both = summed(near[:depth], other[:depth])
            part = jnp.concatenate([both, near[depth : depth + 4], other[depth : depth + 4]], axis=0)
            parts.append(part if k == 0 else far(part, k))
        grad_k, grad_q, grad_v, grad_o, gains = grads_sum(parts)
        gains = after(gains, r_x)
        gains = gains + core(gains)
        gains = gains + across(gains)
    else:
        width = tokens.shape[1]
        attn_grads = lax.psum_scatter(
            grads[0][:width], "dp", scatter_dimension=0, tiled=True
        ).astype(F32)
        grad_k, grad_q, grad_v, grad_o = jnp.split(attn_grads, 4, axis=1)
        extra = grads[0][width : width + 4].astype(F32)
        gains = lax.psum(extra[0::2] + extra[1::2], ("dp", "mp"))

    units = w_gate.shape[1]
    return (
        output,
        grad_tokens,
        grad_q,
        grad_k,
        grad_v,
        grad_o,
        mlp_grads[:, :units].astype(F32),
        mlp_grads[:, units : 2 * units].astype(F32),
        mlp_grads[:, 2 * units :].astype(F32),
        gains[0],
        gains[1],
    )


def solution(mesh):
    rows, weight = P(("dp", "mp"), None), P("dp", "mp")
    return jax.shard_map(
        functools.partial(local, mesh.shape["dp"], mesh.shape["mp"]),
        mesh=mesh,
        in_specs=(rows,) + (weight,) * 7 + (P(), P(), P("dp"), P("dp", None), rows),
        out_specs=(rows, rows) + (weight,) * 7 + (P(), P()),
        check_vma=False,
    )
```

```python
import functools

import jax
import jax.numpy as jnp
from jax import lax
from jax.experimental import pallas as pl
from jax.experimental.pallas import tpu as pltpu
from jax.sharding import PartitionSpec as P

HEAD = 64
BLK = 256
DIRECT = 8
FOLD = 32
EXTRA = 8
ROOT = 0.7978845608028654
eps_norm = 1e-06
neg_large = -1e30
F32 = jnp.float32
BF16 = jnp.bfloat16


def nn(a, b):
    return lax.dot_general(a, b, (((1,), (0,)), ((), ())), preferred_element_type=F32)


def nt(a, b):
    return lax.dot_general(a, b, (((1,), (1,)), ((), ())), preferred_element_type=F32)


def tn(a, b):
    return lax.dot_general(a, b, (((0,), (0,)), ((), ())), preferred_element_type=F32)


def shape(dims, kind):
    return jax.ShapeDtypeStruct(dims, kind)


def whole(dims):
    return pl.BlockSpec(dims, lambda *_: (0,) * len(dims))


SMEM = pl.BlockSpec(memory_space=pltpu.SMEM)
VMEM = pl.BlockSpec(memory_space=pltpu.VMEM)
HBM = pl.BlockSpec(memory_space=pltpu.HBM)
ANY = pl.BlockSpec(memory_space=pl.ANY)


def room(mib):
    return pltpu.CompilerParams(vmem_limit_bytes=mib << 20)


def qkv_kernel(pieces, sc, t0, t1, t2, t3, gain, *rest):
    w_refs, (n1_o, qkvt_o, kn_o, vn_o, wt_o, wo_o, xs, ws) = rest[:pieces], rest[pieces:]
    step = pl.program_id(0)
    cols = kn_o.shape[1]

    @pl.when(step == 0)
    def _():
        if pieces == 1:
            ws[...] = w_refs[0][...]
        else:
            depth = w_refs[0].shape[0]
            for j in range(pieces):
                at = pl.multiple_of((sc[1] ^ j) * depth, 16)
                ws[pl.ds(at, depth), :] = w_refs[j][...]
        turned = ws[...].T
        wt_o[...] = turned[: 3 * cols, :]
        wo_o[...] = turned[3 * cols :, :]

    for j, ref in enumerate((t0, t1, t2, t3)):

        @pl.when(step == j)
        def _(ref=ref):
            xs[...] = ref[...]

    x = xs[...].astype(F32)
    scale = lax.rsqrt(jnp.mean(x * x, axis=-1, keepdims=True) + eps_norm)
    n1 = (x * scale * gain[...]).astype(BF16)
    n1_o[...] = n1
    qkvt_o[...] = nt(wt_o[...], n1).astype(BF16)
    kn_o[...] = nn(n1, ws[:, 0:cols]).astype(BF16)
    vn_o[...] = nn(n1, ws[:, 2 * cols : 3 * cols]).astype(BF16)


def qkv(sc, shards, gain, pieces, cols):
    rows, width = shards[0].shape
    total = rows * len(shards)
    return pl.pallas_call(
        functools.partial(qkv_kernel, len(pieces)),
        grid=(len(shards),),
        in_specs=[SMEM]
        + [whole((rows, width))] * 4
        + [whole((1, width))]
        + [whole(p.shape) for p in pieces],
        out_specs=[
            pl.BlockSpec((rows, width), lambda i: (i, 0)),
            pl.BlockSpec((3 * cols, rows), lambda i: (0, i)),
            pl.BlockSpec((rows, cols), lambda i: (i, 0)),
            pl.BlockSpec((rows, cols), lambda i: (i, 0)),
            whole((3 * cols, width)),
            whole((cols, width)),
        ],
        out_shape=[
            shape((total, width), BF16),
            shape((3 * cols, total), BF16),
            shape((total, cols), BF16),
            shape((total, cols), BF16),
            shape((3 * cols, width), BF16),
            shape((cols, width), BF16),
        ],
        scratch_shapes=[pltpu.VMEM((rows, width), BF16), pltpu.VMEM((width, 4 * cols), BF16)],
        name="qkv",
        cost_estimate=cost(0.01),
    )(sc, *shards, gain, *pieces)


def spread(rows, z_ref):
    heads = rows.shape[0] // HEAD
    z_ref[...] = jnp.zeros(z_ref.shape, z_ref.dtype)
    for h in range(heads):
        z_ref[h, h * HEAD : (h + 1) * HEAD, :] = rows[h * HEAD : (h + 1) * HEAD, :]


def cost(us):
    return pl.CostEstimate(flops=int(us * 1e9), transcendentals=0, bytes_accessed=1024)


def span(sc, half, per, blocks):
    me = sc[0]
    stored = half * blocks + pl.program_id(0)
    shard = (stored // per) ^ me
    inner = lax.rem(stored, per)
    place = shard * per + inner
    low, high = sc[8 + place] // per, (sc[16 + place] + per - 1) // per
    has_own = jnp.logical_and(low <= shard, shard < high)
    count = jnp.maximum(high - low, 0) - has_own.astype(jnp.int32)

    def at(t):
        other = low + t
        other = other + (other >= shard).astype(jnp.int32)
        return other, other ^ me

    return place, inner, (shard, shard ^ me), count, at


def allowed(gkv, queries, at_table, own):
    keys = gkv[at_table, :]
    mask = jnp.concatenate([keys] * (BLK // 128), axis=1) == queries
    if own is not None:
        size = mask.shape
        mask = mask | (
            lax.broadcasted_iota(jnp.int32, size, 0)
            == lax.broadcasted_iota(jnp.int32, size, 1) + own * BLK
        )
    return mask


def forward_kernel(half, per, sc, qt, kn, vt, gq, gkv, ot, lse, zq):
    heads = qt.shape[0] // HEAD
    place, inner, mine, count, at = span(sc, half, per, pl.num_programs(0))
    spread(qt, zq)
    queries = gq[:, pl.ds(pl.multiple_of(place * BLK, BLK), BLK)]

    def where(shard):
        size = per * BLK
        return pl.ds(pl.multiple_of(shard * size, size), size)

    def scores(shards, own):
        mask = allowed(gkv, queries, where(shards[0]), own)
        keys = kn[where(shards[1]), :]
        return [jnp.where(mask, nn(keys, zq[h]), neg_large) for h in range(heads)]

    def mixed(h, shards, p):
        return nn(vt[h * HEAD : (h + 1) * HEAD, where(shards[1])], p.astype(BF16))

    carry = []
    for h, s in enumerate(scores(mine, inner)):
        top = jnp.max(s, axis=0, keepdims=True)
        p = jnp.exp(s - top)
        carry.append((top, jnp.sum(p, axis=0, keepdims=True), mixed(h, mine, p)))

    def body(t, carry):
        shards = at(t)
        out = []
        for h, s in enumerate(scores(shards, None)):
            top, total, acc = carry[h]
            higher = jnp.maximum(top, jnp.max(s, axis=0, keepdims=True))
            p = jnp.exp(s - higher)
            fade = jnp.exp(top - higher)
            out.append(
                (
                    higher,
                    fade * total + jnp.sum(p, axis=0, keepdims=True),
                    fade * acc + mixed(h, shards, p),
                )
            )
        return tuple(out)

    carry = lax.fori_loop(0, count, body, tuple(carry))
    for h, (top, total, acc) in enumerate(carry):
        ot[h * HEAD : (h + 1) * HEAD, :] = (acc / total).astype(BF16)
        lse[h : h + 1, :] = top + jnp.log(total)


def attention(half, sc, qkvt, kn, gq, gkv):
    cols3, total = qkvt.shape
    cols = cols3 // 3
    blocks = total // BLK // 2
    per = total // 4 // BLK
    return pl.pallas_call(
        functools.partial(forward_kernel, half, per),
        grid=(blocks,),
        in_specs=[
            SMEM,
            pl.BlockSpec((cols, BLK), lambda i: (1, half * blocks + i)),
            whole((total, cols)),
            pl.BlockSpec((cols, total), lambda i: (2, 0)),
            whole((1, total)),
            whole((total, 128)),
        ],
        out_specs=[
            pl.BlockSpec((cols, BLK), lambda i: (0, i)),
            pl.BlockSpec((8, BLK), lambda i: (0, i)),
        ],
        out_shape=[shape((cols, blocks * BLK), BF16), shape((8, blocks * BLK), F32)],
        scratch_shapes=[pltpu.VMEM((cols // HEAD, cols, BLK), BF16)],
        compiler_params=room(32),
        name="attention",
        cost_estimate=cost(12),
    )(sc, qkvt, kn, qkvt, gq, gkv)


def backward_block(
    half, per, sc, qt, kn, kt, vn, dot_, ot, lse, gq, gkv, dk, dv, zq, zd
):
    heads = qt.shape[0] // HEAD
    place, inner, mine, count, at = span(sc, half, per, pl.num_programs(0))
    queries = gq[:, pl.ds(pl.multiple_of(place * BLK, BLK), BLK)]
    spread(qt, zq)
    spread(dot_, zd)
    deltas = []
    for h in range(heads):
        part = slice(h * HEAD, (h + 1) * HEAD)
        deltas.append(
            jnp.sum(dot_[part, :].astype(F32) * ot[part, :].astype(F32), axis=0, keepdims=True)
        )

    def where(shard):
        size = per * BLK
        return pl.ds(pl.multiple_of(shard * size, size), size)

    def one(shards, own):
        mask = allowed(gkv, queries, where(shards[0]), own)
        at_keys = where(shards[1])
        keys, values = kn[at_keys, :], vn[at_keys, :]
        out = []
        for h in range(heads):
            part = slice(h * HEAD, (h + 1) * HEAD)
            s = jnp.where(mask, nn(keys, zq[h]), neg_large)
            p = jnp.exp(s - lse[h : h + 1, :])
            ds = (p * (nn(values, zd[h]) - deltas[h])).astype(BF16)
            dv[part, at_keys] += nt(dot_[part, :], p.astype(BF16))
            dk[part, at_keys] += nt(qt[part, :], ds)
            out.append(nn(kt[part, at_keys], ds))
        return out

    carry = one(mine, inner)

    def body(t, carry):
        new = one(at(t), None)
        return tuple(c + n for c, n in zip(carry, new))

    return lax.fori_loop(0, count, body, tuple(carry))


def first_back_kernel(per, sc, qt, kn, kt, vn, dot_, ot, lse, gq, gkv, dqt, dk_o, dv_o, dk, dv, zq, zd):
    step = pl.program_id(0)

    @pl.when(step == 0)
    def _():
        dk[...] = jnp.zeros(dk.shape, F32)
        dv[...] = jnp.zeros(dv.shape, F32)

    dq = backward_block(0, per, sc, qt, kn, kt, vn, dot_, ot, lse, gq, gkv, dk, dv, zq, zd)
    for h, part in enumerate(dq):
        dqt[h * HEAD : (h + 1) * HEAD, :] = part.astype(BF16)

    @pl.when(step == pl.num_programs(0) - 1)
    def _():
        dk_o[...] = dk[...]
        dv_o[...] = dv[...]


def folded(v):
    return sum(v[at : at + FOLD, :] for at in range(0, v.shape[0], FOLD))


def halves(row):
    high = row.astype(BF16)
    return [high, (row - high.astype(F32)).astype(BF16)]


def second_back_kernel(
    per, pieces, sc, qt, kn, kt, vn, dot_, ot, lse, gq, gkv,
    dk_i, dv_i, dqa, go, gox, gain, gain_m, n1_h, wt_h, *rest
):
    r2, r3, dk_o, dv_o = rest[:4]
    outs = rest[4 : 4 + pieces]
    dk, dv, dqb, zq, zd, n1, wt, gs, sems = rest[4 + pieces :]
    step = pl.program_id(0)
    cols = dk.shape[0]
    copies = [
        pltpu.make_async_copy(n1_h, n1, sems.at[0]),
        pltpu.make_async_copy(wt_h, wt, sems.at[1]),
    ]

    @pl.when(step == 0)
    def _():
        for copy in copies:
            copy.start()
        dk[...] = dk_i[...]
        dv[...] = dv_i[...]

    dq = backward_block(1, per, sc, qt, kn, kt, vn, dot_, ot, lse, gq, gkv, dk, dv, zq, zd)
    at = pl.multiple_of(step * BLK, BLK)
    for h, part in enumerate(dq):
        dqb[h * HEAD : (h + 1) * HEAD, pl.ds(at, BLK)] = part.astype(BF16)

    @pl.when(step == pl.num_programs(0) - 1)
    def _():
        for copy in copies:
            copy.wait()
        both = dqb.shape[1]
        dkb, dvb = dk[...].astype(BF16), dv[...].astype(BF16)
        dk_o[...] = dkb[:, :both]
        dv_o[...] = dvb[:, :both]
        grads = jnp.concatenate([dkb[:, both:], dqb[...], dvb[:, both:]], axis=0)
        part = nn(grads.T, wt[0 : 3 * cols, :]).astype(BF16)
        r2[...] = part[: both // 2]
        r3[...] = part[both // 2 :]
        gt = [
            nn(dkb, n1[...]),
            nn(dqa[...], n1[:both, :]) + nn(dqb[...], n1[both:, :]),
            nn(dvb, n1[...]),
        ]
        total = jnp.zeros((FOLD, gain.shape[1]), F32)
        for j in range(3):
            total += folded(gt[j] * wt[j * cols : (j + 1) * cols, :].astype(F32))
        gain_a = jnp.sum(total, axis=0, keepdims=True) / gain[...]
        gt.append(go[...] + gox[...].astype(F32))
        gs[...] = jnp.concatenate(gt, axis=0).T.astype(BF16)
        depth = gs.shape[0] // pieces
        extra = halves(gain_a) + halves(jnp.sum(gain_m[...], axis=0, keepdims=True))
        extra.append(jnp.zeros((EXTRA - len(extra), gain.shape[1]), BF16))
        extra = jnp.concatenate(extra, axis=0)
        for j, out in enumerate(outs):
            start = pl.multiple_of((sc[1] ^ j) * depth, 16) if pieces > 1 else 0
            out[0:depth, :] = gs[pl.ds(start, depth), :]
            out[depth : depth + EXTRA, :] = extra


def back_specs(half, total, cols):
    blocks = total // BLK // 2
    return [
        SMEM,
        pl.BlockSpec((cols, BLK), lambda i: (1, half * blocks + i)),
        whole((total, cols)),
        pl.BlockSpec((cols, total), lambda i: (0, 0)),
        whole((total, cols)),
        pl.BlockSpec((cols, BLK), lambda i: (0, i)),
        pl.BlockSpec((cols, BLK), lambda i: (0, i)),
        pl.BlockSpec((8, BLK), lambda i: (0, i)),
        whole((1, total)),
        whole((total, 128)),
    ]


def spread_scratch(cols):
    return [pltpu.VMEM((cols // HEAD, cols, BLK), BF16)] * 2


def first_back(sc, qkvt, kn, vn, dout, out, lse, gq, gkv):
    total, cols = kn.shape
    blocks = total // BLK // 2
    return pl.pallas_call(
        functools.partial(first_back_kernel, total // 4 // BLK),
        grid=(blocks,),
        in_specs=back_specs(0, total, cols),
        out_specs=[
            pl.BlockSpec((cols, BLK), lambda i: (0, i)),
            whole((cols, total)),
            whole((cols, total)),
        ],
        out_shape=[
            shape((cols, blocks * BLK), BF16),
            shape((cols, total), F32),
            shape((cols, total), F32),
        ],
        scratch_shapes=[pltpu.VMEM((cols, total), F32)] * 2 + spread_scratch(cols),
        name="attention_back",
        cost_estimate=cost(20),
    )(sc, qkvt, kn, qkvt, vn, dout, out, lse, gq, gkv)


def second_back(pieces, sc, qkvt, kn, vn, dout, out, lse, gq, gkv, dk, dv, dqa, go, gox, gain, gain_m, n1, wt):
    total, cols = kn.shape
    blocks = total // BLK // 2
    both = blocks * BLK
    width = n1.shape[1]
    piece = (width // pieces + EXTRA, 4 * cols)
    return pl.pallas_call(
        functools.partial(second_back_kernel, total // 4 // BLK, pieces),
        grid=(blocks,),
        in_specs=back_specs(1, total, cols)
        + [whole((cols, total))] * 2
        + [whole((cols, both))]
        + [whole((cols, width))] * 2
        + [whole((1, width)), whole(gain_m.shape)]
        + [HBM] * 2,
        out_specs=[whole((both // 2, width))] * 2
        + [whole((cols, both))] * 2
        + [whole(piece)] * pieces,
        out_shape=[shape((both // 2, width), BF16)] * 2
        + [shape((cols, both), BF16)] * 2
        + [shape(piece, BF16)] * pieces,
        scratch_shapes=[pltpu.VMEM((cols, total), F32)] * 2
        + [pltpu.VMEM((cols, both), BF16)]
        + spread_scratch(cols)
        + [
            pltpu.VMEM(n1.shape, BF16),
            pltpu.VMEM(wt.shape, BF16),
            pltpu.VMEM((width, 4 * cols), BF16),
            pltpu.SemaphoreType.DMA((2,)),
        ],
        compiler_params=room(48),
        name="attention_back_end",
        cost_estimate=cost(0.01),
    )(sc, qkvt, kn, qkvt, vn, dout, out, lse, gq, gkv, dk, dv, dqa, go, gox, gain, gain_m, n1, wt)


def rows_kernel(fn, counts, n_const, n_out, chunks, split, *refs):
    ins = []
    for count in counts:
        ins.append(refs[:count])
        refs = refs[count:]
    n_in = len(ins)
    consts, refs = refs[:n_const], refs[n_const:]
    outs, refs = refs[:n_out], refs[n_out:]
    pieces, refs = refs[:split], refs[split:]
    sums, refs = refs[: len(refs) - n_in - n_out - 2], refs[len(refs) - n_in - n_out - 2 :]
    held, made, (in_sem, out_sem) = refs[:n_in], refs[n_in:-2], refs[-2:]
    size = held[0].shape[0] // chunks

    def part(c):
        return pl.ds(c * size, size)

    def arrival(i, c):
        src = ins[i][c] if len(ins[i]) > 1 else ins[i][0].at[part(c)]
        return pltpu.make_async_copy(src, held[i].at[part(c)], in_sem.at[i, c])

    def departure(i, c):
        return pltpu.make_async_copy(made[i].at[part(c)], outs[i].at[part(c)], out_sem.at[i, c])

    def apart(c):
        return pltpu.make_async_copy(made[-1].at[part(c)], pieces[c], out_sem.at[n_out, c])

    for c in range(chunks):
        for i in range(n_in):
            arrival(i, c).start()
    totals = [jnp.zeros(r.shape, F32) for r in sums]
    for c in range(chunks):
        for i in range(n_in):
            arrival(i, c).wait()
        results, adds = fn([r[part(c), :] for r in held], [r[...] for r in consts])
        totals = [t + a for t, a in zip(totals, adds)]
        for i, value in enumerate(results):
            made[i][part(c), :] = value
        if split:
            apart(c).start()
        for i in range(n_out):
            departure(i, c).start()
    for ref, t in zip(sums, totals):
        ref[...] = t
    for c in range(chunks):
        if split:
            apart(c).wait()
        for i in range(n_out):
            departure(i, c).wait()


def by_rows(name, fn, ins, arrived, consts, kinds, sums=(), chunks=2, split=0):
    near = len(ins)
    ins = (*ins, *arrived)
    dims = ins[0].shape
    flat = [v if isinstance(v, tuple) else (v,) for v in ins]
    return pl.pallas_call(
        functools.partial(
            rows_kernel, fn, [len(v) for v in flat], len(consts), len(kinds), chunks, split
        ),
        in_specs=[HBM] * near
        + [ANY] * sum(len(v) for v in flat[near:])
        + [VMEM] * len(consts),
        out_specs=[HBM] * (len(kinds) + split) + [VMEM] * len(sums),
        out_shape=[shape(dims, k) for k in kinds]
        + [shape((dims[0] // chunks, dims[1]), kinds[-1])] * split
        + [shape(d, F32) for d in sums],
        scratch_shapes=[pltpu.VMEM(dims, v[0].dtype) for v in flat]
        + [pltpu.VMEM(dims, k) for k in kinds]
        + [
            pltpu.SemaphoreType.DMA((len(ins), chunks)),
            pltpu.SemaphoreType.DMA((len(kinds) + 1, chunks)),
        ],
        compiler_params=room(24),
        name=name,
        cost_estimate=cost(0.01),
    )(*[part for v in flat for part in v], *consts)


def out_kernel(om, ox, wm, wx, own, other, omv, oxv, wmv, wxv, ownv, otherv, sems):
    rows = own.shape[0]
    copies = [
        pltpu.make_async_copy(src, dst, sems.at[i])
        for i, (src, dst) in enumerate(((om, omv), (ox, oxv), (wm, wmv), (wx, wxv)))
    ]
    for copy in copies:
        copy.start()
    for copy in copies:
        copy.wait()
    leave = []
    for i, (at, made, out) in enumerate(((rows, otherv, other), (0, ownv, own))):
        part = slice(at, at + rows)
        made[...] = (nn(omv[:, part].T, wmv[...]) + nn(oxv[:, part].T, wxv[...])).astype(BF16)
        leave.append(pltpu.make_async_copy(made, out, sems.at[4 + i]))
        leave[-1].start()
    for copy in leave:
        copy.wait()


def out_projection(om, ox, wm, wx):
    cols, both = om.shape
    width = wm.shape[1]
    made = (both // 2, width)
    return pl.pallas_call(
        out_kernel,
        in_specs=[HBM, ANY, HBM, ANY],
        out_specs=[HBM] * 2,
        out_shape=[shape(made, BF16)] * 2,
        scratch_shapes=[pltpu.VMEM(v.shape, BF16) for v in (om, ox, wm, wx)]
        + [pltpu.VMEM(made, BF16)] * 2
        + [pltpu.SemaphoreType.DMA((6,))],
        compiler_params=room(24),
        name="out_projection",
        cost_estimate=cost(0.01),
    )(om, ox, wm, wx)


def middle_rows(held, consts):
    tokens, own, got = (v.astype(F32) for v in held)
    h1 = tokens + (own + got)
    scale = lax.rsqrt(jnp.mean(h1 * h1, axis=-1, keepdims=True) + eps_norm)
    return (h1, (h1 * scale * consts[0]).astype(BF16)), ()


def middle(tokens, own, got, gain):
    return by_rows("middle", middle_rows, (tokens, own), (got,), (gain,), (F32, BF16), split=2)


def mlp_kernel(at, aliased, na, nb, ya, yb, w, *refs):
    ma, mb, da, db, hid_o, dgu_o, nv, yv, wv, mv, dv, hv, gv, in_sem, w_sem, out_sem = refs[aliased:]
    rows, units = na.shape[0], hv.shape[1]
    arrivals, departures = [], []
    for c, (n, y, m, d) in enumerate(((na, ya, ma, da), (nb, yb, mb, db))):
        part, place = pl.ds(c * rows, rows), pl.ds(at, rows)
        arrivals += [
            pltpu.make_async_copy(n, nv.at[part], in_sem.at[0, c]),
            pltpu.make_async_copy(y.at[place], yv.at[part], in_sem.at[1, c]),
        ]
        departures.append(
            [
                pltpu.make_async_copy(dv.at[part], d, out_sem.at[0, c]),
                pltpu.make_async_copy(mv.at[part], m.at[place], out_sem.at[1, c]),
                pltpu.make_async_copy(hv.at[part], hid_o.at[part], out_sem.at[2, c]),
                pltpu.make_async_copy(gv.at[part], dgu_o.at[part], out_sem.at[3, c]),
            ]
        )
    weights = [
        pltpu.make_async_copy(
            w.at[:, pl.ds(j * units, units)], wv.at[:, pl.ds(j * units, units)], w_sem.at[j]
        )
        for j in range(3)
    ]
    for copy in weights + arrivals:
        copy.start()
    for copy in weights + arrivals:
        copy.wait()
    wg, wu, wd = (wv.at[:, pl.ds(j * units, units)] for j in range(3))
    tile = min(2 * rows, 512)
    for start in range(0, 2 * rows, tile):
        part = pl.ds(start, tile)
        n2 = nv[part, :]
        gate, up = nn(n2, wg[...]), nn(n2, wu[...])
        dhid = nn(yv[part, :], wd[...])
        square = gate * gate
        share = 0.5 * jnp.tanh(gate * (ROOT + ROOT * 0.044715 * square)) + 0.5
        value = gate * share
        slope = share + value * (1.0 - share) * (2.0 * ROOT + 6.0 * ROOT * 0.044715 * square)
        dgate = (dhid * up * slope).astype(BF16)
        dup = (dhid * value).astype(BF16)
        hidden = (value * up).astype(BF16)
        dv[part, :] = (nt(dgate, wg[...]) + nt(dup, wu[...])).astype(BF16)
        hv[part, :] = hidden
        gv[part, 0:units] = dgate
        gv[part, units : 2 * units] = dup
        mv[part, :] = nt(hidden, wd[...]).astype(BF16)
        for c in range(start // rows, (start + tile) // rows):
            for copy in departures[c]:
                copy.start()
    for copies in departures:
        for copy in copies:
            copy.wait()


def mlp_both(na, nb, ya, yb, weights, at=0, into=(), mib=32):
    rows, width = na.shape
    units = weights.shape[1] // 3
    both = 2 * rows
    return pl.pallas_call(
        functools.partial(mlp_kernel, at, len(into)),
        in_specs=[ANY] * 4 + [HBM] * (1 + len(into)),
        out_specs=[HBM] * 6,
        out_shape=[shape(ya.shape, BF16)] * 2
        + [shape((rows, width), BF16)] * 2
        + [shape((both, units), BF16), shape((both, 2 * units), BF16)],
        scratch_shapes=[
            pltpu.VMEM((both, width), BF16),
            pltpu.VMEM((both, width), BF16),
            pltpu.VMEM(weights.shape, BF16),
            pltpu.VMEM((both, width), BF16),
            pltpu.VMEM((both, width), BF16),
            pltpu.VMEM((both, units), BF16),
            pltpu.VMEM((both, 2 * units), BF16),
            pltpu.SemaphoreType.DMA((2, 2)),
            pltpu.SemaphoreType.DMA((3,)),
            pltpu.SemaphoreType.DMA((4, 2)),
        ],
        input_output_aliases={5 + i: i for i in range(len(into))},
        compiler_params=room(mib),
        name="mlp",
        cost_estimate=cost(8),
    )(na, nb, ya, yb, weights, *into)


def mlp_weights_kernel(order, n_in, *refs):
    ins, (out, *held, total, made, sems, sem) = refs[:n_in], refs[n_in:]
    copies = []
    for group, moves in enumerate(order):
        for which, start, rows, at in moves:
            copy = pltpu.make_async_copy(
                ins[which].at[pl.ds(start, rows)], held[group].at[pl.ds(at, rows)], sems.at[len(copies)]
            )
            copies.append((at + rows, copy))
    length = held[0].shape[0]
    copies.sort(key=lambda v: v[0])
    for _, copy in copies:
        copy.start()
    wide = held[2].shape[1]
    done = 0
    for edge in (length // 2, length):
        for end, copy in copies:
            if done < end <= edge:
                copy.wait()
        rows = pl.ds(done, edge - done)
        n2, dy, dgu, hidden = (r[rows, :] for r in held)
        for at, left, right in ((0, n2, dgu), (wide, dy, hidden)):
            new = nn(left.T, right)
            cols = pl.ds(at, right.shape[1])
            if edge == length:
                made[:, cols] = (total[:, cols] + new).astype(BF16)
            else:
                total[:, cols] = new
        done = edge
    leave = pltpu.make_async_copy(made, out, sem)
    leave.start()
    leave.wait()


def mlp_weights(n2, dy, dgu, hidden):
    ins = (*n2, *dy, *dgu, *hidden)
    rows = n2[0].shape[0]
    half = rows // 2
    first = [(0, 0, rows, 0), (1, 0, rows, rows)]
    order = [
        first + [(2, 0, half, 2 * rows), (4, 0, half, 2 * rows + half), (3, 0, half, 3 * rows), (5, 0, half, 3 * rows + half)],
        [(6 + j, 0, rows, j * rows) for j in range(4)],
    ]
    for base in (10, 13):
        order.append(
            [
                (base, 0, 2 * rows, 0),
                (base + 1, 0, half, 2 * rows),
                (base + 2, 0, half, 2 * rows + half),
                (base + 1, half, half, 3 * rows),
                (base + 2, half, half, 3 * rows + half),
            ]
        )
    width = n2[0].shape[1]
    dims = (width, dgu[0].shape[1] + hidden[0].shape[1])
    return pl.pallas_call(
        functools.partial(mlp_weights_kernel, order, len(ins)),
        in_specs=[HBM] * len(ins),
        out_specs=HBM,
        out_shape=shape(dims, BF16),
        scratch_shapes=[
            pltpu.VMEM((4 * rows, v.shape[1]), BF16) for v in (n2[0], dy[0], dgu[0], hidden[0])
        ]
        + [
            pltpu.VMEM(dims, F32),
            pltpu.VMEM(dims, BF16),
            pltpu.SemaphoreType.DMA((sum(len(v) for v in order),)),
            pltpu.SemaphoreType.DMA,
        ],
        compiler_params=room(48),
        name="mlp_weights",
        cost_estimate=cost(10),
    )(*ins)


def middle_back_rows(held, consts):
    dy, h1, *shares = (v.astype(F32) for v in held)
    dn2 = sum(shares[1:], shares[0])
    scale = lax.rsqrt(jnp.mean(h1 * h1, axis=-1, keepdims=True) + eps_norm)
    hat = dn2 * consts[0]
    dh1 = (
        dy
        + scale * hat
        - h1 * (scale * scale * scale) * jnp.mean(hat * h1, axis=-1, keepdims=True)
    )
    return (dh1, dh1.astype(BF16)), (folded(dn2 * h1 * scale),)


def middle_back(dy, h1, a, b, c, gain):
    return by_rows(
        "middle_back",
        middle_back_rows,
        (dy, h1, a),
        (b, c),
        (gain,),
        (F32, BF16),
        sums=((FOLD, dy.shape[1]),),
    )


def out_back_kernel(own, other, wm, wx, om, ox, dm_o, dx_o, gm_o, gx_o, *scratch):
    refs = (own, other, wm, wx, om, ox)
    held, made, sems = scratch[:6], scratch[6:10], scratch[10]
    copies = [pltpu.make_async_copy(src, dst, sems.at[i]) for i, (src, dst) in enumerate(zip(refs, held))]
    for copy in copies:
        copy.start()
    ownv, otherv, wmv, wxv, omv, oxv = held
    dm, dx, gm, gx = made
    rows = own.shape[0]
    for copy in copies:
        copy.wait()
    leave = [
        pltpu.make_async_copy(src, dst, sems.at[6 + i])
        for i, (src, dst) in enumerate(((dx, dx_o), (dm, dm_o), (gx, gx_o), (gm, gm_o)))
    ]
    for i, (w, out) in enumerate(((wxv, dx), (wmv, dm))):
        for at, ref in ((0, ownv), (rows, otherv)):
            out[:, at : at + rows] = nt(w[...], ref[...]).astype(BF16)
        leave[i].start()
    gx[...] = (nn(oxv[:, :rows], ownv[...]) + nn(oxv[:, rows:], otherv[...])).astype(BF16)
    leave[2].start()
    gm[...] = nn(omv[:, :rows], ownv[...]) + nn(omv[:, rows:], otherv[...])
    leave[3].start()
    for copy in leave:
        copy.wait()


def out_back(own, other, wm, wx, om, ox):
    cols, both = om.shape
    width = own.shape[1]
    ins = (own, other, wm, wx, om, ox)
    outs = [
        ((cols, both), BF16),
        ((cols, both), BF16),
        ((cols, width), F32),
        ((cols, width), BF16),
    ]
    return pl.pallas_call(
        out_back_kernel,
        in_specs=[HBM, ANY, HBM, ANY, HBM, ANY],
        out_specs=[HBM] * 4,
        out_shape=[shape(*v) for v in outs],
        scratch_shapes=[pltpu.VMEM(v.shape, BF16) for v in ins]
        + [pltpu.VMEM(*v) for v in outs]
        + [pltpu.SemaphoreType.DMA((10,))],
        compiler_params=room(24),
        name="out_back",
        cost_estimate=cost(0.01),
    )(*ins)


def rows_back_kernel(dk, dq, dv, wt, a_o, b_o):
    rows = a_o.shape[0]
    grads = jnp.concatenate([dk[...], dq[...], dv[...]], axis=0)
    part = nn(grads.T, wt[0 : grads.shape[0], :]).astype(BF16)
    a_o[...] = part[:rows]
    b_o[...] = part[rows:]


def rows_back(dk, dq, dv, wt):
    cols, both = dq.shape
    width = wt.shape[1]
    return pl.pallas_call(
        rows_back_kernel,
        out_shape=[shape((both // 2, width), BF16)] * 2,
        compiler_params=room(24),
        name="rows_back",
        cost_estimate=cost(0.01),
    )(dk, dq, dv, wt)


def last_rows(held, consts):
    x, dh1, *shares = (v.astype(F32) for v in held)
    dn1 = sum(shares[1:], shares[0])
    scale = lax.rsqrt(jnp.mean(x * x, axis=-1, keepdims=True) + eps_norm)
    hat = dn1 * consts[0]
    out = (
        dh1
        + scale * hat
        - x * (scale * scale * scale) * jnp.mean(hat * x, axis=-1, keepdims=True)
    )
    return (out.astype(BF16),), ()


def last(tokens, dh1, a, b, c, gain):
    return by_rows("last", last_rows, (tokens, dh1, a), (b, c), (gain,), (BF16,))[0]


def output_rows(held, consts):
    h1, a, b, c = (v.astype(F32) for v in held)
    return ((h1 + (a + b + c)).astype(BF16),), ()


def grads_sum_kernel(count, *refs):
    ins, outs, gains_o = refs[:count], refs[count:-1], refs[-1]
    rows, cols = outs[0].shape
    total = ins[0][0:rows, :].astype(F32)
    for ref in ins[1:]:
        total = total + ref[0:rows, :].astype(F32)
    for j, ref in enumerate(outs):
        ref[...] = total[:, j * cols : (j + 1) * cols]
    tail = [ref[rows : rows + EXTRA, :].astype(F32) for ref in ins]
    gains = tail[0]
    for part in tail[1:]:
        gains = gains + part
    gains = gains[0:4, :] + gains[4:8, :]
    gains_o[...] = jnp.concatenate(
        [gains[0:1, :] + gains[1:2, :], gains[2:3, :] + gains[3:4, :]], axis=0
    )


def grads_sum(parts):
    rows, width = parts[0].shape
    rows -= EXTRA
    return pl.pallas_call(
        functools.partial(grads_sum_kernel, len(parts)),
        out_shape=[shape((rows, width // 4), F32)] * 4 + [shape((2, width), F32)],
        compiler_params=room(16),
        name="grads_sum",
        cost_estimate=cost(0.01),
    )(*parts)


def local(
    dp,
    mp,
    tokens,
    w_query,
    w_key,
    w_value,
    w_out,
    w_gate,
    w_up,
    w_down,
    norm_attn,
    norm_mlp,
    valid_counts,
    group_ids,
    cotangent,
):
    me, row = lax.axis_index("mp"), lax.axis_index("dp")
    cols = w_query.shape[1]
    length = group_ids.shape[1]

    def core(v):
        return lax.ppermute(v, "mp", [(i, i ^ 1) for i in range(mp)])

    def across(v):
        return lax.ppermute(v, "mp", [(i, i ^ 2) for i in range(mp)])

    def far(v, k):
        return lax.ppermute(v, "dp", [(i, i ^ k) for i in range(dp)])

    def after(v, *others):
        return lax.optimization_barrier((v, *others))[0]

    def summed(a, b):
        return (a.astype(F32) + b.astype(F32)).astype(BF16)

    direct = dp <= DIRECT
    gain_a, gain_m = norm_attn[None], norm_mlp[None]

    gq = group_ids
    flat = group_ids[0]
    valid = valid_counts[0]
    tiles = flat.reshape(length // BLK, BLK)
    low = jnp.sum(flat[None, :] < tiles[:, :1], axis=1) // BLK
    high = jnp.minimum(jnp.sum(flat[None, :] <= tiles[:, -1:], axis=1), valid)
    high = (high + BLK - 1) // BLK
    head = jnp.stack([me, row, valid, valid, valid, valid, valid, valid])
    sc = jnp.concatenate([head, low, high]).astype(jnp.int32)
    keyed = jnp.where(jnp.arange(length, dtype=jnp.int32) < valid, flat, -1)
    gkv = jnp.broadcast_to(keyed[:, None], (length, 128))

    tok2 = across(tokens)
    w_attn = jnp.concatenate([w_key, w_query, w_value, w_out], axis=1)
    w_mlp = jnp.concatenate([w_gate, w_up, w_down], axis=1)
    if direct:
        near = [w_attn] + [far(w_attn, k) for k in range(2, dp, 2)]
        near[1] = after(near[1], sc, gkv, w_mlp)
        w_pieces = [p for v in near for p in (v, far(v, 1))]
        tok1 = core(after(tokens, w_pieces[1]))
    else:
        w_pieces = [lax.all_gather(w_attn, "dp", axis=0, tiled=True)]
        tok1 = core(tokens)
    w_mlp = lax.all_gather(w_mlp, "dp", axis=0, tiled=True)
    tok3 = core(after(tok2, *w_pieces[1::2]))

    n1, qkvt, kn, vn, wt, wo = qkv(sc, (tokens, tok1, tok2, tok3), gain_a, w_pieces, cols)
    wo_x = across(wo)
    dy0 = cotangent
    dy2 = across(after(cotangent, tok2))
    dy1 = core(after(cotangent, tok3))

    o_far, lse_far = attention(1, sc, qkvt, kn, gq, gkv)
    o_x = across(after(o_far, dy2, wo_x))
    dy3 = core(after(dy2, o_far))
    o_own, lse_own = attention(0, after(sc, o_far), qkvt, kn, gq, gkv)
    p_own, p_other = out_projection(o_own, o_x, wo, wo_x)
    h1, n2, n2_a, n2_b = middle(tokens, p_own, core(p_other), gain_m)

    half = n2.shape[0] // 2
    n2_1 = core(n2)
    far_a = across(n2_a)
    far_b = across(n2_b)
    m0, m1, d0, d1, hid_o, dgu_o = mlp_both(n2, n2_1, dy0, dy1, w_mlp, mib=60)
    side_a = core(after(far_a, d0))
    m2, m3, d2a, d3a, hid_a, dgu_a = mlp_both(far_a, side_a, dy2, dy3, w_mlp)
    dsum_a = summed(d2a, core(d3a))
    dx_a = across(dsum_a)
    side_b = core(after(far_b, d2a))
    far_b = after(far_b, dsum_a)
    m2, m3, d2b, d3b, hid_b, dgu_b = mlp_both(far_b, side_b, dy2, dy3, w_mlp, half, (m2, m3))

    d_sum = summed(d2b, core(after(d3b, dx_a)))
    dx_b = across(d_sum)
    mlp_all = mlp_weights(
        (n2, n2_1, far_a, side_a, far_b, side_b),
        (dy0, dy1, dy2, dy3),
        (dgu_o, dgu_a, dgu_b),
        (after(hid_o, d_sum), hid_a, hid_b),
    )
    mlp_grads = lax.psum_scatter(mlp_all, "dp", scatter_dimension=0, tiled=True)
    m_sum, m_core = summed(after(m2, d_sum), core(m3)), core(after(m1, d_sum))
    dh1, da, gain_m_part = middle_back(
        dy0,
        h1,
        d0,
        core(after(d1, d_sum)),
        (dx_a, after(dx_b, mlp_all, m_sum, m_core)),
        gain_m,
    )

    do_own, do_send, go, go_send = out_back(da, core(da), wo, wo_x, o_own, o_x)
    do_far = across(do_send)
    go_x = across(go_send)
    m_x = across(after(m_sum, do_send))
    dq_own, dk, dv = first_back(sc, qkvt, kn, vn, do_own, o_own, lse_own, gq, gkv)
    r2, r3, dk_own, dv_own, *grads = second_back(
        dp if direct else 1,
        sc, qkvt, kn, vn, do_far, o_far, lse_far, gq, gkv,
        dk, dv, dq_own, go, go_x, gain_a, gain_m_part, n1, wt,
    )
    r_sum = summed(r2, core(after(r3, m_x)))
    r_x = across(r_sum)
    depth = w_query.shape[0]
    parts = []
    if direct:
        others = {}
        for k in range(dp - 2, -1, -2):
            sent = grads[k + 1]
            others[k] = far(after(sent, others[k + dp // 2]) if k + dp // 2 in others else sent, 1)
        for k in range(0, dp, 2):
            near, other = grads[k], after(others[k], r_sum)
            both = summed(near[:depth], other[:depth])
            part = jnp.concatenate([both, near[depth : depth + 4], other[depth : depth + 4]], axis=0)
            parts.append(part if k == 0 else far(part, k))
    r0, r1 = rows_back(after(dk_own, r_sum), dq_own, dv_own, wt)
    grad_tokens = last(tokens, dh1, r0, core(r1), r_x, gain_a)
    (output,) = by_rows(
        "output", output_rows, (h1, m0), (m_core, after(m_x, r_sum)), (), (BF16,)
    )
    units = w_gate.shape[1]
    grad_gate, grad_up, grad_down = (
        mlp_grads[:, j * units : (j + 1) * units].astype(F32) for j in range(3)
    )
    if direct:
        parts[0] = after(parts[0], grad_tokens, output, grad_gate)
        grad_k, grad_q, grad_v, grad_o, gains = grads_sum(parts)
        gains = gains + core(gains)
        gains = gains + across(gains)
    else:
        width = tokens.shape[1]
        attn_grads = lax.psum_scatter(
            grads[0][:width], "dp", scatter_dimension=0, tiled=True
        ).astype(F32)
        grad_k, grad_q, grad_v, grad_o = jnp.split(attn_grads, 4, axis=1)
        extra = grads[0][width : width + 4].astype(F32)
        gains = lax.psum(extra[0::2] + extra[1::2], ("dp", "mp"))

    return (
        output,
        grad_tokens,
        grad_q,
        grad_k,
        grad_v,
        grad_o,
        grad_gate,
        grad_up,
        grad_down,
        gains[0],
        gains[1],
    )


def solution(mesh):
    rows, weight = P(("dp", "mp"), None), P("dp", "mp")
    return jax.shard_map(
        functools.partial(local, mesh.shape["dp"], mesh.shape["mp"]),
        mesh=mesh,
        in_specs=(rows,) + (weight,) * 7 + (P(), P(), P("dp"), P("dp", None), rows),
        out_specs=(rows, rows) + (weight,) * 7 + (P(), P()),
        check_vma=False,
    )
```

```python
import functools

import jax
import jax.numpy as jnp
from jax import lax
from jax.experimental import pallas as pl
from jax.experimental.pallas import tpu as pltpu
from jax.sharding import PartitionSpec as P

HEAD = 64
BLK = 256
DIRECT = 8
FOLD = 32
EXTRA = 8
ROOT = 0.7978845608028654
eps_norm = 1e-06
neg_large = -1e30
F32 = jnp.float32
BF16 = jnp.bfloat16


def nn(a, b):
    return lax.dot_general(a, b, (((1,), (0,)), ((), ())), preferred_element_type=F32)


def nt(a, b):
    return lax.dot_general(a, b, (((1,), (1,)), ((), ())), preferred_element_type=F32)


def tn(a, b):
    return lax.dot_general(a, b, (((0,), (0,)), ((), ())), preferred_element_type=F32)


def shape(dims, kind):
    return jax.ShapeDtypeStruct(dims, kind)


def whole(dims):
    return pl.BlockSpec(dims, lambda *_: (0,) * len(dims))


SMEM = pl.BlockSpec(memory_space=pltpu.SMEM)
VMEM = pl.BlockSpec(memory_space=pltpu.VMEM)
HBM = pl.BlockSpec(memory_space=pltpu.HBM)
ANY = pl.BlockSpec(memory_space=pl.ANY)


def room(mib):
    return pltpu.CompilerParams(vmem_limit_bytes=mib << 20)


def qkv_kernel(pieces, sc, t0, t1, t2, t3, gain, *rest):
    w_refs, (n1_o, qkvt_o, kn_o, vn_o, wt_o, wo_o, xs, ws) = rest[:pieces], rest[pieces:]
    step = pl.program_id(0)
    cols = kn_o.shape[1]

    @pl.when(step == 0)
    def _():
        if pieces == 1:
            ws[...] = w_refs[0][...]
        else:
            depth = w_refs[0].shape[0]
            for j in range(pieces):
                at = pl.multiple_of((sc[1] ^ j) * depth, 16)
                ws[pl.ds(at, depth), :] = w_refs[j][...]
        turned = ws[...].T
        wt_o[...] = turned[: 3 * cols, :]
        wo_o[...] = turned[3 * cols :, :]

    for j, ref in enumerate((t0, t1, t2, t3)):

        @pl.when(step == j)
        def _(ref=ref):
            xs[...] = ref[...]

    x = xs[...].astype(F32)
    scale = lax.rsqrt(jnp.mean(x * x, axis=-1, keepdims=True) + eps_norm)
    n1 = (x * scale * gain[...]).astype(BF16)
    n1_o[...] = n1
    qkvt_o[...] = nt(wt_o[...], n1).astype(BF16)
    kn_o[...] = nn(n1, ws[:, 0:cols]).astype(BF16)
    vn_o[...] = nn(n1, ws[:, 2 * cols : 3 * cols]).astype(BF16)


def qkv(sc, shards, gain, pieces, cols):
    rows, width = shards[0].shape
    total = rows * len(shards)
    return pl.pallas_call(
        functools.partial(qkv_kernel, len(pieces)),
        grid=(len(shards),),
        in_specs=[SMEM]
        + [whole((rows, width))] * 4
        + [whole((1, width))]
        + [whole(p.shape) for p in pieces],
        out_specs=[
            pl.BlockSpec((rows, width), lambda i: (i, 0)),
            pl.BlockSpec((3 * cols, rows), lambda i: (0, i)),
            pl.BlockSpec((rows, cols), lambda i: (i, 0)),
            pl.BlockSpec((rows, cols), lambda i: (i, 0)),
            whole((3 * cols, width)),
            whole((cols, width)),
        ],
        out_shape=[
            shape((total, width), BF16),
            shape((3 * cols, total), BF16),
            shape((total, cols), BF16),
            shape((total, cols), BF16),
            shape((3 * cols, width), BF16),
            shape((cols, width), BF16),
        ],
        scratch_shapes=[pltpu.VMEM((rows, width), BF16), pltpu.VMEM((width, 4 * cols), BF16)],
        name="qkv",
        cost_estimate=cost(0.01),
    )(sc, *shards, gain, *pieces)


def spread(rows, z_ref):
    heads = rows.shape[0] // HEAD
    z_ref[...] = jnp.zeros(z_ref.shape, z_ref.dtype)
    for h in range(heads):
        z_ref[h, h * HEAD : (h + 1) * HEAD, :] = rows[h * HEAD : (h + 1) * HEAD, :]


def cost(us):
    return pl.CostEstimate(flops=int(us * 1e9), transcendentals=0, bytes_accessed=1024)


def span(sc, half, per, blocks):
    me = sc[0]
    stored = half * blocks + pl.program_id(0)
    shard = (stored // per) ^ me
    place = shard * per + lax.rem(stored, per)
    low, high = sc[8 + place] // per, (sc[16 + place] + per - 1) // per
    has_own = jnp.logical_and(low <= shard, shard < high)
    count = jnp.maximum(high - low, 0) - has_own.astype(jnp.int32)

    def at(t):
        other = low + t - 1
        other = jnp.where(t == 0, shard, other + (other >= shard).astype(jnp.int32))
        return other, other ^ me

    return place, count + 1, at


def allowed(gkv, queries, place, shard, size, own=True):
    keys = gkv[pl.ds(pl.multiple_of(shard * size, size), size), :]
    mask = jnp.concatenate([keys] * (BLK // 128), axis=1) == queries
    if not own:
        return mask
    key_at = lax.broadcasted_iota(jnp.int32, mask.shape, 0)
    query_at = lax.broadcasted_iota(jnp.int32, mask.shape, 1) + (place * BLK - shard * size)
    return mask | (key_at == query_at)


def forward_kernel(half, per, sc, qt, kn, vt, gq, gkv, ot, lse, zq):
    heads = qt.shape[0] // HEAD
    size = per * BLK
    place, count, at = span(sc, half, per, pl.num_programs(0))
    spread(qt, zq)
    queries = gq[:, pl.ds(pl.multiple_of(place * BLK, BLK), BLK)]

    def scores(t, own):
        shard, stored = at(t)
        mask = allowed(gkv, queries, place, shard, size, own)
        where = pl.ds(pl.multiple_of(stored * size, size), size)
        keys = kn[where, :]
        return where, [jnp.where(mask, nn(keys, zq[h]), neg_large) for h in range(heads)]

    def mixed(h, where, p):
        return nn(vt[h * HEAD : (h + 1) * HEAD, where], p.astype(BF16))

    carry = []
    where, first = scores(0, True)
    for h, s in enumerate(first):
        top = jnp.max(s, axis=0, keepdims=True)
        p = jnp.exp(s - top)
        carry.append((top, jnp.sum(p, axis=0, keepdims=True), mixed(h, where, p)))

    def body(t, carry):
        where, more = scores(t, False)
        out = []
        for h, s in enumerate(more):
            top, total, acc = carry[h]
            higher = jnp.maximum(top, jnp.max(s, axis=0, keepdims=True))
            p = jnp.exp(s - higher)
            fade = jnp.exp(top - higher)
            out.append(
                (
                    higher,
                    fade * total + jnp.sum(p, axis=0, keepdims=True),
                    fade * acc + mixed(h, where, p),
                )
            )
        return tuple(out)

    carry = lax.fori_loop(1, count, body, tuple(carry))
    for h, (top, total, acc) in enumerate(carry):
        ot[h * HEAD : (h + 1) * HEAD, :] = (acc / total).astype(BF16)
        lse[h : h + 1, :] = top + jnp.log(total)


def attention(half, sc, qkvt, kn, gq, gkv):
    cols3, total = qkvt.shape
    cols = cols3 // 3
    blocks = total // BLK // 2
    per = total // 4 // BLK
    return pl.pallas_call(
        functools.partial(forward_kernel, half, per),
        grid=(blocks,),
        in_specs=[
            SMEM,
            pl.BlockSpec((cols, BLK), lambda i: (1, half * blocks + i)),
            whole((total, cols)),
            pl.BlockSpec((cols, total), lambda i: (2, 0)),
            whole((1, total)),
            whole((total, 128)),
        ],
        out_specs=[
            pl.BlockSpec((cols, BLK), lambda i: (0, i)),
            pl.BlockSpec((8, BLK), lambda i: (0, i)),
        ],
        out_shape=[shape((cols, blocks * BLK), BF16), shape((8, blocks * BLK), F32)],
        scratch_shapes=[pltpu.VMEM((cols // HEAD, cols, BLK), BF16)],
        compiler_params=room(32),
        name="attention",
        cost_estimate=cost(12),
    )(sc, qkvt, kn, qkvt, gq, gkv)


def backward_block(
    half, per, sc, qt, kn, kt, vn, dot_, ot, lse, gq, gkv, dk, dv, zq, zd
):
    heads = qt.shape[0] // HEAD
    size = per * BLK
    place, count, at = span(sc, half, per, pl.num_programs(0))
    queries = gq[:, pl.ds(pl.multiple_of(place * BLK, BLK), BLK)]
    spread(qt, zq)
    spread(dot_, zd)
    deltas = []
    for h in range(heads):
        part = slice(h * HEAD, (h + 1) * HEAD)
        deltas.append(
            jnp.sum(dot_[part, :].astype(F32) * ot[part, :].astype(F32), axis=0, keepdims=True)
        )

    def body(t, carry):
        shard, stored = at(t)
        mask = allowed(gkv, queries, place, shard, size)
        at_keys = pl.ds(pl.multiple_of(stored * size, size), size)
        keys, values = kn[at_keys, :], vn[at_keys, :]
        out = []
        for h in range(heads):
            part = slice(h * HEAD, (h + 1) * HEAD)
            s = jnp.where(mask, nn(keys, zq[h]), neg_large)
            p = jnp.exp(s - lse[h : h + 1, :])
            ds = (p * (nn(values, zd[h]) - deltas[h])).astype(BF16)
            dv[part, at_keys] += nt(dot_[part, :], p.astype(BF16))
            dk[part, at_keys] += nt(qt[part, :], ds)
            out.append(carry[h] + nn(kt[part, at_keys], ds))
        return tuple(out)

    zero = jnp.zeros((HEAD, BLK), F32)
    return lax.fori_loop(0, count, body, (zero,) * heads)


def first_back_kernel(per, sc, qt, kn, kt, vn, dot_, ot, lse, gq, gkv, dqt, dk_o, dv_o, dk, dv, zq, zd):
    step = pl.program_id(0)

    @pl.when(step == 0)
    def _():
        dk[...] = jnp.zeros(dk.shape, F32)
        dv[...] = jnp.zeros(dv.shape, F32)

    dq = backward_block(0, per, sc, qt, kn, kt, vn, dot_, ot, lse, gq, gkv, dk, dv, zq, zd)
    for h, part in enumerate(dq):
        dqt[h * HEAD : (h + 1) * HEAD, :] = part.astype(BF16)

    @pl.when(step == pl.num_programs(0) - 1)
    def _():
        dk_o[...] = dk[...]
        dv_o[...] = dv[...]


def folded(v):
    return sum(v[at : at + FOLD, :] for at in range(0, v.shape[0], FOLD))


def halves(row):
    high = row.astype(BF16)
    return [high, (row - high.astype(F32)).astype(BF16)]


def second_back_kernel(
    per, pieces, sc, qt, kn, kt, vn, dot_, ot, lse, gq, gkv,
    dk_i, dv_i, dqa, go, gox, gain, gain_m, n1_h, wt_h, *rest
):
    r2, r3, dk_o, dv_o = rest[:4]
    outs = rest[4 : 4 + pieces]
    dk, dv, dqb, zq, zd, n1, wt, gs, sems = rest[4 + pieces :]
    step = pl.program_id(0)
    cols = dk.shape[0]
    copies = [
        pltpu.make_async_copy(n1_h, n1, sems.at[0]),
        pltpu.make_async_copy(wt_h, wt, sems.at[1]),
    ]

    @pl.when(step == 0)
    def _():
        for copy in copies:
            copy.start()
        dk[...] = dk_i[...]
        dv[...] = dv_i[...]

    dq = backward_block(1, per, sc, qt, kn, kt, vn, dot_, ot, lse, gq, gkv, dk, dv, zq, zd)
    at = pl.multiple_of(step * BLK, BLK)
    for h, part in enumerate(dq):
        dqb[h * HEAD : (h + 1) * HEAD, pl.ds(at, BLK)] = part.astype(BF16)

    @pl.when(step == pl.num_programs(0) - 1)
    def _():
        for copy in copies:
            copy.wait()
        both = dqb.shape[1]
        dkb, dvb = dk[...].astype(BF16), dv[...].astype(BF16)
        dk_o[...] = dkb[:, :both]
        dv_o[...] = dvb[:, :both]
        grads = jnp.concatenate([dkb[:, both:], dqb[...], dvb[:, both:]], axis=0)
        part = nn(grads.T, wt[0 : 3 * cols, :]).astype(BF16)
        r2[...] = part[: both // 2]
        r3[...] = part[both // 2 :]
        gt = [
            nn(dkb, n1[...]),
            nn(dqa[...], n1[:both, :]) + nn(dqb[...], n1[both:, :]),
            nn(dvb, n1[...]),
        ]
        total = jnp.zeros((FOLD, gain.shape[1]), F32)
        for j in range(3):
            total += folded(gt[j] * wt[j * cols : (j + 1) * cols, :].astype(F32))
        gain_a = jnp.sum(total, axis=0, keepdims=True) / gain[...]
        gt.append(go[...] + gox[...].astype(F32))
        gs[...] = jnp.concatenate(gt, axis=0).T.astype(BF16)
        depth = gs.shape[0] // pieces
        extra = halves(gain_a) + halves(jnp.sum(gain_m[...], axis=0, keepdims=True))
        extra.append(jnp.zeros((EXTRA - len(extra), gain.shape[1]), BF16))
        extra = jnp.concatenate(extra, axis=0)
        for j, out in enumerate(outs):
            start = pl.multiple_of((sc[1] ^ j) * depth, 16) if pieces > 1 else 0
            out[0:depth, :] = gs[pl.ds(start, depth), :]
            out[depth : depth + EXTRA, :] = extra


def back_specs(half, total, cols):
    blocks = total // BLK // 2
    return [
        SMEM,
        pl.BlockSpec((cols, BLK), lambda i: (1, half * blocks + i)),
        whole((total, cols)),
        pl.BlockSpec((cols, total), lambda i: (0, 0)),
        whole((total, cols)),
        pl.BlockSpec((cols, BLK), lambda i: (0, i)),
        pl.BlockSpec((cols, BLK), lambda i: (0, i)),
        pl.BlockSpec((8, BLK), lambda i: (0, i)),
        whole((1, total)),
        whole((total, 128)),
    ]


def spread_scratch(cols):
    return [pltpu.VMEM((cols // HEAD, cols, BLK), BF16)] * 2


def first_back(sc, qkvt, kn, vn, dout, out, lse, gq, gkv):
    total, cols = kn.shape
    blocks = total // BLK // 2
    return pl.pallas_call(
        functools.partial(first_back_kernel, total // 4 // BLK),
        grid=(blocks,),
        in_specs=back_specs(0, total, cols),
        out_specs=[
            pl.BlockSpec((cols, BLK), lambda i: (0, i)),
            whole((cols, total)),
            whole((cols, total)),
        ],
        out_shape=[
            shape((cols, blocks * BLK), BF16),
            shape((cols, total), F32),
            shape((cols, total), F32),
        ],
        scratch_shapes=[pltpu.VMEM((cols, total), F32)] * 2 + spread_scratch(cols),
        name="attention_back",
        cost_estimate=cost(20),
    )(sc, qkvt, kn, qkvt, vn, dout, out, lse, gq, gkv)


def second_back(pieces, sc, qkvt, kn, vn, dout, out, lse, gq, gkv, dk, dv, dqa, go, gox, gain, gain_m, n1, wt):
    total, cols = kn.shape
    blocks = total // BLK // 2
    both = blocks * BLK
    width = n1.shape[1]
    piece = (width // pieces + EXTRA, 4 * cols)
    return pl.pallas_call(
        functools.partial(second_back_kernel, total // 4 // BLK, pieces),
        grid=(blocks,),
        in_specs=back_specs(1, total, cols)
        + [whole((cols, total))] * 2
        + [whole((cols, both))]
        + [whole((cols, width))] * 2
        + [whole((1, width)), whole(gain_m.shape)]
        + [HBM] * 2,
        out_specs=[whole((both // 2, width))] * 2
        + [whole((cols, both))] * 2
        + [whole(piece)] * pieces,
        out_shape=[shape((both // 2, width), BF16)] * 2
        + [shape((cols, both), BF16)] * 2
        + [shape(piece, BF16)] * pieces,
        scratch_shapes=[pltpu.VMEM((cols, total), F32)] * 2
        + [pltpu.VMEM((cols, both), BF16)]
        + spread_scratch(cols)
        + [
            pltpu.VMEM(n1.shape, BF16),
            pltpu.VMEM(wt.shape, BF16),
            pltpu.VMEM((width, 4 * cols), BF16),
            pltpu.SemaphoreType.DMA((2,)),
        ],
        compiler_params=room(48),
        name="attention_back_end",
        cost_estimate=cost(0.01),
    )(sc, qkvt, kn, qkvt, vn, dout, out, lse, gq, gkv, dk, dv, dqa, go, gox, gain, gain_m, n1, wt)


def rows_kernel(fn, counts, n_const, n_out, chunks, split, *refs):
    ins = []
    for count in counts:
        ins.append(refs[:count])
        refs = refs[count:]
    n_in = len(ins)
    consts, refs = refs[:n_const], refs[n_const:]
    outs, refs = refs[:n_out], refs[n_out:]
    pieces, refs = refs[:split], refs[split:]
    sums, refs = refs[: len(refs) - n_in - n_out - 2], refs[len(refs) - n_in - n_out - 2 :]
    held, made, (in_sem, out_sem) = refs[:n_in], refs[n_in:-2], refs[-2:]
    size = held[0].shape[0] // chunks

    def part(c):
        return pl.ds(pl.multiple_of(c * size, size), size)

    def arrival(i, c):
        src = ins[i][c] if len(ins[i]) > 1 else ins[i][0].at[part(c)]
        return pltpu.make_async_copy(src, held[i].at[part(c)], in_sem.at[i, c])

    def departure(i, c):
        return pltpu.make_async_copy(made[i].at[part(c)], outs[i].at[part(c)], out_sem.at[i, c])

    def apart(c):
        return pltpu.make_async_copy(made[-1].at[part(c)], pieces[c], out_sem.at[n_out, c])

    for c in range(chunks):
        for i in range(n_in):
            arrival(i, c).start()
    def each(c, of_chunk, many):
        if not many:
            of_chunk(c)
            return
        for known in range(chunks):

            @pl.when(c == known)
            def _(known=known):
                of_chunk(known)

    def body(c, totals):
        for i in range(n_in):
            each(c, lambda c, i=i: arrival(i, c).wait(), len(ins[i]) > 1)
        where = pl.ds(pl.multiple_of(c * size, size), size)
        results, adds = fn([r[where, :] for r in held], [r[...] for r in consts])
        for i, value in enumerate(results):
            made[i][where, :] = value
        if split:
            each(c, lambda c: apart(c).start(), True)
        for i in range(n_out):
            departure(i, c).start()
        return tuple(t + a for t, a in zip(totals, adds))

    totals = lax.fori_loop(0, chunks, body, tuple(jnp.zeros(r.shape, F32) for r in sums))
    for ref, t in zip(sums, totals):
        ref[...] = t
    for c in range(chunks):
        if split:
            apart(c).wait()
        for i in range(n_out):
            departure(i, c).wait()


def by_rows(name, fn, ins, arrived, consts, kinds, sums=(), chunks=2, split=0):
    near = len(ins)
    ins = (*ins, *arrived)
    dims = ins[0].shape
    flat = [v if isinstance(v, tuple) else (v,) for v in ins]
    return pl.pallas_call(
        functools.partial(
            rows_kernel, fn, [len(v) for v in flat], len(consts), len(kinds), chunks, split
        ),
        in_specs=[HBM] * near
        + [ANY] * sum(len(v) for v in flat[near:])
        + [VMEM] * len(consts),
        out_specs=[HBM] * (len(kinds) + split) + [VMEM] * len(sums),
        out_shape=[shape(dims, k) for k in kinds]
        + [shape((dims[0] // chunks, dims[1]), kinds[-1])] * split
        + [shape(d, F32) for d in sums],
        scratch_shapes=[pltpu.VMEM(dims, v[0].dtype) for v in flat]
        + [pltpu.VMEM(dims, k) for k in kinds]
        + [
            pltpu.SemaphoreType.DMA((len(ins), chunks)),
            pltpu.SemaphoreType.DMA((len(kinds) + 1, chunks)),
        ],
        compiler_params=room(24),
        name=name,
        cost_estimate=cost(0.01),
    )(*[part for v in flat for part in v], *consts)


def out_kernel(om, ox, wm, wx, own, other, omv, oxv, wmv, wxv, ownv, otherv, sems):
    rows = own.shape[0]
    copies = [
        pltpu.make_async_copy(src, dst, sems.at[i])
        for i, (src, dst) in enumerate(((om, omv), (ox, oxv), (wm, wmv), (wx, wxv)))
    ]
    for copy in copies:
        copy.start()
    for copy in copies:
        copy.wait()
    leave = [
        pltpu.make_async_copy(made, out, sems.at[4 + i])
        for i, (made, out) in enumerate(((otherv, other), (ownv, own)))
    ]

    def body(i, carry):
        where = pl.ds(pl.multiple_of((1 - i) * rows, rows), rows)
        part = (nn(omv[:, where].T, wmv[...]) + nn(oxv[:, where].T, wxv[...])).astype(BF16)
        for c, (made, copy) in enumerate(zip((otherv, ownv), leave)):

            @pl.when(i == c)
            def _(made=made, copy=copy):
                made[...] = part
                copy.start()

        return carry

    lax.fori_loop(0, 2, body, 0)
    for copy in leave:
        copy.wait()


def out_projection(om, ox, wm, wx):
    cols, both = om.shape
    width = wm.shape[1]
    made = (both // 2, width)
    return pl.pallas_call(
        out_kernel,
        in_specs=[HBM, ANY, HBM, ANY],
        out_specs=[HBM] * 2,
        out_shape=[shape(made, BF16)] * 2,
        scratch_shapes=[pltpu.VMEM(v.shape, BF16) for v in (om, ox, wm, wx)]
        + [pltpu.VMEM(made, BF16)] * 2
        + [pltpu.SemaphoreType.DMA((6,))],
        compiler_params=room(24),
        name="out_projection",
        cost_estimate=cost(0.01),
    )(om, ox, wm, wx)


def middle_rows(held, consts):
    tokens, own, got = (v.astype(F32) for v in held)
    h1 = tokens + (own + got)
    scale = lax.rsqrt(jnp.mean(h1 * h1, axis=-1, keepdims=True) + eps_norm)
    return (h1, (h1 * scale * consts[0]).astype(BF16)), ()


def middle(tokens, own, got, gain):
    return by_rows("middle", middle_rows, (tokens, own), (got,), (gain,), (F32, BF16), split=2)


def mlp_kernel(at, aliased, na, nb, ya, yb, w, *refs):
    ma, mb, da, db, hid_o, dgu_o, nv, yv, wv, mv, dv, hv, gv, in_sem, w_sem, out_sem = refs[aliased:]
    rows, units = na.shape[0], hv.shape[1]
    arrivals, departures = [], []
    for c, (n, y, m, d) in enumerate(((na, ya, ma, da), (nb, yb, mb, db))):
        part, place = pl.ds(c * rows, rows), pl.ds(at, rows)
        arrivals += [
            pltpu.make_async_copy(n, nv.at[part], in_sem.at[0, c]),
            pltpu.make_async_copy(y.at[place], yv.at[part], in_sem.at[1, c]),
        ]
        departures.append(
            [
                pltpu.make_async_copy(dv.at[part], d, out_sem.at[0, c]),
                pltpu.make_async_copy(mv.at[part], m.at[place], out_sem.at[1, c]),
                pltpu.make_async_copy(hv.at[part], hid_o.at[part], out_sem.at[2, c]),
                pltpu.make_async_copy(gv.at[part], dgu_o.at[part], out_sem.at[3, c]),
            ]
        )
    weights = [
        pltpu.make_async_copy(
            w.at[:, pl.ds(j * units, units)], wv.at[:, pl.ds(j * units, units)], w_sem.at[j]
        )
        for j in range(3)
    ]
    for copy in weights + arrivals:
        copy.start()
    for copy in weights + arrivals:
        copy.wait()
    wg, wu, wd = (wv.at[:, pl.ds(j * units, units)] for j in range(3))
    tile = rows if rows < 512 else 512

    def body(i, carry):
        part = pl.ds(pl.multiple_of(i * tile, tile), tile)
        n2 = nv[part, :]
        gate, up = nn(n2, wg[...]), nn(n2, wu[...])
        dhid = nn(yv[part, :], wd[...])
        square = gate * gate
        share = 0.5 * jnp.tanh(gate * (ROOT + ROOT * 0.044715 * square)) + 0.5
        value = gate * share
        slope = share + value * (1.0 - share) * (2.0 * ROOT + 6.0 * ROOT * 0.044715 * square)
        dgate = (dhid * up * slope).astype(BF16)
        dup = (dhid * value).astype(BF16)
        hidden = (value * up).astype(BF16)
        dv[part, :] = (nt(dgate, wg[...]) + nt(dup, wu[...])).astype(BF16)
        hv[part, :] = hidden
        gv[part, 0:units] = dgate
        gv[part, units : 2 * units] = dup
        mv[part, :] = nt(hidden, wd[...]).astype(BF16)
        for c, copies in enumerate(departures):

            @pl.when(i == c * rows // tile)
            def _(copies=copies):
                for copy in copies:
                    copy.start()

        return carry

    lax.fori_loop(0, 2 * rows // tile, body, 0)
    for copies in departures:
        for copy in copies:
            copy.wait()


def mlp_both(na, nb, ya, yb, weights, at=0, into=(), mib=32):
    rows, width = na.shape
    units = weights.shape[1] // 3
    both = 2 * rows
    return pl.pallas_call(
        functools.partial(mlp_kernel, at, len(into)),
        in_specs=[ANY] * 4 + [HBM] * (1 + len(into)),
        out_specs=[HBM] * 6,
        out_shape=[shape(ya.shape, BF16)] * 2
        + [shape((rows, width), BF16)] * 2
        + [shape((both, units), BF16), shape((both, 2 * units), BF16)],
        scratch_shapes=[
            pltpu.VMEM((both, width), BF16),
            pltpu.VMEM((both, width), BF16),
            pltpu.VMEM(weights.shape, BF16),
            pltpu.VMEM((both, width), BF16),
            pltpu.VMEM((both, width), BF16),
            pltpu.VMEM((both, units), BF16),
            pltpu.VMEM((both, 2 * units), BF16),
            pltpu.SemaphoreType.DMA((2, 2)),
            pltpu.SemaphoreType.DMA((3,)),
            pltpu.SemaphoreType.DMA((4, 2)),
        ],
        input_output_aliases={5 + i: i for i in range(len(into))},
        compiler_params=room(mib),
        name="mlp",
        cost_estimate=cost(8),
    )(na, nb, ya, yb, weights, *into)


def mlp_weights_kernel(order, n_in, *refs):
    ins, (out, *held, total, made, sems, sem) = refs[:n_in], refs[n_in:]
    copies = []
    for group, moves in enumerate(order):
        for which, start, rows, at in moves:
            copy = pltpu.make_async_copy(
                ins[which].at[pl.ds(start, rows)], held[group].at[pl.ds(at, rows)], sems.at[len(copies)]
            )
            copies.append((at + rows, copy))
    size = held[0].shape[0] // 2
    copies.sort(key=lambda v: v[0])
    for _, copy in copies:
        copy.start()
    wide = held[2].shape[1]

    def body(i, carry):
        for c in range(2):

            @pl.when(i == c)
            def _(c=c):
                for end, copy in copies:
                    if c * size < end <= (c + 1) * size:
                        copy.wait()

        rows = pl.ds(pl.multiple_of(i * size, size), size)
        n2, dy, dgu, hidden = (r[rows, :] for r in held)
        for at, left, right in ((0, n2, dgu), (wide, dy, hidden)):
            cols = pl.ds(at, right.shape[1])
            new = nn(left.T, right) + total[:, cols]
            total[:, cols] = new
            made[:, cols] = new.astype(BF16)
        return carry

    total[...] = jnp.zeros(total.shape, F32)
    lax.fori_loop(0, 2, body, 0)
    leave = pltpu.make_async_copy(made, out, sem)
    leave.start()
    leave.wait()


def mlp_weights(n2, dy, dgu, hidden):
    ins = (*n2, *dy, *dgu, *hidden)
    rows = n2[0].shape[0]
    half = rows // 2
    first = [(0, 0, rows, 0), (1, 0, rows, rows)]
    order = [
        first + [(2, 0, half, 2 * rows), (4, 0, half, 2 * rows + half), (3, 0, half, 3 * rows), (5, 0, half, 3 * rows + half)],
        [(6 + j, 0, rows, j * rows) for j in range(4)],
    ]
    for base in (10, 13):
        order.append(
            [
                (base, 0, 2 * rows, 0),
                (base + 1, 0, half, 2 * rows),
                (base + 2, 0, half, 2 * rows + half),
                (base + 1, half, half, 3 * rows),
                (base + 2, half, half, 3 * rows + half),
            ]
        )
    width = n2[0].shape[1]
    dims = (width, dgu[0].shape[1] + hidden[0].shape[1])
    return pl.pallas_call(
        functools.partial(mlp_weights_kernel, order, len(ins)),
        in_specs=[HBM] * len(ins),
        out_specs=HBM,
        out_shape=shape(dims, BF16),
        scratch_shapes=[
            pltpu.VMEM((4 * rows, v.shape[1]), BF16) for v in (n2[0], dy[0], dgu[0], hidden[0])
        ]
        + [
            pltpu.VMEM(dims, F32),
            pltpu.VMEM(dims, BF16),
            pltpu.SemaphoreType.DMA((sum(len(v) for v in order),)),
            pltpu.SemaphoreType.DMA,
        ],
        compiler_params=room(48),
        name="mlp_weights",
        cost_estimate=cost(10),
    )(*ins)


def middle_back_rows(held, consts):
    dy, h1, *shares = (v.astype(F32) for v in held)
    dn2 = sum(shares[1:], shares[0])
    scale = lax.rsqrt(jnp.mean(h1 * h1, axis=-1, keepdims=True) + eps_norm)
    hat = dn2 * consts[0]
    dh1 = (
        dy
        + scale * hat
        - h1 * (scale * scale * scale) * jnp.mean(hat * h1, axis=-1, keepdims=True)
    )
    return (dh1, dh1.astype(BF16)), (folded(dn2 * h1 * scale),)


def middle_back(dy, h1, a, b, c, gain):
    return by_rows(
        "middle_back",
        middle_back_rows,
        (dy, h1, a),
        (b, c),
        (gain,),
        (F32, BF16),
        sums=((FOLD, dy.shape[1]),),
    )


def out_back_kernel(own, other, wm, wx, om, ox, dm_o, dx_o, gm_o, gx_o, *scratch):
    refs = (own, other, wm, wx, om, ox)
    held, made, sems = scratch[:6], scratch[6:10], scratch[10]
    copies = [pltpu.make_async_copy(src, dst, sems.at[i]) for i, (src, dst) in enumerate(zip(refs, held))]
    for copy in copies:
        copy.start()
    ownv, otherv, wmv, wxv, omv, oxv = held
    dm, dx, gm, gx = made
    rows = own.shape[0]
    for copy in copies:
        copy.wait()
    leave = [
        pltpu.make_async_copy(src, dst, sems.at[6 + i])
        for i, (src, dst) in enumerate(((dx, dx_o), (dm, dm_o), (gx, gx_o), (gm, gm_o)))
    ]
    for i, (w, out) in enumerate(((wxv, dx), (wmv, dm))):
        for at, ref in ((0, ownv), (rows, otherv)):
            out[:, at : at + rows] = nt(w[...], ref[...]).astype(BF16)
        leave[i].start()
    gx[...] = (nn(oxv[:, :rows], ownv[...]) + nn(oxv[:, rows:], otherv[...])).astype(BF16)
    leave[2].start()
    gm[...] = nn(omv[:, :rows], ownv[...]) + nn(omv[:, rows:], otherv[...])
    leave[3].start()
    for copy in leave:
        copy.wait()


def out_back(own, other, wm, wx, om, ox):
    cols, both = om.shape
    width = own.shape[1]
    ins = (own, other, wm, wx, om, ox)
    outs = [
        ((cols, both), BF16),
        ((cols, both), BF16),
        ((cols, width), F32),
        ((cols, width), BF16),
    ]
    return pl.pallas_call(
        out_back_kernel,
        in_specs=[HBM, ANY, HBM, ANY, HBM, ANY],
        out_specs=[HBM] * 4,
        out_shape=[shape(*v) for v in outs],
        scratch_shapes=[pltpu.VMEM(v.shape, BF16) for v in ins]
        + [pltpu.VMEM(*v) for v in outs]
        + [pltpu.SemaphoreType.DMA((10,))],
        compiler_params=room(24),
        name="out_back",
        cost_estimate=cost(0.01),
    )(*ins)


def rows_back_kernel(dk, dq, dv, wt, a_o, b_o):
    rows = a_o.shape[0]

    def body(i, carry):
        where = pl.ds(pl.multiple_of(i * rows, rows), rows)
        grads = jnp.concatenate([dk[:, where], dq[:, where], dv[:, where]], axis=0)
        part = nn(grads.T, wt[...]).astype(BF16)
        for c, ref in enumerate((a_o, b_o)):

            @pl.when(i == c)
            def _(ref=ref):
                ref[...] = part

        return carry

    lax.fori_loop(0, 2, body, 0)


def rows_back(dk, dq, dv, wt):
    cols, both = dq.shape
    width = wt.shape[1]
    return pl.pallas_call(
        rows_back_kernel,
        out_shape=[shape((both // 2, width), BF16)] * 2,
        compiler_params=room(24),
        name="rows_back",
        cost_estimate=cost(0.01),
    )(dk, dq, dv, wt)


def last_rows(held, consts):
    x, dh1, *shares = (v.astype(F32) for v in held)
    dn1 = sum(shares[1:], shares[0])
    scale = lax.rsqrt(jnp.mean(x * x, axis=-1, keepdims=True) + eps_norm)
    hat = dn1 * consts[0]
    out = (
        dh1
        + scale * hat
        - x * (scale * scale * scale) * jnp.mean(hat * x, axis=-1, keepdims=True)
    )
    return (out.astype(BF16),), ()


def last(tokens, dh1, a, b, c, gain):
    return by_rows("last", last_rows, (tokens, dh1, a), (b, c), (gain,), (BF16,))[0]


def grads_sum_kernel(count, *refs):
    ins, outs, gains_o = refs[:count], refs[count:-1], refs[-1]
    rows, cols = outs[0].shape
    total = ins[0][0:rows, :].astype(F32)
    for ref in ins[1:]:
        total = total + ref[0:rows, :].astype(F32)
    for j, ref in enumerate(outs):
        ref[...] = total[:, j * cols : (j + 1) * cols]
    tail = [ref[rows : rows + EXTRA, :].astype(F32) for ref in ins]
    gains = tail[0]
    for part in tail[1:]:
        gains = gains + part
    gains = gains[0:4, :] + gains[4:8, :]
    gains_o[...] = jnp.concatenate(
        [gains[0:1, :] + gains[1:2, :], gains[2:3, :] + gains[3:4, :]], axis=0
    )


def grads_sum(parts):
    rows, width = parts[0].shape
    rows -= EXTRA
    return pl.pallas_call(
        functools.partial(grads_sum_kernel, len(parts)),
        out_shape=[shape((rows, width // 4), F32)] * 4 + [shape((2, width), F32)],
        compiler_params=room(16),
        name="grads_sum",
        cost_estimate=cost(0.01),
    )(*parts)


def local(
    dp,
    mp,
    tokens,
    w_query,
    w_key,
    w_value,
    w_out,
    w_gate,
    w_up,
    w_down,
    norm_attn,
    norm_mlp,
    valid_counts,
    group_ids,
    cotangent,
):
    me, row = lax.axis_index("mp"), lax.axis_index("dp")
    cols = w_query.shape[1]
    length = group_ids.shape[1]

    def core(v):
        return lax.ppermute(v, "mp", [(i, i ^ 1) for i in range(mp)])

    def across(v):
        return lax.ppermute(v, "mp", [(i, i ^ 2) for i in range(mp)])

    def far(v, k):
        return lax.ppermute(v, "dp", [(i, i ^ k) for i in range(dp)])

    def after(v, *others):
        return lax.optimization_barrier((v, *others))[0]

    def summed(a, b):
        return (a.astype(F32) + b.astype(F32)).astype(BF16)

    direct = dp <= DIRECT
    gain_a, gain_m = norm_attn[None], norm_mlp[None]

    gq = group_ids
    flat = group_ids[0]
    valid = valid_counts[0]
    tiles = flat.reshape(length // BLK, BLK)
    low = jnp.sum(flat[None, :] < tiles[:, :1], axis=1) // BLK
    high = jnp.minimum(jnp.sum(flat[None, :] <= tiles[:, -1:], axis=1), valid)
    high = (high + BLK - 1) // BLK
    head = jnp.stack([me, row, valid, valid, valid, valid, valid, valid])
    sc = jnp.concatenate([head, low, high]).astype(jnp.int32)
    keyed = jnp.where(jnp.arange(length, dtype=jnp.int32) < valid, flat, -1)
    gkv = jnp.broadcast_to(keyed[:, None], (length, 128))

    tok2 = across(tokens)
    w_attn = jnp.concatenate([w_key, w_query, w_value, w_out], axis=1)
    w_mlp = jnp.concatenate([w_gate, w_up, w_down], axis=1)
    if direct:
        near = [w_attn] + [far(w_attn, k) for k in range(2, dp, 2)]
        near[1] = after(near[1], sc, gkv, w_mlp)
        w_pieces = [p for v in near for p in (v, far(v, 1))]
        tok1 = core(after(tokens, w_pieces[1]))
    else:
        w_pieces = [lax.all_gather(w_attn, "dp", axis=0, tiled=True)]
        tok1 = core(tokens)
    w_mlp = lax.all_gather(w_mlp, "dp", axis=0, tiled=True)
    tok3 = core(after(tok2, *w_pieces[1::2]))

    n1, qkvt, kn, vn, wt, wo = qkv(sc, (tokens, tok1, tok2, tok3), gain_a, w_pieces, cols)
    wo_x = across(wo)
    dy0 = cotangent
    dy2 = across(after(cotangent, tok2))
    dy1 = core(after(cotangent, tok3))

    o_far, lse_far = attention(1, sc, qkvt, kn, gq, gkv)
    o_x = across(after(o_far, dy2, wo_x))
    dy3 = core(after(dy2, o_far))
    o_own, lse_own = attention(0, after(sc, o_far), qkvt, kn, gq, gkv)
    p_own, p_other = out_projection(o_own, o_x, wo, wo_x)
    h1, n2, n2_a, n2_b = middle(tokens, p_own, core(p_other), gain_m)

    half = n2.shape[0] // 2
    n2_1 = core(n2)
    far_a = across(n2_a)
    far_b = across(n2_b)
    m0, m1, d0, d1, hid_o, dgu_o = mlp_both(n2, n2_1, dy0, dy1, w_mlp, mib=60)
    side_a = core(after(far_a, d0))
    m2, m3, d2a, d3a, hid_a, dgu_a = mlp_both(far_a, side_a, dy2, dy3, w_mlp)
    dsum_a = summed(d2a, core(d3a))
    dx_a = across(dsum_a)
    side_b = core(after(far_b, d2a))
    far_b = after(far_b, dsum_a)
    m2, m3, d2b, d3b, hid_b, dgu_b = mlp_both(far_b, side_b, dy2, dy3, w_mlp, half, (m2, m3))

    d_sum = summed(d2b, core(after(d3b, dx_a)))
    dx_b = across(d_sum)
    mlp_all = mlp_weights(
        (n2, n2_1, far_a, side_a, far_b, side_b),
        (dy0, dy1, dy2, dy3),
        (dgu_o, dgu_a, dgu_b),
        (after(hid_o, d_sum), hid_a, hid_b),
    )
    mlp_grads = lax.psum_scatter(mlp_all, "dp", scatter_dimension=0, tiled=True)
    m_sum, m_core = summed(after(m2, d_sum), core(m3)), core(after(m1, d_sum))
    dh1, da, gain_m_part = middle_back(
        dy0,
        h1,
        d0,
        core(after(d1, d_sum)),
        (dx_a, after(dx_b, mlp_all, m_sum, m_core)),
        gain_m,
    )

    do_own, do_send, go, go_send = out_back(da, core(da), wo, wo_x, o_own, o_x)
    do_far = across(do_send)
    go_x = across(go_send)
    m_x = across(after(m_sum, do_send))
    dq_own, dk, dv = first_back(sc, qkvt, kn, vn, do_own, o_own, lse_own, gq, gkv)
    r2, r3, dk_own, dv_own, *grads = second_back(
        dp if direct else 1,
        sc, qkvt, kn, vn, do_far, o_far, lse_far, gq, gkv,
        dk, dv, dq_own, go, go_x, gain_a, gain_m_part, n1, wt,
    )
    r_sum = summed(r2, core(after(r3, m_x)))
    r_x = across(r_sum)
    depth = w_query.shape[0]
    parts = []
    if direct:
        others = {}
        for k in range(dp - 2, -1, -2):
            sent = grads[k + 1]
            others[k] = far(after(sent, others[k + dp // 2]) if k + dp // 2 in others else sent, 1)
        for k in range(0, dp, 2):
            near, other = grads[k], after(others[k], r_sum)
            both = summed(near[:depth], other[:depth])
            part = jnp.concatenate([both, near[depth : depth + 4], other[depth : depth + 4]], axis=0)
            parts.append(part if k == 0 else far(part, k))
    r0, r1 = rows_back(after(dk_own, r_sum), dq_own, dv_own, wt)
    grad_tokens = last(tokens, dh1, r0, core(r1), r_x, gain_a)
    output = (
        h1 + (m0.astype(F32) + m_core.astype(F32) + after(m_x, r_sum).astype(F32))
    ).astype(BF16)
    units = w_gate.shape[1]
    grad_gate, grad_up, grad_down = (
        mlp_grads[:, j * units : (j + 1) * units].astype(F32) for j in range(3)
    )
    if direct:
        parts[0] = after(parts[0], grad_tokens, output, grad_gate)
        grad_k, grad_q, grad_v, grad_o, gains = grads_sum(parts)
        gains = gains + core(gains)
        gains = gains + across(gains)
    else:
        width = tokens.shape[1]
        attn_grads = lax.psum_scatter(
            grads[0][:width], "dp", scatter_dimension=0, tiled=True
        ).astype(F32)
        grad_k, grad_q, grad_v, grad_o = jnp.split(attn_grads, 4, axis=1)
        extra = grads[0][width : width + 4].astype(F32)
        gains = lax.psum(extra[0::2] + extra[1::2], ("dp", "mp"))

    return (
        output,
        grad_tokens,
        grad_q,
        grad_k,
        grad_v,
        grad_o,
        grad_gate,
        grad_up,
        grad_down,
        gains[0],
        gains[1],
    )


def solution(mesh):
    rows, weight = P(("dp", "mp"), None), P("dp", "mp")
    return jax.shard_map(
        functools.partial(local, mesh.shape["dp"], mesh.shape["mp"]),
        mesh=mesh,
        in_specs=(rows,) + (weight,) * 7 + (P(), P(), P("dp"), P("dp", None), rows),
        out_specs=(rows, rows) + (weight,) * 7 + (P(), P()),
        check_vma=False,
    )
```

```python
import functools

import jax
import jax.numpy as jnp
from jax import lax
from jax.experimental import pallas as pl
from jax.experimental.pallas import tpu as pltpu
from jax.sharding import PartitionSpec as P

HEAD = 64
BLK = 256
DIRECT = 8
FOLD = 32
EXTRA = 8
ROOT = 0.7978845608028654
eps_norm = 1e-06
neg_large = -1e30
F32 = jnp.float32
BF16 = jnp.bfloat16


def nn(a, b):
    return lax.dot_general(a, b, (((1,), (0,)), ((), ())), preferred_element_type=F32)


def nt(a, b):
    return lax.dot_general(a, b, (((1,), (1,)), ((), ())), preferred_element_type=F32)


def tn(a, b):
    return lax.dot_general(a, b, (((0,), (0,)), ((), ())), preferred_element_type=F32)


def shape(dims, kind):
    return jax.ShapeDtypeStruct(dims, kind)


def whole(dims):
    return pl.BlockSpec(dims, lambda *_: (0,) * len(dims))


SMEM = pl.BlockSpec(memory_space=pltpu.SMEM)
VMEM = pl.BlockSpec(memory_space=pltpu.VMEM)
HBM = pl.BlockSpec(memory_space=pltpu.HBM)
ANY = pl.BlockSpec(memory_space=pl.ANY)


def room(mib):
    return pltpu.CompilerParams(vmem_limit_bytes=mib << 20)


def qkv_kernel(pieces, sc, t0, t1, t2, t3, gain, *rest):
    w_refs, (n1_o, qkvt_o, kn_o, vn_o, wt_o, wo_o, xs, ws) = rest[:pieces], rest[pieces:]
    step = pl.program_id(0)
    cols = kn_o.shape[1]

    @pl.when(step == 0)
    def _():
        if pieces == 1:
            ws[...] = w_refs[0][...]
        else:
            depth = w_refs[0].shape[0]
            for j in range(pieces):
                at = pl.multiple_of((sc[1] ^ j) * depth, 16)
                ws[pl.ds(at, depth), :] = w_refs[j][...]
        turned = ws[...].T
        wt_o[...] = turned[: 3 * cols, :]
        wo_o[...] = turned[3 * cols :, :]

    for j, ref in enumerate((t0, t1, t2, t3)):

        @pl.when(step == j)
        def _(ref=ref):
            xs[...] = ref[...]

    x = xs[...].astype(F32)
    scale = lax.rsqrt(jnp.mean(x * x, axis=-1, keepdims=True) + eps_norm)
    n1 = (x * scale * gain[...]).astype(BF16)
    n1_o[...] = n1
    qkvt_o[...] = nt(wt_o[...], n1).astype(BF16)
    kn_o[...] = nn(n1, ws[:, 0:cols]).astype(BF16)
    vn_o[...] = nn(n1, ws[:, 2 * cols : 3 * cols]).astype(BF16)


def qkv(sc, shards, gain, pieces, cols):
    rows, width = shards[0].shape
    total = rows * len(shards)
    return pl.pallas_call(
        functools.partial(qkv_kernel, len(pieces)),
        grid=(len(shards),),
        in_specs=[SMEM]
        + [whole((rows, width))] * 4
        + [whole((1, width))]
        + [whole(p.shape) for p in pieces],
        out_specs=[
            pl.BlockSpec((rows, width), lambda i: (i, 0)),
            pl.BlockSpec((3 * cols, rows), lambda i: (0, i)),
            pl.BlockSpec((rows, cols), lambda i: (i, 0)),
            pl.BlockSpec((rows, cols), lambda i: (i, 0)),
            whole((3 * cols, width)),
            whole((cols, width)),
        ],
        out_shape=[
            shape((total, width), BF16),
            shape((3 * cols, total), BF16),
            shape((total, cols), BF16),
            shape((total, cols), BF16),
            shape((3 * cols, width), BF16),
            shape((cols, width), BF16),
        ],
        scratch_shapes=[pltpu.VMEM((rows, width), BF16), pltpu.VMEM((width, 4 * cols), BF16)],
        name="qkv",
        cost_estimate=cost(0.01),
    )(sc, *shards, gain, *pieces)


def spread(rows, z_ref):
    heads = rows.shape[0] // HEAD
    z_ref[...] = jnp.zeros(z_ref.shape, z_ref.dtype)
    for h in range(heads):
        z_ref[h, h * HEAD : (h + 1) * HEAD, :] = rows[h * HEAD : (h + 1) * HEAD, :]


def cost(us):
    return pl.CostEstimate(flops=int(us * 1e9), transcendentals=0, bytes_accessed=1024)


def span(sc, half, per, blocks):
    me = sc[0]
    stored = half * blocks + pl.program_id(0)
    shard = (stored // per) ^ me
    place = shard * per + lax.rem(stored, per)
    low, high = sc[8 + place] // per, (sc[16 + place] + per - 1) // per
    has_own = jnp.logical_and(low <= shard, shard < high)
    count = jnp.maximum(high - low, 0) - has_own.astype(jnp.int32)

    def at(t):
        other = low + t - 1
        other = jnp.where(t == 0, shard, other + (other >= shard).astype(jnp.int32))
        return other, other ^ me

    return place, count + 1, at


def allowed(gkv, queries, place, shard, size, own=True):
    keys = gkv[pl.ds(pl.multiple_of(shard * size, size), size), :]
    mask = jnp.concatenate([keys] * (BLK // 128), axis=1) == queries
    if not own:
        return mask
    key_at = lax.broadcasted_iota(jnp.int32, mask.shape, 0)
    query_at = lax.broadcasted_iota(jnp.int32, mask.shape, 1) + (place * BLK - shard * size)
    return mask | (key_at == query_at)


def forward_kernel(half, per, sc, qt, kn, vt, gq, gkv, ot, lse, zq):
    heads = qt.shape[0] // HEAD
    size = per * BLK
    place, count, at = span(sc, half, per, pl.num_programs(0))
    spread(qt, zq)
    queries = gq[:, pl.ds(pl.multiple_of(place * BLK, BLK), BLK)]

    def scores(t, own):
        shard, stored = at(t)
        mask = allowed(gkv, queries, place, shard, size, own)
        where = pl.ds(pl.multiple_of(stored * size, size), size)
        keys = kn[where, :]
        return where, [jnp.where(mask, nn(keys, zq[h]), neg_large) for h in range(heads)]

    def mixed(h, where, p):
        return nn(vt[h * HEAD : (h + 1) * HEAD, where], p.astype(BF16))

    carry = []
    where, first = scores(0, True)
    for h, s in enumerate(first):
        top = jnp.max(s, axis=0, keepdims=True)
        p = jnp.exp(s - top)
        carry.append((top, jnp.sum(p, axis=0, keepdims=True), mixed(h, where, p)))

    def body(t, carry):
        where, more = scores(t, False)
        out = []
        for h, s in enumerate(more):
            top, total, acc = carry[h]
            higher = jnp.maximum(top, jnp.max(s, axis=0, keepdims=True))
            p = jnp.exp(s - higher)
            fade = jnp.exp(top - higher)
            out.append(
                (
                    higher,
                    fade * total + jnp.sum(p, axis=0, keepdims=True),
                    fade * acc + mixed(h, where, p),
                )
            )
        return tuple(out)

    carry = lax.fori_loop(1, count, body, tuple(carry))
    for h, (top, total, acc) in enumerate(carry):
        ot[h * HEAD : (h + 1) * HEAD, :] = (acc / total).astype(BF16)
        lse[h : h + 1, :] = top + jnp.log(total)


def attention(half, sc, qkvt, kn, gq, gkv):
    cols3, total = qkvt.shape
    cols = cols3 // 3
    blocks = total // BLK // 2
    per = total // 4 // BLK
    return pl.pallas_call(
        functools.partial(forward_kernel, half, per),
        grid=(blocks,),
        in_specs=[
            SMEM,
            pl.BlockSpec((cols, BLK), lambda i: (1, half * blocks + i)),
            whole((total, cols)),
            pl.BlockSpec((cols, total), lambda i: (2, 0)),
            whole((1, total)),
            whole((total, 128)),
        ],
        out_specs=[
            pl.BlockSpec((cols, BLK), lambda i: (0, i)),
            pl.BlockSpec((8, BLK), lambda i: (0, i)),
        ],
        out_shape=[shape((cols, blocks * BLK), BF16), shape((8, blocks * BLK), F32)],
        scratch_shapes=[pltpu.VMEM((cols // HEAD, cols, BLK), BF16)],
        compiler_params=room(32),
        name="attention",
        cost_estimate=cost(12),
    )(sc, qkvt, kn, qkvt, gq, gkv)


def backward_block(
    half, per, sc, qt, kn, kt, vn, dot_, ot, lse, gq, gkv, dk, dv, zq, zd
):
    heads = qt.shape[0] // HEAD
    size = per * BLK
    place, count, at = span(sc, half, per, pl.num_programs(0))
    queries = gq[:, pl.ds(pl.multiple_of(place * BLK, BLK), BLK)]
    spread(qt, zq)
    spread(dot_, zd)
    deltas = []
    for h in range(heads):
        part = slice(h * HEAD, (h + 1) * HEAD)
        deltas.append(
            jnp.sum(dot_[part, :].astype(F32) * ot[part, :].astype(F32), axis=0, keepdims=True)
        )

    def body(t, carry):
        shard, stored = at(t)
        mask = allowed(gkv, queries, place, shard, size)
        at_keys = pl.ds(pl.multiple_of(stored * size, size), size)
        keys, values = kn[at_keys, :], vn[at_keys, :]
        out = []
        for h in range(heads):
            part = slice(h * HEAD, (h + 1) * HEAD)
            s = jnp.where(mask, nn(keys, zq[h]), neg_large)
            p = jnp.exp(s - lse[h : h + 1, :])
            ds = (p * (nn(values, zd[h]) - deltas[h])).astype(BF16)
            dv[part, at_keys] += nt(dot_[part, :], p.astype(BF16))
            dk[part, at_keys] += nt(qt[part, :], ds)
            out.append(carry[h] + nn(kt[part, at_keys], ds))
        return tuple(out)

    zero = jnp.zeros((HEAD, BLK), F32)
    return lax.fori_loop(0, count, body, (zero,) * heads)


def first_back_kernel(per, sc, qt, kn, kt, vn, dot_, ot, lse, gq, gkv, dqt, dk_o, dv_o, dk, dv, zq, zd):
    step = pl.program_id(0)

    @pl.when(step == 0)
    def _():
        dk[...] = jnp.zeros(dk.shape, F32)
        dv[...] = jnp.zeros(dv.shape, F32)

    dq = backward_block(0, per, sc, qt, kn, kt, vn, dot_, ot, lse, gq, gkv, dk, dv, zq, zd)
    for h, part in enumerate(dq):
        dqt[h * HEAD : (h + 1) * HEAD, :] = part.astype(BF16)

    @pl.when(step == pl.num_programs(0) - 1)
    def _():
        dk_o[...] = dk[...]
        dv_o[...] = dv[...]


def folded(v):
    return sum(v[at : at + FOLD, :] for at in range(0, v.shape[0], FOLD))


def halves(row):
    high = row.astype(BF16)
    return [high, (row - high.astype(F32)).astype(BF16)]


def second_back_kernel(
    per, pieces, sc, qt, kn, kt, vn, dot_, ot, lse, gq, gkv,
    dk_i, dv_i, dqa, go, gox, gain, gain_m, n1_h, wt_h, *rest
):
    r2, r3, dk_o, dv_o = rest[:4]
    outs = rest[4 : 4 + pieces]
    dk, dv, dqb, zq, zd, n1, wt, gs, sems = rest[4 + pieces :]
    step = pl.program_id(0)
    cols = dk.shape[0]
    copies = [
        pltpu.make_async_copy(n1_h, n1, sems.at[0]),
        pltpu.make_async_copy(wt_h, wt, sems.at[1]),
    ]

    @pl.when(step == 0)
    def _():
        for copy in copies:
            copy.start()
        dk[...] = dk_i[...]
        dv[...] = dv_i[...]

    dq = backward_block(1, per, sc, qt, kn, kt, vn, dot_, ot, lse, gq, gkv, dk, dv, zq, zd)
    at = pl.multiple_of(step * BLK, BLK)
    for h, part in enumerate(dq):
        dqb[h * HEAD : (h + 1) * HEAD, pl.ds(at, BLK)] = part.astype(BF16)

    @pl.when(step == pl.num_programs(0) - 1)
    def _():
        for copy in copies:
            copy.wait()
        both = dqb.shape[1]
        dkb, dvb = dk[...].astype(BF16), dv[...].astype(BF16)
        dk_o[...] = dkb[:, :both]
        dv_o[...] = dvb[:, :both]
        grads = jnp.concatenate([dkb[:, both:], dqb[...], dvb[:, both:]], axis=0)
        part = nn(grads.T, wt[0 : 3 * cols, :]).astype(BF16)
        r2[...] = part[: both // 2]
        r3[...] = part[both // 2 :]
        gt = [
            nn(dkb, n1[...]),
            nn(dqa[...], n1[:both, :]) + nn(dqb[...], n1[both:, :]),
            nn(dvb, n1[...]),
        ]
        total = jnp.zeros((FOLD, gain.shape[1]), F32)
        for j in range(3):
            total += folded(gt[j] * wt[j * cols : (j + 1) * cols, :].astype(F32))
        gain_a = jnp.sum(total, axis=0, keepdims=True) / gain[...]
        gt.append(go[...] + gox[...].astype(F32))
        gs[...] = jnp.concatenate(gt, axis=0).T.astype(BF16)
        depth = gs.shape[0] // pieces
        extra = halves(gain_a) + halves(jnp.sum(gain_m[...], axis=0, keepdims=True))
        extra.append(jnp.zeros((EXTRA - len(extra), gain.shape[1]), BF16))
        extra = jnp.concatenate(extra, axis=0)
        for j, out in enumerate(outs):
            start = pl.multiple_of((sc[1] ^ j) * depth, 16) if pieces > 1 else 0
            out[0:depth, :] = gs[pl.ds(start, depth), :]
            out[depth : depth + EXTRA, :] = extra


def back_specs(half, total, cols):
    blocks = total // BLK // 2
    return [
        SMEM,
        pl.BlockSpec((cols, BLK), lambda i: (1, half * blocks + i)),
        whole((total, cols)),
        pl.BlockSpec((cols, total), lambda i: (0, 0)),
        whole((total, cols)),
        pl.BlockSpec((cols, BLK), lambda i: (0, i)),
        pl.BlockSpec((cols, BLK), lambda i: (0, i)),
        pl.BlockSpec((8, BLK), lambda i: (0, i)),
        whole((1, total)),
        whole((total, 128)),
    ]


def spread_scratch(cols):
    return [pltpu.VMEM((cols // HEAD, cols, BLK), BF16)] * 2


def first_back(sc, qkvt, kn, vn, dout, out, lse, gq, gkv):
    total, cols = kn.shape
    blocks = total // BLK // 2
    return pl.pallas_call(
        functools.partial(first_back_kernel, total // 4 // BLK),
        grid=(blocks,),
        in_specs=back_specs(0, total, cols),
        out_specs=[
            pl.BlockSpec((cols, BLK), lambda i: (0, i)),
            whole((cols, total)),
            whole((cols, total)),
        ],
        out_shape=[
            shape((cols, blocks * BLK), BF16),
            shape((cols, total), F32),
            shape((cols, total), F32),
        ],
        scratch_shapes=[pltpu.VMEM((cols, total), F32)] * 2 + spread_scratch(cols),
        name="attention_back",
        cost_estimate=cost(20),
    )(sc, qkvt, kn, qkvt, vn, dout, out, lse, gq, gkv)


def second_back(pieces, sc, qkvt, kn, vn, dout, out, lse, gq, gkv, dk, dv, dqa, go, gox, gain, gain_m, n1, wt):
    total, cols = kn.shape
    blocks = total // BLK // 2
    both = blocks * BLK
    width = n1.shape[1]
    piece = (width // pieces + EXTRA, 4 * cols)
    return pl.pallas_call(
        functools.partial(second_back_kernel, total // 4 // BLK, pieces),
        grid=(blocks,),
        in_specs=back_specs(1, total, cols)
        + [whole((cols, total))] * 2
        + [whole((cols, both))]
        + [whole((cols, width))] * 2
        + [whole((1, width)), whole(gain_m.shape)]
        + [HBM] * 2,
        out_specs=[whole((both // 2, width))] * 2
        + [whole((cols, both))] * 2
        + [whole(piece)] * pieces,
        out_shape=[shape((both // 2, width), BF16)] * 2
        + [shape((cols, both), BF16)] * 2
        + [shape(piece, BF16)] * pieces,
        scratch_shapes=[pltpu.VMEM((cols, total), F32)] * 2
        + [pltpu.VMEM((cols, both), BF16)]
        + spread_scratch(cols)
        + [
            pltpu.VMEM(n1.shape, BF16),
            pltpu.VMEM(wt.shape, BF16),
            pltpu.VMEM((width, 4 * cols), BF16),
            pltpu.SemaphoreType.DMA((2,)),
        ],
        compiler_params=room(48),
        name="attention_back_end",
        cost_estimate=cost(0.01),
    )(sc, qkvt, kn, qkvt, vn, dout, out, lse, gq, gkv, dk, dv, dqa, go, gox, gain, gain_m, n1, wt)


def rows_kernel(fn, counts, n_const, n_out, chunks, split, *refs):
    ins = []
    for count in counts:
        ins.append(refs[:count])
        refs = refs[count:]
    n_in = len(ins)
    consts, refs = refs[:n_const], refs[n_const:]
    outs, refs = refs[:n_out], refs[n_out:]
    pieces, refs = refs[:split], refs[split:]
    sums, refs = refs[: len(refs) - n_in - n_out - 2], refs[len(refs) - n_in - n_out - 2 :]
    held, made, (in_sem, out_sem) = refs[:n_in], refs[n_in:-2], refs[-2:]
    size = held[0].shape[0] // chunks

    def part(c):
        return pl.ds(pl.multiple_of(c * size, size), size)

    def arrival(i, c):
        src = ins[i][c] if len(ins[i]) > 1 else ins[i][0].at[part(c)]
        return pltpu.make_async_copy(src, held[i].at[part(c)], in_sem.at[i, c])

    def departure(i, c):
        return pltpu.make_async_copy(made[i].at[part(c)], outs[i].at[part(c)], out_sem.at[i, c])

    def apart(c):
        return pltpu.make_async_copy(made[-1].at[part(c)], pieces[c], out_sem.at[n_out, c])

    for c in range(chunks):
        for i in range(n_in):
            arrival(i, c).start()
    def each(c, of_chunk, many):
        if not many:
            of_chunk(c)
            return
        for known in range(chunks):

            @pl.when(c == known)
            def _(known=known):
                of_chunk(known)

    def body(c, totals):
        for i in range(n_in):
            each(c, lambda c, i=i: arrival(i, c).wait(), len(ins[i]) > 1)
        where = pl.ds(pl.multiple_of(c * size, size), size)
        results, adds = fn([r[where, :] for r in held], [r[...] for r in consts])
        for i, value in enumerate(results):
            made[i][where, :] = value
        if split:
            each(c, lambda c: apart(c).start(), True)
        for i in range(n_out):
            departure(i, c).start()
        return tuple(t + a for t, a in zip(totals, adds))

    totals = lax.fori_loop(0, chunks, body, tuple(jnp.zeros(r.shape, F32) for r in sums))
    for ref, t in zip(sums, totals):
        ref[...] = t
    for c in range(chunks):
        if split:
            apart(c).wait()
        for i in range(n_out):
            departure(i, c).wait()


def by_rows(name, fn, ins, arrived, consts, kinds, sums=(), chunks=2, split=0):
    near = len(ins)
    ins = (*ins, *arrived)
    dims = ins[0].shape
    flat = [v if isinstance(v, tuple) else (v,) for v in ins]
    return pl.pallas_call(
        functools.partial(
            rows_kernel, fn, [len(v) for v in flat], len(consts), len(kinds), chunks, split
        ),
        in_specs=[HBM] * near
        + [ANY] * sum(len(v) for v in flat[near:])
        + [VMEM] * len(consts),
        out_specs=[HBM] * (len(kinds) + split) + [VMEM] * len(sums),
        out_shape=[shape(dims, k) for k in kinds]
        + [shape((dims[0] // chunks, dims[1]), kinds[-1])] * split
        + [shape(d, F32) for d in sums],
        scratch_shapes=[pltpu.VMEM(dims, v[0].dtype) for v in flat]
        + [pltpu.VMEM(dims, k) for k in kinds]
        + [
            pltpu.SemaphoreType.DMA((len(ins), chunks)),
            pltpu.SemaphoreType.DMA((len(kinds) + 1, chunks)),
        ],
        compiler_params=room(24),
        name=name,
        cost_estimate=cost(0.01),
    )(*[part for v in flat for part in v], *consts)


def out_kernel(om, ox, wm, wx, own, other, omv, oxv, wmv, wxv, ownv, otherv, sems):
    rows = own.shape[0]
    copies = [
        pltpu.make_async_copy(src, dst, sems.at[i])
        for i, (src, dst) in enumerate(((om, omv), (ox, oxv), (wm, wmv), (wx, wxv)))
    ]
    for copy in copies:
        copy.start()
    for copy in copies:
        copy.wait()
    leave = [
        pltpu.make_async_copy(made, out, sems.at[4 + i])
        for i, (made, out) in enumerate(((otherv, other), (ownv, own)))
    ]

    def body(i, carry):
        where = pl.ds(pl.multiple_of((1 - i) * rows, rows), rows)
        part = (nn(omv[:, where].T, wmv[...]) + nn(oxv[:, where].T, wxv[...])).astype(BF16)
        for c, (made, copy) in enumerate(zip((otherv, ownv), leave)):

            @pl.when(i == c)
            def _(made=made, copy=copy):
                made[...] = part
                copy.start()

        return carry

    lax.fori_loop(0, 2, body, 0)
    for copy in leave:
        copy.wait()


def out_projection(om, ox, wm, wx):
    cols, both = om.shape
    width = wm.shape[1]
    made = (both // 2, width)
    return pl.pallas_call(
        out_kernel,
        in_specs=[HBM, ANY, HBM, ANY],
        out_specs=[HBM] * 2,
        out_shape=[shape(made, BF16)] * 2,
        scratch_shapes=[pltpu.VMEM(v.shape, BF16) for v in (om, ox, wm, wx)]
        + [pltpu.VMEM(made, BF16)] * 2
        + [pltpu.SemaphoreType.DMA((6,))],
        compiler_params=room(24),
        name="out_projection",
        cost_estimate=cost(0.01),
    )(om, ox, wm, wx)


def middle_rows(held, consts):
    tokens, own, got = (v.astype(F32) for v in held)
    h1 = tokens + (own + got)
    scale = lax.rsqrt(jnp.mean(h1 * h1, axis=-1, keepdims=True) + eps_norm)
    return (h1, (h1 * scale * consts[0]).astype(BF16)), ()


def middle(tokens, own, got, gain):
    return by_rows("middle", middle_rows, (tokens, own), (got,), (gain,), (F32, BF16), split=2)


def mlp_kernel(at, aliased, na, nb, ya, yb, w, *refs):
    ma, mb, da, db, hid_o, dgu_o, nv, yv, wv, mv, dv, hv, gv, in_sem, w_sem, out_sem = refs[aliased:]
    rows, units = na.shape[0], hv.shape[1]
    arrivals, departures = [], []
    for c, (n, y, m, d) in enumerate(((na, ya, ma, da), (nb, yb, mb, db))):
        part, place = pl.ds(c * rows, rows), pl.ds(at, rows)
        arrivals += [
            pltpu.make_async_copy(n, nv.at[part], in_sem.at[0, c]),
            pltpu.make_async_copy(y.at[place], yv.at[part], in_sem.at[1, c]),
        ]
        departures.append(
            [
                pltpu.make_async_copy(dv.at[part], d, out_sem.at[0, c]),
                pltpu.make_async_copy(mv.at[part], m.at[place], out_sem.at[1, c]),
                pltpu.make_async_copy(hv.at[part], hid_o.at[part], out_sem.at[2, c]),
                pltpu.make_async_copy(gv.at[part], dgu_o.at[part], out_sem.at[3, c]),
            ]
        )
    weights = [
        pltpu.make_async_copy(
            w.at[:, pl.ds(j * units, units)], wv.at[:, pl.ds(j * units, units)], w_sem.at[j]
        )
        for j in range(3)
    ]
    for copy in weights + arrivals:
        copy.start()
    for copy in weights + arrivals:
        copy.wait()
    wg, wu, wd = (wv.at[:, pl.ds(j * units, units)] for j in range(3))
    tile = rows if rows < 512 else 512

    def body(i, carry):
        part = pl.ds(pl.multiple_of(i * tile, tile), tile)
        n2 = nv[part, :]
        gate, up = nn(n2, wg[...]), nn(n2, wu[...])
        dhid = nn(yv[part, :], wd[...])
        square = gate * gate
        share = 0.5 * jnp.tanh(gate * (ROOT + ROOT * 0.044715 * square)) + 0.5
        value = gate * share
        slope = share + value * (1.0 - share) * (2.0 * ROOT + 6.0 * ROOT * 0.044715 * square)
        dgate = (dhid * up * slope).astype(BF16)
        dup = (dhid * value).astype(BF16)
        hidden = (value * up).astype(BF16)
        dv[part, :] = (nt(dgate, wg[...]) + nt(dup, wu[...])).astype(BF16)
        hv[part, :] = hidden
        gv[part, 0:units] = dgate
        gv[part, units : 2 * units] = dup
        mv[part, :] = nt(hidden, wd[...]).astype(BF16)
        for c, copies in enumerate(departures):

            @pl.when(i == c * rows // tile)
            def _(copies=copies):
                for copy in copies:
                    copy.start()

        return carry

    lax.fori_loop(0, 2 * rows // tile, body, 0)
    for copies in departures:
        for copy in copies:
            copy.wait()


def mlp_both(na, nb, ya, yb, weights, at=0, into=(), mib=32):
    rows, width = na.shape
    units = weights.shape[1] // 3
    both = 2 * rows
    return pl.pallas_call(
        functools.partial(mlp_kernel, at, len(into)),
        in_specs=[ANY] * 4 + [HBM] * (1 + len(into)),
        out_specs=[HBM] * 6,
        out_shape=[shape(ya.shape, BF16)] * 2
        + [shape((rows, width), BF16)] * 2
        + [shape((both, units), BF16), shape((both, 2 * units), BF16)],
        scratch_shapes=[
            pltpu.VMEM((both, width), BF16),
            pltpu.VMEM((both, width), BF16),
            pltpu.VMEM(weights.shape, BF16),
            pltpu.VMEM((both, width), BF16),
            pltpu.VMEM((both, width), BF16),
            pltpu.VMEM((both, units), BF16),
            pltpu.VMEM((both, 2 * units), BF16),
            pltpu.SemaphoreType.DMA((2, 2)),
            pltpu.SemaphoreType.DMA((3,)),
            pltpu.SemaphoreType.DMA((4, 2)),
        ],
        input_output_aliases={5 + i: i for i in range(len(into))},
        compiler_params=room(mib),
        name="mlp",
        cost_estimate=cost(8),
    )(na, nb, ya, yb, weights, *into)


def mlp_weights_kernel(order, n_in, *refs):
    ins, (out, *held, total, made, sems, sem) = refs[:n_in], refs[n_in:]
    copies = []
    for group, moves in enumerate(order):
        for which, start, rows, at in moves:
            copy = pltpu.make_async_copy(
                ins[which].at[pl.ds(start, rows)], held[group].at[pl.ds(at, rows)], sems.at[len(copies)]
            )
            copies.append((at + rows, copy))
    size = held[0].shape[0] // 2
    copies.sort(key=lambda v: v[0])
    for _, copy in copies:
        copy.start()
    wide = held[2].shape[1]

    def body(i, carry):
        for c in range(2):

            @pl.when(i == c)
            def _(c=c):
                for end, copy in copies:
                    if c * size < end <= (c + 1) * size:
                        copy.wait()

        rows = pl.ds(pl.multiple_of(i * size, size), size)
        n2, dy, dgu, hidden = (r[rows, :] for r in held)
        for at, left, right in ((0, n2, dgu), (wide, dy, hidden)):
            cols = pl.ds(at, right.shape[1])
            new = nn(left.T, right) + total[:, cols]
            total[:, cols] = new
            made[:, cols] = new.astype(BF16)
        return carry

    total[...] = jnp.zeros(total.shape, F32)
    lax.fori_loop(0, 2, body, 0)
    leave = pltpu.make_async_copy(made, out, sem)
    leave.start()
    leave.wait()


def mlp_weights(n2, dy, dgu, hidden):
    ins = (*n2, *dy, *dgu, *hidden)
    rows = n2[0].shape[0]
    half = rows // 2
    first = [(0, 0, rows, 0), (1, 0, rows, rows)]
    order = [
        first + [(2, 0, half, 2 * rows), (4, 0, half, 2 * rows + half), (3, 0, half, 3 * rows), (5, 0, half, 3 * rows + half)],
        [(6 + j, 0, rows, j * rows) for j in range(4)],
    ]
    for base in (10, 13):
        order.append(
            [
                (base, 0, 2 * rows, 0),
                (base + 1, 0, half, 2 * rows),
                (base + 2, 0, half, 2 * rows + half),
                (base + 1, half, half, 3 * rows),
                (base + 2, half, half, 3 * rows + half),
            ]
        )
    width = n2[0].shape[1]
    dims = (width, dgu[0].shape[1] + hidden[0].shape[1])
    return pl.pallas_call(
        functools.partial(mlp_weights_kernel, order, len(ins)),
        in_specs=[HBM] * len(ins),
        out_specs=HBM,
        out_shape=shape(dims, BF16),
        scratch_shapes=[
            pltpu.VMEM((4 * rows, v.shape[1]), BF16) for v in (n2[0], dy[0], dgu[0], hidden[0])
        ]
        + [
            pltpu.VMEM(dims, F32),
            pltpu.VMEM(dims, BF16),
            pltpu.SemaphoreType.DMA((sum(len(v) for v in order),)),
            pltpu.SemaphoreType.DMA,
        ],
        compiler_params=room(48),
        name="mlp_weights",
        cost_estimate=cost(10),
    )(*ins)


def middle_back_rows(held, consts):
    dy, h1, *shares = (v.astype(F32) for v in held)
    dn2 = sum(shares[1:], shares[0])
    scale = lax.rsqrt(jnp.mean(h1 * h1, axis=-1, keepdims=True) + eps_norm)
    hat = dn2 * consts[0]
    dh1 = (
        dy
        + scale * hat
        - h1 * (scale * scale * scale) * jnp.mean(hat * h1, axis=-1, keepdims=True)
    )
    return (dh1, dh1.astype(BF16)), (folded(dn2 * h1 * scale),)


def middle_back(dy, h1, a, b, c, gain):
    return by_rows(
        "middle_back",
        middle_back_rows,
        (dy, h1, a),
        (b, c),
        (gain,),
        (F32, BF16),
        sums=((FOLD, dy.shape[1]),),
    )


def out_back_kernel(own, other, wm, wx, om, ox, dm_o, dx_o, gm_o, gx_o, *scratch):
    refs = (own, other, wm, wx, om, ox)
    held, made, sems = scratch[:6], scratch[6:10], scratch[10]
    copies = [pltpu.make_async_copy(src, dst, sems.at[i]) for i, (src, dst) in enumerate(zip(refs, held))]
    for copy in copies:
        copy.start()
    ownv, otherv, wmv, wxv, omv, oxv = held
    dm, dx, gm, gx = made
    rows = own.shape[0]
    for copy in copies:
        copy.wait()
    leave = [
        pltpu.make_async_copy(src, dst, sems.at[6 + i])
        for i, (src, dst) in enumerate(((dx, dx_o), (dm, dm_o), (gx, gx_o), (gm, gm_o)))
    ]
    for i, (w, out) in enumerate(((wxv, dx), (wmv, dm))):
        for at, ref in ((0, ownv), (rows, otherv)):
            out[:, at : at + rows] = nt(w[...], ref[...]).astype(BF16)
        leave[i].start()
    gx[...] = (nn(oxv[:, :rows], ownv[...]) + nn(oxv[:, rows:], otherv[...])).astype(BF16)
    leave[2].start()
    gm[...] = nn(omv[:, :rows], ownv[...]) + nn(omv[:, rows:], otherv[...])
    leave[3].start()
    for copy in leave:
        copy.wait()


def out_back(own, other, wm, wx, om, ox):
    cols, both = om.shape
    width = own.shape[1]
    ins = (own, other, wm, wx, om, ox)
    outs = [
        ((cols, both), BF16),
        ((cols, both), BF16),
        ((cols, width), F32),
        ((cols, width), BF16),
    ]
    return pl.pallas_call(
        out_back_kernel,
        in_specs=[HBM, ANY, HBM, ANY, HBM, ANY],
        out_specs=[HBM] * 4,
        out_shape=[shape(*v) for v in outs],
        scratch_shapes=[pltpu.VMEM(v.shape, BF16) for v in ins]
        + [pltpu.VMEM(*v) for v in outs]
        + [pltpu.SemaphoreType.DMA((10,))],
        compiler_params=room(24),
        name="out_back",
        cost_estimate=cost(0.01),
    )(*ins)


def rows_back_kernel(dk, dq, dv, wt, a_o, b_o):
    rows = a_o.shape[0]

    def body(i, carry):
        where = pl.ds(pl.multiple_of(i * rows, rows), rows)
        grads = jnp.concatenate([dk[:, where], dq[:, where], dv[:, where]], axis=0)
        part = nn(grads.T, wt[...]).astype(BF16)
        for c, ref in enumerate((a_o, b_o)):

            @pl.when(i == c)
            def _(ref=ref):
                ref[...] = part

        return carry

    lax.fori_loop(0, 2, body, 0)


def rows_back(dk, dq, dv, wt):
    cols, both = dq.shape
    width = wt.shape[1]
    return pl.pallas_call(
        rows_back_kernel,
        out_shape=[shape((both // 2, width), BF16)] * 2,
        compiler_params=room(24),
        name="rows_back",
        cost_estimate=cost(0.01),
    )(dk, dq, dv, wt)


def last_rows(held, consts):
    x, dh1, *shares = (v.astype(F32) for v in held)
    dn1 = sum(shares[1:], shares[0])
    scale = lax.rsqrt(jnp.mean(x * x, axis=-1, keepdims=True) + eps_norm)
    hat = dn1 * consts[0]
    out = (
        dh1
        + scale * hat
        - x * (scale * scale * scale) * jnp.mean(hat * x, axis=-1, keepdims=True)
    )
    return (out.astype(BF16),), ()


def last(tokens, dh1, a, b, c, gain):
    return by_rows("last", last_rows, (tokens, dh1, a), (b, c), (gain,), (BF16,))[0]


def grads_sum_kernel(count, *refs):
    ins, outs, gains_o = refs[:count], refs[count:-1], refs[-1]
    rows, cols = outs[0].shape
    total = ins[0][0:rows, :].astype(F32)
    for ref in ins[1:]:
        total = total + ref[0:rows, :].astype(F32)
    for j, ref in enumerate(outs):
        ref[...] = total[:, j * cols : (j + 1) * cols]
    tail = [ref[rows : rows + EXTRA, :].astype(F32) for ref in ins]
    gains = tail[0]
    for part in tail[1:]:
        gains = gains + part
    gains = gains[0:4, :] + gains[4:8, :]
    gains_o[...] = jnp.concatenate(
        [gains[0:1, :] + gains[1:2, :], gains[2:3, :] + gains[3:4, :]], axis=0
    )


def grads_sum(parts):
    rows, width = parts[0].shape
    rows -= EXTRA
    return pl.pallas_call(
        functools.partial(grads_sum_kernel, len(parts)),
        out_shape=[shape((rows, width // 4), F32)] * 4 + [shape((2, width), F32)],
        compiler_params=room(16),
        name="grads_sum",
        cost_estimate=cost(0.01),
    )(*parts)


def local(
    dp,
    mp,
    tokens,
    w_query,
    w_key,
    w_value,
    w_out,
    w_gate,
    w_up,
    w_down,
    norm_attn,
    norm_mlp,
    valid_counts,
    group_ids,
    cotangent,
):
    me, row = lax.axis_index("mp"), lax.axis_index("dp")
    cols = w_query.shape[1]
    length = group_ids.shape[1]

    def core(v):
        return lax.ppermute(v, "mp", [(i, i ^ 1) for i in range(mp)])

    def across(v):
        return lax.ppermute(v, "mp", [(i, i ^ 2) for i in range(mp)])

    def core_across(v):
        return lax.ppermute(v, "mp", [(i, i ^ 3) for i in range(mp)])

    def far(v, k):
        return lax.ppermute(v, "dp", [(i, i ^ k) for i in range(dp)])

    def after(v, *others):
        return lax.optimization_barrier((v, *others))[0]

    def summed(a, b):
        return (a.astype(F32) + b.astype(F32)).astype(BF16)

    direct = dp <= DIRECT
    gain_a, gain_m = norm_attn[None], norm_mlp[None]

    gq = group_ids
    flat = group_ids[0]
    valid = valid_counts[0]
    tiles = flat.reshape(length // BLK, BLK)
    low = jnp.sum(flat[None, :] < tiles[:, :1], axis=1) // BLK
    high = jnp.minimum(jnp.sum(flat[None, :] <= tiles[:, -1:], axis=1), valid)
    high = (high + BLK - 1) // BLK
    head = jnp.stack([me, row, valid, valid, valid, valid, valid, valid])
    sc = jnp.concatenate([head, low, high]).astype(jnp.int32)
    keyed = jnp.where(jnp.arange(length, dtype=jnp.int32) < valid, flat, -1)
    gkv = jnp.broadcast_to(keyed[:, None], (length, 128))

    tok2 = across(tokens)
    w_attn = jnp.concatenate([w_key, w_query, w_value, w_out], axis=1)
    w_mlp = jnp.concatenate([w_gate, w_up, w_down], axis=1)
    if direct:
        near = [w_attn] + [far(w_attn, k) for k in range(2, dp, 2)]
        middle_way = len(near) // 2
        near[middle_way] = after(near[middle_way], sc, gkv, w_mlp)
        w_pieces = [p for v in near for p in (v, far(v, 1))]
        tok1 = core(after(tokens, w_pieces[1]))
    else:
        w_pieces = [lax.all_gather(w_attn, "dp", axis=0, tiled=True)]
        tok1 = core(tokens)
    w_mlp = lax.all_gather(w_mlp, "dp", axis=0, tiled=True)
    tok3 = core(after(tok2, *w_pieces[1::2]))

    n1, qkvt, kn, vn, wt, wo = qkv(sc, (tokens, tok1, tok2, tok3), gain_a, w_pieces, cols)
    wo_x = across(wo)
    dy0 = cotangent
    dy2 = across(after(cotangent, tok2))
    dy1 = core(after(cotangent, tok3))

    o_far, lse_far = attention(1, sc, qkvt, kn, gq, gkv)
    o_x = across(after(o_far, dy2, wo_x))
    dy3 = core(after(dy2, o_far))
    o_own, lse_own = attention(0, after(sc, o_far), qkvt, kn, gq, gkv)
    p_own, p_other = out_projection(o_own, o_x, wo, wo_x)
    h1, n2, n2_a, n2_b = middle(tokens, p_own, core(p_other), gain_m)

    half = n2.shape[0] // 2
    n2_1 = core(n2)
    far_a = across(n2_a)
    far_b = across(n2_b)
    m0, m1, d0, d1, hid_o, dgu_o = mlp_both(n2, n2_1, dy0, dy1, w_mlp, mib=60)
    side_a = core(after(far_a, d0))
    m2, m3, d2a, d3a, hid_a, dgu_a = mlp_both(far_a, side_a, dy2, dy3, w_mlp)
    dsum_a = summed(d2a, core(d3a))
    dx_a = across(dsum_a)
    side_b = core(after(far_b, d2a))
    far_b = after(far_b, dsum_a)
    m2, m3, d2b, d3b, hid_b, dgu_b = mlp_both(far_b, side_b, dy2, dy3, w_mlp, half, (m2, m3))

    d_sum = summed(d2b, core(after(d3b, dx_a)))
    dx_b = across(d_sum)
    mlp_all = mlp_weights(
        (n2, n2_1, far_a, side_a, far_b, side_b),
        (dy0, dy1, dy2, dy3),
        (dgu_o, dgu_a, dgu_b),
        (after(hid_o, d_sum), hid_a, hid_b),
    )
    mlp_grads = lax.psum_scatter(mlp_all, "dp", scatter_dimension=0, tiled=True)
    m_other, m_core = core(m3), core(after(m1, d_sum))
    dh1, da, gain_m_part = middle_back(
        dy0,
        h1,
        d0,
        core(after(d1, d_sum)),
        (dx_a, after(dx_b, mlp_all, m_other, m_core)),
        gain_m,
    )

    do_own, do_send, go, go_send = out_back(da, core(da), wo, wo_x, o_own, o_x)
    do_far = across(do_send)
    go_x = across(go_send)
    m_x = across(after(summed(after(m2, da), m_other), do_send))
    dq_own, dk, dv = first_back(sc, qkvt, kn, vn, do_own, o_own, lse_own, gq, gkv)
    r2, r3, dk_own, dv_own, *grads = second_back(
        dp if direct else 1,
        sc, qkvt, kn, vn, do_far, o_far, lse_far, gq, gkv,
        dk, dv, dq_own, go, go_x, gain_a, gain_m_part, n1, wt,
    )
    r_sum = summed(r2, core(after(r3, m_x)))
    r_x = across(r_sum)
    depth = w_query.shape[0]
    parts = []
    if direct:
        for k in range(dp - 2, -1, -2):
            sent = grads[k + 1]
            if k < dp // 2 and parts:
                sent = after(sent, parts[k // 2 - dp // 4])
            near, other = grads[k], after(far(sent, 1), r_sum)
            both = summed(near[:depth], other[:depth])
            part = jnp.concatenate([both, near[depth : depth + 4], other[depth : depth + 4]], axis=0)
            parts.insert(0, part)
        parts = [part if k == 0 else far(part, 2 * k) for k, part in enumerate(parts)]
    r0, r1 = rows_back(after(dk_own, r_sum), dq_own, dv_own, wt)
    grad_tokens = last(tokens, dh1, r0, core(r1), r_x, gain_a)
    output = (
        h1 + (m0.astype(F32) + m_core.astype(F32) + after(m_x, r_sum).astype(F32))
    ).astype(BF16)
    units = w_gate.shape[1]
    grad_gate, grad_up, grad_down = (
        mlp_grads[:, j * units : (j + 1) * units].astype(F32) for j in range(3)
    )
    if direct:
        parts[0] = after(parts[0], grad_tokens, output, grad_gate)
        grad_k, grad_q, grad_v, grad_o, gains = grads_sum(parts)
        gains = gains + core(gains) + across(gains) + core_across(gains)
    else:
        width = tokens.shape[1]
        attn_grads = lax.psum_scatter(
            grads[0][:width], "dp", scatter_dimension=0, tiled=True
        ).astype(F32)
        grad_k, grad_q, grad_v, grad_o = jnp.split(attn_grads, 4, axis=1)
        extra = grads[0][width : width + 4].astype(F32)
        gains = lax.psum(extra[0::2] + extra[1::2], ("dp", "mp"))

    return (
        output,
        grad_tokens,
        grad_q,
        grad_k,
        grad_v,
        grad_o,
        grad_gate,
        grad_up,
        grad_down,
        gains[0],
        gains[1],
    )


def solution(mesh):
    rows, weight = P(("dp", "mp"), None), P("dp", "mp")
    return jax.shard_map(
        functools.partial(local, mesh.shape["dp"], mesh.shape["mp"]),
        mesh=mesh,
        in_specs=(rows,) + (weight,) * 7 + (P(), P(), P("dp"), P("dp", None), rows),
        out_specs=(rows, rows) + (weight,) * 7 + (P(), P()),
        check_vma=False,
    )
```

```python
import functools

import jax
import jax.numpy as jnp
from jax import lax
from jax.experimental import pallas as pl
from jax.experimental.pallas import tpu as pltpu
from jax.sharding import PartitionSpec as P

HEAD = 64
BLK = 256
DIRECT = 8
FOLD = 32
EXTRA = 8
ROOT = 0.7978845608028654
eps_norm = 1e-06
neg_large = -1e30
F32 = jnp.float32
BF16 = jnp.bfloat16


def nn(a, b):
    return lax.dot_general(a, b, (((1,), (0,)), ((), ())), preferred_element_type=F32)


def nt(a, b):
    return lax.dot_general(a, b, (((1,), (1,)), ((), ())), preferred_element_type=F32)


def tn(a, b):
    return lax.dot_general(a, b, (((0,), (0,)), ((), ())), preferred_element_type=F32)


def shape(dims, kind):
    return jax.ShapeDtypeStruct(dims, kind)


def whole(dims):
    return pl.BlockSpec(dims, lambda *_: (0,) * len(dims))


SMEM = pl.BlockSpec(memory_space=pltpu.SMEM)
VMEM = pl.BlockSpec(memory_space=pltpu.VMEM)
HBM = pl.BlockSpec(memory_space=pltpu.HBM)
ANY = pl.BlockSpec(memory_space=pl.ANY)


def room(mib):
    return pltpu.CompilerParams(vmem_limit_bytes=mib << 20)


def qkv_kernel(pieces, sc, t0, t1, t2, t3, gain, *rest):
    w_refs, (n1_o, qkvt_o, kn_o, vn_o, wt_o, wo_o, xs, ws) = rest[:pieces], rest[pieces:]
    step = pl.program_id(0)
    cols = kn_o.shape[1]

    @pl.when(step == 0)
    def _():
        if pieces == 1:
            ws[...] = w_refs[0][...]
        else:
            depth = w_refs[0].shape[0]
            for j in range(pieces):
                at = pl.multiple_of((sc[1] ^ j) * depth, 16)
                ws[pl.ds(at, depth), :] = w_refs[j][...]
        turned = ws[...].T
        wt_o[...] = turned[: 3 * cols, :]
        wo_o[...] = turned[3 * cols :, :]

    for j, ref in enumerate((t0, t1, t2, t3)):

        @pl.when(step == j)
        def _(ref=ref):
            xs[...] = ref[...]

    x = xs[...].astype(F32)
    scale = lax.rsqrt(jnp.mean(x * x, axis=-1, keepdims=True) + eps_norm)
    n1 = (x * scale * gain[...]).astype(BF16)
    n1_o[...] = n1
    qkvt_o[...] = nt(wt_o[...], n1).astype(BF16)
    kn_o[...] = nn(n1, ws[:, 0:cols]).astype(BF16)
    vn_o[...] = nn(n1, ws[:, 2 * cols : 3 * cols]).astype(BF16)


def qkv(sc, shards, gain, pieces, cols):
    rows, width = shards[0].shape
    total = rows * len(shards)
    return pl.pallas_call(
        functools.partial(qkv_kernel, len(pieces)),
        grid=(len(shards),),
        in_specs=[SMEM]
        + [whole((rows, width))] * 4
        + [whole((1, width))]
        + [whole(p.shape) for p in pieces],
        out_specs=[
            pl.BlockSpec((rows, width), lambda i: (i, 0)),
            pl.BlockSpec((3 * cols, rows), lambda i: (0, i)),
            pl.BlockSpec((rows, cols), lambda i: (i, 0)),
            pl.BlockSpec((rows, cols), lambda i: (i, 0)),
            whole((3 * cols, width)),
            whole((cols, width)),
        ],
        out_shape=[
            shape((total, width), BF16),
            shape((3 * cols, total), BF16),
            shape((total, cols), BF16),
            shape((total, cols), BF16),
            shape((3 * cols, width), BF16),
            shape((cols, width), BF16),
        ],
        scratch_shapes=[pltpu.VMEM((rows, width), BF16), pltpu.VMEM((width, 4 * cols), BF16)],
        name="qkv",
        cost_estimate=cost(0.01),
    )(sc, *shards, gain, *pieces)


def spread(rows, z_ref):
    heads = rows.shape[0] // HEAD
    z_ref[...] = jnp.zeros(z_ref.shape, z_ref.dtype)
    for h in range(heads):
        z_ref[h, h * HEAD : (h + 1) * HEAD, :] = rows[h * HEAD : (h + 1) * HEAD, :]


def cost(us):
    return pl.CostEstimate(flops=int(us * 1e9), transcendentals=0, bytes_accessed=1024)


def span(sc, half, per, blocks):
    me = sc[0]
    stored = half * blocks + pl.program_id(0)
    shard = (stored // per) ^ me
    place = shard * per + lax.rem(stored, per)
    low, high = sc[8 + place] // per, (sc[16 + place] + per - 1) // per
    has_own = jnp.logical_and(low <= shard, shard < high)
    count = jnp.maximum(high - low, 0) - has_own.astype(jnp.int32)

    def at(t):
        other = low + t - 1
        other = jnp.where(t == 0, shard, other + (other >= shard).astype(jnp.int32))
        return other, other ^ me

    return place, count + 1, at


def allowed(gkv, queries, place, shard, size, own=True):
    keys = gkv[pl.ds(pl.multiple_of(shard * size, size), size), :]
    mask = jnp.concatenate([keys] * (BLK // 128), axis=1) == queries
    if not own:
        return mask
    key_at = lax.broadcasted_iota(jnp.int32, mask.shape, 0)
    query_at = lax.broadcasted_iota(jnp.int32, mask.shape, 1) + (place * BLK - shard * size)
    return mask | (key_at == query_at)


def forward_kernel(half, per, sc, qt, kn, vt, gq, gkv, ot, lse, zq):
    heads = qt.shape[0] // HEAD
    size = per * BLK
    place, count, at = span(sc, half, per, pl.num_programs(0))
    spread(qt, zq)
    queries = gq[:, pl.ds(pl.multiple_of(place * BLK, BLK), BLK)]

    def scores(t, own):
        shard, stored = at(t)
        mask = allowed(gkv, queries, place, shard, size, own)
        where = pl.ds(pl.multiple_of(stored * size, size), size)
        keys = kn[where, :]
        return where, [jnp.where(mask, nn(keys, zq[h]), neg_large) for h in range(heads)]

    def mixed(h, where, p):
        return nn(vt[h * HEAD : (h + 1) * HEAD, where], p.astype(BF16))

    carry = []
    where, first = scores(0, True)
    for h, s in enumerate(first):
        top = jnp.max(s, axis=0, keepdims=True)
        p = jnp.exp(s - top)
        carry.append((top, jnp.sum(p, axis=0, keepdims=True), mixed(h, where, p)))

    def body(t, carry):
        where, more = scores(t, False)
        out = []
        for h, s in enumerate(more):
            top, total, acc = carry[h]
            higher = jnp.maximum(top, jnp.max(s, axis=0, keepdims=True))
            p = jnp.exp(s - higher)
            fade = jnp.exp(top - higher)
            out.append(
                (
                    higher,
                    fade * total + jnp.sum(p, axis=0, keepdims=True),
                    fade * acc + mixed(h, where, p),
                )
            )
        return tuple(out)

    carry = lax.fori_loop(1, count, body, tuple(carry))
    for h, (top, total, acc) in enumerate(carry):
        ot[h * HEAD : (h + 1) * HEAD, :] = (acc / total).astype(BF16)
        lse[h : h + 1, :] = top + jnp.log(total)


def attention(half, sc, qkvt, kn, gq, gkv):
    cols3, total = qkvt.shape
    cols = cols3 // 3
    blocks = total // BLK // 2
    per = total // 4 // BLK
    return pl.pallas_call(
        functools.partial(forward_kernel, half, per),
        grid=(blocks,),
        in_specs=[
            SMEM,
            pl.BlockSpec((cols, BLK), lambda i: (1, half * blocks + i)),
            whole((total, cols)),
            pl.BlockSpec((cols, total), lambda i: (2, 0)),
            whole((1, total)),
            whole((total, 128)),
        ],
        out_specs=[
            pl.BlockSpec((cols, BLK), lambda i: (0, i)),
            pl.BlockSpec((8, BLK), lambda i: (0, i)),
        ],
        out_shape=[shape((cols, blocks * BLK), BF16), shape((8, blocks * BLK), F32)],
        scratch_shapes=[pltpu.VMEM((cols // HEAD, cols, BLK), BF16)],
        compiler_params=room(32),
        name="attention",
        cost_estimate=cost(12),
    )(sc, qkvt, kn, qkvt, gq, gkv)


def backward_block(
    half, per, sc, qt, kn, kt, vn, dot_, ot, lse, gq, gkv, dk, dv, zq, zd
):
    heads = qt.shape[0] // HEAD
    size = per * BLK
    place, count, at = span(sc, half, per, pl.num_programs(0))
    queries = gq[:, pl.ds(pl.multiple_of(place * BLK, BLK), BLK)]
    spread(qt, zq)
    spread(dot_, zd)
    deltas = []
    for h in range(heads):
        part = slice(h * HEAD, (h + 1) * HEAD)
        deltas.append(
            jnp.sum(dot_[part, :].astype(F32) * ot[part, :].astype(F32), axis=0, keepdims=True)
        )

    def body(t, carry):
        shard, stored = at(t)
        mask = allowed(gkv, queries, place, shard, size)
        at_keys = pl.ds(pl.multiple_of(stored * size, size), size)
        keys, values = kn[at_keys, :], vn[at_keys, :]
        out = []
        for h in range(heads):
            part = slice(h * HEAD, (h + 1) * HEAD)
            s = jnp.where(mask, nn(keys, zq[h]), neg_large)
            p = jnp.exp(s - lse[h : h + 1, :])
            ds = (p * (nn(values, zd[h]) - deltas[h])).astype(BF16)
            dv[part, at_keys] += nt(dot_[part, :], p.astype(BF16))
            dk[part, at_keys] += nt(qt[part, :], ds)
            out.append(carry[h] + nn(kt[part, at_keys], ds))
        return tuple(out)

    zero = jnp.zeros((HEAD, BLK), F32)
    return lax.fori_loop(0, count, body, (zero,) * heads)


def first_back_kernel(per, sc, qt, kn, kt, vn, dot_, ot, lse, gq, gkv, dqt, dk_o, dv_o, dk, dv, zq, zd):
    step = pl.program_id(0)

    @pl.when(step == 0)
    def _():
        dk[...] = jnp.zeros(dk.shape, F32)
        dv[...] = jnp.zeros(dv.shape, F32)

    dq = backward_block(0, per, sc, qt, kn, kt, vn, dot_, ot, lse, gq, gkv, dk, dv, zq, zd)
    for h, part in enumerate(dq):
        dqt[h * HEAD : (h + 1) * HEAD, :] = part.astype(BF16)

    @pl.when(step == pl.num_programs(0) - 1)
    def _():
        dk_o[...] = dk[...]
        dv_o[...] = dv[...]


def folded(v):
    return sum(v[at : at + FOLD, :] for at in range(0, v.shape[0], FOLD))


def halves(row):
    high = row.astype(BF16)
    return [high, (row - high.astype(F32)).astype(BF16)]


def second_back_kernel(
    per, pieces, sc, qt, kn, kt, vn, dot_, ot, lse, gq, gkv,
    dk_i, dv_i, dqa, go, gox, gain, gain_m, n1_h, wt_h, *rest
):
    r2, r3, dk_o, dv_o = rest[:4]
    outs = rest[4 : 4 + pieces]
    dk, dv, dqb, zq, zd, n1, wt, gs, sems = rest[4 + pieces :]
    step = pl.program_id(0)
    cols = dk.shape[0]
    copies = [
        pltpu.make_async_copy(n1_h, n1, sems.at[0]),
        pltpu.make_async_copy(wt_h, wt, sems.at[1]),
    ]

    @pl.when(step == 0)
    def _():
        for copy in copies:
            copy.start()
        dk[...] = dk_i[...]
        dv[...] = dv_i[...]

    dq = backward_block(1, per, sc, qt, kn, kt, vn, dot_, ot, lse, gq, gkv, dk, dv, zq, zd)
    at = pl.multiple_of(step * BLK, BLK)
    for h, part in enumerate(dq):
        dqb[h * HEAD : (h + 1) * HEAD, pl.ds(at, BLK)] = part.astype(BF16)

    @pl.when(step == pl.num_programs(0) - 1)
    def _():
        for copy in copies:
            copy.wait()
        both = dqb.shape[1]
        dkb, dvb = dk[...].astype(BF16), dv[...].astype(BF16)
        dk_o[...] = dkb[:, :both]
        dv_o[...] = dvb[:, :both]
        grads = jnp.concatenate([dkb[:, both:], dqb[...], dvb[:, both:]], axis=0)
        part = nn(grads.T, wt[0 : 3 * cols, :]).astype(BF16)
        r2[...] = part[: both // 2]
        r3[...] = part[both // 2 :]
        gt = [
            nn(dkb, n1[...]),
            nn(dqa[...], n1[:both, :]) + nn(dqb[...], n1[both:, :]),
            nn(dvb, n1[...]),
        ]
        total = jnp.zeros((FOLD, gain.shape[1]), F32)
        for j in range(3):
            total += folded(gt[j] * wt[j * cols : (j + 1) * cols, :].astype(F32))
        gain_a = jnp.sum(total, axis=0, keepdims=True) / gain[...]
        gt.append(go[...] + gox[...].astype(F32))
        gs[...] = jnp.concatenate(gt, axis=0).T.astype(BF16)
        depth = gs.shape[0] // pieces
        extra = halves(gain_a) + halves(jnp.sum(gain_m[...], axis=0, keepdims=True))
        extra.append(jnp.zeros((EXTRA - len(extra), gain.shape[1]), BF16))
        extra = jnp.concatenate(extra, axis=0)
        for j, out in enumerate(outs):
            start = pl.multiple_of((sc[1] ^ j) * depth, 16) if pieces > 1 else 0
            out[0:depth, :] = gs[pl.ds(start, depth), :]
            out[depth : depth + EXTRA, :] = extra


def back_specs(half, total, cols):
    blocks = total // BLK // 2
    return [
        SMEM,
        pl.BlockSpec((cols, BLK), lambda i: (1, half * blocks + i)),
        whole((total, cols)),
        pl.BlockSpec((cols, total), lambda i: (0, 0)),
        whole((total, cols)),
        pl.BlockSpec((cols, BLK), lambda i: (0, i)),
        pl.BlockSpec((cols, BLK), lambda i: (0, i)),
        pl.BlockSpec((8, BLK), lambda i: (0, i)),
        whole((1, total)),
        whole((total, 128)),
    ]


def spread_scratch(cols):
    return [pltpu.VMEM((cols // HEAD, cols, BLK), BF16)] * 2


def first_back(sc, qkvt, kn, vn, dout, out, lse, gq, gkv):
    total, cols = kn.shape
    blocks = total // BLK // 2
    return pl.pallas_call(
        functools.partial(first_back_kernel, total // 4 // BLK),
        grid=(blocks,),
        in_specs=back_specs(0, total, cols),
        out_specs=[
            pl.BlockSpec((cols, BLK), lambda i: (0, i)),
            whole((cols, total)),
            whole((cols, total)),
        ],
        out_shape=[
            shape((cols, blocks * BLK), BF16),
            shape((cols, total), F32),
            shape((cols, total), F32),
        ],
        scratch_shapes=[pltpu.VMEM((cols, total), F32)] * 2 + spread_scratch(cols),
        name="attention_back",
        cost_estimate=cost(20),
    )(sc, qkvt, kn, qkvt, vn, dout, out, lse, gq, gkv)


def second_back(pieces, sc, qkvt, kn, vn, dout, out, lse, gq, gkv, dk, dv, dqa, go, gox, gain, gain_m, n1, wt):
    total, cols = kn.shape
    blocks = total // BLK // 2
    both = blocks * BLK
    width = n1.shape[1]
    piece = (width // pieces + EXTRA, 4 * cols)
    return pl.pallas_call(
        functools.partial(second_back_kernel, total // 4 // BLK, pieces),
        grid=(blocks,),
        in_specs=back_specs(1, total, cols)
        + [whole((cols, total))] * 2
        + [whole((cols, both))]
        + [whole((cols, width))] * 2
        + [whole((1, width)), whole(gain_m.shape)]
        + [HBM] * 2,
        out_specs=[whole((both // 2, width))] * 2
        + [whole((cols, both))] * 2
        + [whole(piece)] * pieces,
        out_shape=[shape((both // 2, width), BF16)] * 2
        + [shape((cols, both), BF16)] * 2
        + [shape(piece, BF16)] * pieces,
        scratch_shapes=[pltpu.VMEM((cols, total), F32)] * 2
        + [pltpu.VMEM((cols, both), BF16)]
        + spread_scratch(cols)
        + [
            pltpu.VMEM(n1.shape, BF16),
            pltpu.VMEM(wt.shape, BF16),
            pltpu.VMEM((width, 4 * cols), BF16),
            pltpu.SemaphoreType.DMA((2,)),
        ],
        compiler_params=room(48),
        name="attention_back_end",
        cost_estimate=cost(0.01),
    )(sc, qkvt, kn, qkvt, vn, dout, out, lse, gq, gkv, dk, dv, dqa, go, gox, gain, gain_m, n1, wt)


def rows_kernel(fn, counts, n_const, n_out, chunks, split, *refs):
    ins = []
    for count in counts:
        ins.append(refs[:count])
        refs = refs[count:]
    n_in = len(ins)
    consts, refs = refs[:n_const], refs[n_const:]
    outs, refs = refs[:n_out], refs[n_out:]
    pieces, refs = refs[:split], refs[split:]
    sums, refs = refs[: len(refs) - n_in - n_out - 2], refs[len(refs) - n_in - n_out - 2 :]
    held, made, (in_sem, out_sem) = refs[:n_in], refs[n_in:-2], refs[-2:]
    size = held[0].shape[0] // chunks

    def part(c):
        return pl.ds(pl.multiple_of(c * size, size), size)

    def arrival(i, c):
        src = ins[i][c] if len(ins[i]) > 1 else ins[i][0].at[part(c)]
        return pltpu.make_async_copy(src, held[i].at[part(c)], in_sem.at[i, c])

    def departure(i, c):
        return pltpu.make_async_copy(made[i].at[part(c)], outs[i].at[part(c)], out_sem.at[i, c])

    def apart(c):
        return pltpu.make_async_copy(made[-1].at[part(c)], pieces[c], out_sem.at[n_out, c])

    for c in range(chunks):
        for i in range(n_in):
            arrival(i, c).start()
    def each(c, of_chunk, many):
        if not many:
            of_chunk(c)
            return
        for known in range(chunks):

            @pl.when(c == known)
            def _(known=known):
                of_chunk(known)

    def body(c, totals):
        for i in range(n_in):
            each(c, lambda c, i=i: arrival(i, c).wait(), len(ins[i]) > 1)
        where = pl.ds(pl.multiple_of(c * size, size), size)
        results, adds = fn([r[where, :] for r in held], [r[...] for r in consts])
        for i, value in enumerate(results):
            made[i][where, :] = value
        if split:
            each(c, lambda c: apart(c).start(), True)
        for i in range(n_out):
            departure(i, c).start()
        return tuple(t + a for t, a in zip(totals, adds))

    totals = lax.fori_loop(0, chunks, body, tuple(jnp.zeros(r.shape, F32) for r in sums))
    for ref, t in zip(sums, totals):
        ref[...] = t
    for c in range(chunks):
        if split:
            apart(c).wait()
        for i in range(n_out):
            departure(i, c).wait()


def by_rows(name, fn, ins, arrived, consts, kinds, sums=(), chunks=2, split=0):
    near = len(ins)
    ins = (*ins, *arrived)
    dims = ins[0].shape
    flat = [v if isinstance(v, tuple) else (v,) for v in ins]
    return pl.pallas_call(
        functools.partial(
            rows_kernel, fn, [len(v) for v in flat], len(consts), len(kinds), chunks, split
        ),
        in_specs=[HBM] * near
        + [ANY] * sum(len(v) for v in flat[near:])
        + [VMEM] * len(consts),
        out_specs=[HBM] * (len(kinds) + split) + [VMEM] * len(sums),
        out_shape=[shape(dims, k) for k in kinds]
        + [shape((dims[0] // chunks, dims[1]), kinds[-1])] * split
        + [shape(d, F32) for d in sums],
        scratch_shapes=[pltpu.VMEM(dims, v[0].dtype) for v in flat]
        + [pltpu.VMEM(dims, k) for k in kinds]
        + [
            pltpu.SemaphoreType.DMA((len(ins), chunks)),
            pltpu.SemaphoreType.DMA((len(kinds) + 1, chunks)),
        ],
        compiler_params=room(24),
        name=name,
        cost_estimate=cost(0.01),
    )(*[part for v in flat for part in v], *consts)


def out_kernel(om, ox, wm, wx, own, other, omv, oxv, wmv, wxv, ownv, otherv, sems):
    rows = own.shape[0]
    copies = [
        pltpu.make_async_copy(src, dst, sems.at[i])
        for i, (src, dst) in enumerate(((om, omv), (ox, oxv), (wm, wmv), (wx, wxv)))
    ]
    for copy in copies:
        copy.start()
    for copy in copies:
        copy.wait()
    leave = [
        pltpu.make_async_copy(made, out, sems.at[4 + i])
        for i, (made, out) in enumerate(((otherv, other), (ownv, own)))
    ]

    def body(i, carry):
        where = pl.ds(pl.multiple_of((1 - i) * rows, rows), rows)
        part = (nn(omv[:, where].T, wmv[...]) + nn(oxv[:, where].T, wxv[...])).astype(BF16)
        for c, (made, copy) in enumerate(zip((otherv, ownv), leave)):

            @pl.when(i == c)
            def _(made=made, copy=copy):
                made[...] = part
                copy.start()

        return carry

    lax.fori_loop(0, 2, body, 0)
    for copy in leave:
        copy.wait()


def out_projection(om, ox, wm, wx):
    cols, both = om.shape
    width = wm.shape[1]
    made = (both // 2, width)
    return pl.pallas_call(
        out_kernel,
        in_specs=[HBM, ANY, HBM, ANY],
        out_specs=[HBM] * 2,
        out_shape=[shape(made, BF16)] * 2,
        scratch_shapes=[pltpu.VMEM(v.shape, BF16) for v in (om, ox, wm, wx)]
        + [pltpu.VMEM(made, BF16)] * 2
        + [pltpu.SemaphoreType.DMA((6,))],
        compiler_params=room(24),
        name="out_projection",
        cost_estimate=cost(0.01),
    )(om, ox, wm, wx)


def middle_rows(held, consts):
    tokens, own, got = (v.astype(F32) for v in held)
    h1 = tokens + (own + got)
    scale = lax.rsqrt(jnp.mean(h1 * h1, axis=-1, keepdims=True) + eps_norm)
    return (h1, (h1 * scale * consts[0]).astype(BF16)), ()


def middle(tokens, own, got, gain):
    return by_rows("middle", middle_rows, (tokens, own), (got,), (gain,), (F32, BF16), split=2)


def mlp_kernel(at, aliased, na, nb, ya, yb, w, *refs):
    ma, mb, da, db, hid_o, dgu_o, nv, yv, wv, mv, dv, hv, gv, in_sem, w_sem, out_sem = refs[aliased:]
    rows, units = na.shape[0], hv.shape[1]
    arrivals, departures = [], []
    for c, (n, y, m, d) in enumerate(((na, ya, ma, da), (nb, yb, mb, db))):
        part, place = pl.ds(c * rows, rows), pl.ds(at, rows)
        arrivals += [
            pltpu.make_async_copy(n, nv.at[part], in_sem.at[0, c]),
            pltpu.make_async_copy(y.at[place], yv.at[part], in_sem.at[1, c]),
        ]
        departures.append(
            [
                pltpu.make_async_copy(dv.at[part], d, out_sem.at[0, c]),
                pltpu.make_async_copy(mv.at[part], m.at[place], out_sem.at[1, c]),
                pltpu.make_async_copy(hv.at[part], hid_o.at[part], out_sem.at[2, c]),
                pltpu.make_async_copy(gv.at[part], dgu_o.at[part], out_sem.at[3, c]),
            ]
        )
    weights = [
        pltpu.make_async_copy(
            w.at[:, pl.ds(j * units, units)], wv.at[:, pl.ds(j * units, units)], w_sem.at[j]
        )
        for j in range(3)
    ]
    for copy in weights + arrivals:
        copy.start()
    for copy in weights + arrivals:
        copy.wait()
    wg, wu, wd = (wv.at[:, pl.ds(j * units, units)] for j in range(3))
    tile = rows if rows < 512 else 512

    def body(i, carry):
        part = pl.ds(pl.multiple_of(i * tile, tile), tile)
        n2 = nv[part, :]
        gate, up = nn(n2, wg[...]), nn(n2, wu[...])
        dhid = nn(yv[part, :], wd[...])
        square = gate * gate
        share = 0.5 * jnp.tanh(gate * (ROOT + ROOT * 0.044715 * square)) + 0.5
        value = gate * share
        slope = share + value * (1.0 - share) * (2.0 * ROOT + 6.0 * ROOT * 0.044715 * square)
        dgate = (dhid * up * slope).astype(BF16)
        dup = (dhid * value).astype(BF16)
        hidden = (value * up).astype(BF16)
        dv[part, :] = (nt(dgate, wg[...]) + nt(dup, wu[...])).astype(BF16)
        hv[part, :] = hidden
        gv[part, 0:units] = dgate
        gv[part, units : 2 * units] = dup
        mv[part, :] = nt(hidden, wd[...]).astype(BF16)
        for c, copies in enumerate(departures):

            @pl.when(i == c * rows // tile)
            def _(copies=copies):
                for copy in copies:
                    copy.start()

        return carry

    lax.fori_loop(0, 2 * rows // tile, body, 0)
    for copies in departures:
        for copy in copies:
            copy.wait()


def mlp_both(na, nb, ya, yb, weights, at=0, into=(), mib=32):
    rows, width = na.shape
    units = weights.shape[1] // 3
    both = 2 * rows
    return pl.pallas_call(
        functools.partial(mlp_kernel, at, len(into)),
        in_specs=[ANY] * 4 + [HBM] * (1 + len(into)),
        out_specs=[HBM] * 6,
        out_shape=[shape(ya.shape, BF16)] * 2
        + [shape((rows, width), BF16)] * 2
        + [shape((both, units), BF16), shape((both, 2 * units), BF16)],
        scratch_shapes=[
            pltpu.VMEM((both, width), BF16),
            pltpu.VMEM((both, width), BF16),
            pltpu.VMEM(weights.shape, BF16),
            pltpu.VMEM((both, width), BF16),
            pltpu.VMEM((both, width), BF16),
            pltpu.VMEM((both, units), BF16),
            pltpu.VMEM((both, 2 * units), BF16),
            pltpu.SemaphoreType.DMA((2, 2)),
            pltpu.SemaphoreType.DMA((3,)),
            pltpu.SemaphoreType.DMA((4, 2)),
        ],
        input_output_aliases={5 + i: i for i in range(len(into))},
        compiler_params=room(mib),
        name="mlp",
        cost_estimate=cost(8),
    )(na, nb, ya, yb, weights, *into)


def mlp_weights_kernel(order, n_in, *refs):
    ins, (out, *held, total, made, sems, sem) = refs[:n_in], refs[n_in:]
    copies = []
    for group, moves in enumerate(order):
        for which, start, rows, at in moves:
            copy = pltpu.make_async_copy(
                ins[which].at[pl.ds(start, rows)], held[group].at[pl.ds(at, rows)], sems.at[len(copies)]
            )
            copies.append((at + rows, copy))
    size = held[0].shape[0] // 2
    copies.sort(key=lambda v: v[0])
    for _, copy in copies:
        copy.start()
    wide = held[2].shape[1]

    def body(i, carry):
        for c in range(2):

            @pl.when(i == c)
            def _(c=c):
                for end, copy in copies:
                    if c * size < end <= (c + 1) * size:
                        copy.wait()

        rows = pl.ds(pl.multiple_of(i * size, size), size)
        n2, dy, dgu, hidden = (r[rows, :] for r in held)
        for at, left, right in ((0, n2, dgu), (wide, dy, hidden)):
            cols = pl.ds(at, right.shape[1])
            new = nn(left.T, right) + total[:, cols]
            total[:, cols] = new
            made[:, cols] = new.astype(BF16)
        return carry

    total[...] = jnp.zeros(total.shape, F32)
    lax.fori_loop(0, 2, body, 0)
    leave = pltpu.make_async_copy(made, out, sem)
    leave.start()
    leave.wait()


def mlp_weights(n2, dy, dgu, hidden):
    ins = (*n2, *dy, *dgu, *hidden)
    rows = n2[0].shape[0]
    half = rows // 2
    first = [(0, 0, rows, 0), (1, 0, rows, rows)]
    order = [
        first + [(2, 0, half, 2 * rows), (4, 0, half, 2 * rows + half), (3, 0, half, 3 * rows), (5, 0, half, 3 * rows + half)],
        [(6 + j, 0, rows, j * rows) for j in range(4)],
    ]
    for base in (10, 13):
        order.append(
            [
                (base, 0, 2 * rows, 0),
                (base + 1, 0, half, 2 * rows),
                (base + 2, 0, half, 2 * rows + half),
                (base + 1, half, half, 3 * rows),
                (base + 2, half, half, 3 * rows + half),
            ]
        )
    width = n2[0].shape[1]
    dims = (width, dgu[0].shape[1] + hidden[0].shape[1])
    return pl.pallas_call(
        functools.partial(mlp_weights_kernel, order, len(ins)),
        in_specs=[HBM] * len(ins),
        out_specs=HBM,
        out_shape=shape(dims, BF16),
        scratch_shapes=[
            pltpu.VMEM((4 * rows, v.shape[1]), BF16) for v in (n2[0], dy[0], dgu[0], hidden[0])
        ]
        + [
            pltpu.VMEM(dims, F32),
            pltpu.VMEM(dims, BF16),
            pltpu.SemaphoreType.DMA((sum(len(v) for v in order),)),
            pltpu.SemaphoreType.DMA,
        ],
        compiler_params=room(48),
        name="mlp_weights",
        cost_estimate=cost(10),
    )(*ins)


def middle_back_rows(held, consts):
    dy, h1, *shares = (v.astype(F32) for v in held)
    dn2 = sum(shares[1:], shares[0])
    scale = lax.rsqrt(jnp.mean(h1 * h1, axis=-1, keepdims=True) + eps_norm)
    hat = dn2 * consts[0]
    dh1 = (
        dy
        + scale * hat
        - h1 * (scale * scale * scale) * jnp.mean(hat * h1, axis=-1, keepdims=True)
    )
    return (dh1, dh1.astype(BF16)), (folded(dn2 * h1 * scale),)


def middle_back(dy, h1, a, b, c, gain):
    return by_rows(
        "middle_back",
        middle_back_rows,
        (dy, h1, a),
        (b, c),
        (gain,),
        (F32, BF16),
        sums=((FOLD, dy.shape[1]),),
    )


def out_back_kernel(own, other, wm, wx, om, ox, dm_o, dx_o, gm_o, gx_o, *scratch):
    refs = (own, other, wm, wx, om, ox)
    held, made, sems = scratch[:6], scratch[6:10], scratch[10]
    copies = [pltpu.make_async_copy(src, dst, sems.at[i]) for i, (src, dst) in enumerate(zip(refs, held))]
    for copy in copies:
        copy.start()
    ownv, otherv, wmv, wxv, omv, oxv = held
    dm, dx, gm, gx = made
    rows = own.shape[0]
    for copy in copies:
        copy.wait()
    leave = [
        pltpu.make_async_copy(src, dst, sems.at[6 + i])
        for i, (src, dst) in enumerate(((dx, dx_o), (dm, dm_o), (gx, gx_o), (gm, gm_o)))
    ]
    for i, (w, out) in enumerate(((wxv, dx), (wmv, dm))):
        for at, ref in ((0, ownv), (rows, otherv)):
            out[:, at : at + rows] = nt(w[...], ref[...]).astype(BF16)
        leave[i].start()
    gx[...] = (nn(oxv[:, :rows], ownv[...]) + nn(oxv[:, rows:], otherv[...])).astype(BF16)
    leave[2].start()
    gm[...] = nn(omv[:, :rows], ownv[...]) + nn(omv[:, rows:], otherv[...])
    leave[3].start()
    for copy in leave:
        copy.wait()


def out_back(own, other, wm, wx, om, ox):
    cols, both = om.shape
    width = own.shape[1]
    ins = (own, other, wm, wx, om, ox)
    outs = [
        ((cols, both), BF16),
        ((cols, both), BF16),
        ((cols, width), F32),
        ((cols, width), BF16),
    ]
    return pl.pallas_call(
        out_back_kernel,
        in_specs=[HBM, ANY, HBM, ANY, HBM, ANY],
        out_specs=[HBM] * 4,
        out_shape=[shape(*v) for v in outs],
        scratch_shapes=[pltpu.VMEM(v.shape, BF16) for v in ins]
        + [pltpu.VMEM(*v) for v in outs]
        + [pltpu.SemaphoreType.DMA((10,))],
        compiler_params=room(24),
        name="out_back",
        cost_estimate=cost(0.01),
    )(*ins)


def rows_back_kernel(dk, dq, dv, wt, a_o, b_o):
    rows = a_o.shape[0]

    def body(i, carry):
        where = pl.ds(pl.multiple_of(i * rows, rows), rows)
        grads = jnp.concatenate([dk[:, where], dq[:, where], dv[:, where]], axis=0)
        part = nn(grads.T, wt[...]).astype(BF16)
        for c, ref in enumerate((a_o, b_o)):

            @pl.when(i == c)
            def _(ref=ref):
                ref[...] = part

        return carry

    lax.fori_loop(0, 2, body, 0)


def rows_back(dk, dq, dv, wt):
    cols, both = dq.shape
    width = wt.shape[1]
    return pl.pallas_call(
        rows_back_kernel,
        out_shape=[shape((both // 2, width), BF16)] * 2,
        compiler_params=room(24),
        name="rows_back",
        cost_estimate=cost(0.01),
    )(dk, dq, dv, wt)


def last_rows(held, consts):
    x, dh1, *shares = (v.astype(F32) for v in held)
    dn1 = sum(shares[1:], shares[0])
    scale = lax.rsqrt(jnp.mean(x * x, axis=-1, keepdims=True) + eps_norm)
    hat = dn1 * consts[0]
    out = (
        dh1
        + scale * hat
        - x * (scale * scale * scale) * jnp.mean(hat * x, axis=-1, keepdims=True)
    )
    return (out.astype(BF16),), ()


def last(tokens, dh1, a, b, c, gain):
    return by_rows("last", last_rows, (tokens, dh1, a), (b, c), (gain,), (BF16,))[0]


def grads_sum_kernel(count, *refs):
    ins, outs, gains_o = refs[:count], refs[count:-1], refs[-1]
    rows, cols = outs[0].shape
    total = ins[0][0:rows, :].astype(F32)
    for ref in ins[1:]:
        total = total + ref[0:rows, :].astype(F32)
    for j, ref in enumerate(outs):
        ref[...] = total[:, j * cols : (j + 1) * cols]
    tail = [ref[rows : rows + EXTRA, :].astype(F32) for ref in ins]
    gains = tail[0]
    for part in tail[1:]:
        gains = gains + part
    gains = gains[0:4, :] + gains[4:8, :]
    gains_o[...] = jnp.concatenate(
        [gains[0:1, :] + gains[1:2, :], gains[2:3, :] + gains[3:4, :]], axis=0
    )


def grads_sum(parts):
    rows, width = parts[0].shape
    rows -= EXTRA
    return pl.pallas_call(
        functools.partial(grads_sum_kernel, len(parts)),
        out_shape=[shape((rows, width // 4), F32)] * 4 + [shape((2, width), F32)],
        compiler_params=room(16),
        name="grads_sum",
        cost_estimate=cost(0.01),
    )(*parts)


def local(
    dp,
    mp,
    tokens,
    w_query,
    w_key,
    w_value,
    w_out,
    w_gate,
    w_up,
    w_down,
    norm_attn,
    norm_mlp,
    valid_counts,
    group_ids,
    cotangent,
):
    me, row = lax.axis_index("mp"), lax.axis_index("dp")
    cols = w_query.shape[1]
    length = group_ids.shape[1]

    def core(v):
        return lax.ppermute(v, "mp", [(i, i ^ 1) for i in range(mp)])

    def across(v):
        return lax.ppermute(v, "mp", [(i, i ^ 2) for i in range(mp)])

    def core_across(v):
        return lax.ppermute(v, "mp", [(i, i ^ 3) for i in range(mp)])

    def far(v, k):
        return lax.ppermute(v, "dp", [(i, i ^ k) for i in range(dp)])

    def after(v, *others):
        return lax.optimization_barrier((v, *others))[0]

    def summed(a, b):
        return (a.astype(F32) + b.astype(F32)).astype(BF16)

    direct = dp <= DIRECT
    gain_a, gain_m = norm_attn[None], norm_mlp[None]

    gq = group_ids
    flat = group_ids[0]
    valid = valid_counts[0]
    tiles = flat.reshape(length // BLK, BLK)
    low = jnp.sum(flat[None, :] < tiles[:, :1], axis=1) // BLK
    high = jnp.minimum(jnp.sum(flat[None, :] <= tiles[:, -1:], axis=1), valid)
    high = (high + BLK - 1) // BLK
    head = jnp.stack([me, row, valid, valid, valid, valid, valid, valid])
    sc = jnp.concatenate([head, low, high]).astype(jnp.int32)
    keyed = jnp.where(jnp.arange(length, dtype=jnp.int32) < valid, flat, -1)
    gkv = jnp.broadcast_to(keyed[:, None], (length, 128))

    tok2 = across(tokens)
    w_attn = jnp.concatenate([w_key, w_query, w_value, w_out], axis=1)
    w_mlp = jnp.concatenate([w_gate, w_up, w_down], axis=1)
    if direct:
        near = [w_attn] + [far(w_attn, k) for k in range(2, dp, 2)]
        middle_way = len(near) // 2
        near[middle_way] = after(near[middle_way], sc, gkv, w_mlp)
        w_pieces = [p for v in near for p in (v, far(v, 1))]
        tok1 = core(after(tokens, w_pieces[1]))
    else:
        w_pieces = [lax.all_gather(w_attn, "dp", axis=0, tiled=True)]
        tok1 = core(tokens)
    w_mlp = lax.all_gather(w_mlp, "dp", axis=0, tiled=True)
    tok3 = core(after(tok2, *w_pieces[1::2]))

    n1, qkvt, kn, vn, wt, wo = qkv(sc, (tokens, tok1, tok2, tok3), gain_a, w_pieces, cols)
    wo_x = across(wo)
    dy0 = cotangent
    dy2 = across(after(cotangent, tok2))
    dy1 = core(after(cotangent, tok3))

    o_far, lse_far = attention(1, sc, qkvt, kn, gq, gkv)
    o_x = across(after(o_far, dy2, wo_x))
    dy3 = core(after(dy2, o_far))
    o_own, lse_own = attention(0, after(sc, o_far), qkvt, kn, gq, gkv)
    p_own, p_other = out_projection(o_own, o_x, wo, wo_x)
    h1, n2, n2_a, n2_b = middle(tokens, p_own, core(p_other), gain_m)

    half = n2.shape[0] // 2
    n2_1 = core(n2)
    far_a = across(n2_a)
    far_b = across(n2_b)
    m0, m1, d0, d1, hid_o, dgu_o = mlp_both(n2, n2_1, dy0, dy1, w_mlp, mib=60)
    side_a = core(after(far_a, d0))
    m2, m3, d2a, d3a, hid_a, dgu_a = mlp_both(far_a, side_a, dy2, dy3, w_mlp)
    dsum_a = summed(d2a, core(d3a))
    dx_a = across(dsum_a)
    side_b = core(after(far_b, d2a))
    far_b = after(far_b, dsum_a)
    m2, m3, d2b, d3b, hid_b, dgu_b = mlp_both(far_b, side_b, dy2, dy3, w_mlp, half, (m2, m3))

    d_sum = summed(d2b, core(after(d3b, dx_a)))
    dx_b = across(d_sum)
    mlp_all = mlp_weights(
        (n2, n2_1, far_a, side_a, far_b, side_b),
        (dy0, dy1, dy2, dy3),
        (dgu_o, dgu_a, dgu_b),
        (after(hid_o, d_sum), hid_a, hid_b),
    )
    mlp_grads = lax.psum_scatter(mlp_all, "dp", scatter_dimension=0, tiled=True)
    m_other, m_core = core(m3), core(after(m1, d_sum))
    dh1, da, gain_m_part = middle_back(
        dy0,
        h1,
        d0,
        core(after(d1, d_sum)),
        (dx_a, after(dx_b, mlp_all, m_other, m_core)),
        gain_m,
    )

    do_own, do_send, go, go_send = out_back(da, core(da), wo, wo_x, o_own, o_x)
    do_far = across(do_send)
    go_x = across(go_send)
    m_x = across(after(summed(after(m2, da), m_other), do_send))
    dq_own, dk, dv = first_back(sc, qkvt, kn, vn, do_own, o_own, lse_own, gq, gkv)
    r2, r3, dk_own, dv_own, *grads = second_back(
        dp if direct else 1,
        sc, qkvt, kn, vn, do_far, o_far, lse_far, gq, gkv,
        dk, dv, dq_own, go, go_x, gain_a, gain_m_part, n1, wt,
    )
    r_sum = summed(r2, core(after(r3, m_x)))
    r_x = across(r_sum)
    depth = w_query.shape[0]
    parts = []
    if direct:
        for k in range(dp - 2, 0, -2):
            sent = grads[k + 1]
            if k < dp // 2 and parts:
                sent = after(sent, parts[-1])
            near, other = grads[k], after(far(sent, 1), r_sum)
            both = summed(near[:depth], other[:depth])
            part = jnp.concatenate([both, near[depth : depth + 4], other[depth : depth + 4]], axis=0)
            parts.insert(0, part)
        last_sent = after(grads[1], parts[0]) if parts else grads[1]
        parts = [far(part, 2 * k + 2) for k, part in enumerate(parts)]
        parts = [grads[0], far(last_sent, 1)] + parts
    r0, r1 = rows_back(after(dk_own, r_sum), dq_own, dv_own, wt)
    grad_tokens = last(tokens, dh1, r0, core(r1), r_x, gain_a)
    output = (
        h1 + (m0.astype(F32) + m_core.astype(F32) + after(m_x, r_sum).astype(F32))
    ).astype(BF16)
    units = w_gate.shape[1]
    grad_gate, grad_up, grad_down = (
        mlp_grads[:, j * units : (j + 1) * units].astype(F32) for j in range(3)
    )
    if direct:
        parts[0] = after(parts[0], grad_tokens, output, grad_gate)
        grad_k, grad_q, grad_v, grad_o, gains = grads_sum(parts)
        gains = gains + core(gains) + across(gains) + core_across(gains)
    else:
        width = tokens.shape[1]
        attn_grads = lax.psum_scatter(
            grads[0][:width], "dp", scatter_dimension=0, tiled=True
        ).astype(F32)
        grad_k, grad_q, grad_v, grad_o = jnp.split(attn_grads, 4, axis=1)
        extra = grads[0][width : width + 4].astype(F32)
        gains = lax.psum(extra[0::2] + extra[1::2], ("dp", "mp"))

    return (
        output,
        grad_tokens,
        grad_q,
        grad_k,
        grad_v,
        grad_o,
        grad_gate,
        grad_up,
        grad_down,
        gains[0],
        gains[1],
    )


def solution(mesh):
    rows, weight = P(("dp", "mp"), None), P("dp", "mp")
    return jax.shard_map(
        functools.partial(local, mesh.shape["dp"], mesh.shape["mp"]),
        mesh=mesh,
        in_specs=(rows,) + (weight,) * 7 + (P(), P(), P("dp"), P("dp", None), rows),
        out_specs=(rows, rows) + (weight,) * 7 + (P(), P()),
        check_vma=False,
    )
```

```python
import functools

import jax
import jax.numpy as jnp
from jax import lax
from jax.experimental import pallas as pl
from jax.experimental.pallas import tpu as pltpu
from jax.sharding import PartitionSpec as P

HEAD = 64
BLK = 256
DIRECT = 8
FOLD = 32
EXTRA = 8
ROOT = 0.7978845608028654
eps_norm = 1e-06
neg_large = -1e30
F32 = jnp.float32
BF16 = jnp.bfloat16


def nn(a, b):
    return lax.dot_general(a, b, (((1,), (0,)), ((), ())), preferred_element_type=F32)


def nt(a, b):
    return lax.dot_general(a, b, (((1,), (1,)), ((), ())), preferred_element_type=F32)


def tn(a, b):
    return lax.dot_general(a, b, (((0,), (0,)), ((), ())), preferred_element_type=F32)


def shape(dims, kind):
    return jax.ShapeDtypeStruct(dims, kind)


def whole(dims):
    return pl.BlockSpec(dims, lambda *_: (0,) * len(dims))


SMEM = pl.BlockSpec(memory_space=pltpu.SMEM)
VMEM = pl.BlockSpec(memory_space=pltpu.VMEM)
HBM = pl.BlockSpec(memory_space=pltpu.HBM)
ANY = pl.BlockSpec(memory_space=pl.ANY)


def room(mib):
    return pltpu.CompilerParams(vmem_limit_bytes=mib << 20)


def qkv_kernel(pieces, sc, t0, t1, t2, t3, gain, *rest):
    w_refs, (n1_o, qkvt_o, kn_o, vn_o, wt_o, wo_o, xs, ws) = rest[:pieces], rest[pieces:]
    step = pl.program_id(0)
    cols = kn_o.shape[1]

    @pl.when(step == 0)
    def _():
        if pieces == 1:
            ws[...] = w_refs[0][...]
        else:
            depth = w_refs[0].shape[0]
            for j in range(pieces):
                at = pl.multiple_of((sc[1] ^ j) * depth, 16)
                ws[pl.ds(at, depth), :] = w_refs[j][...]
        turned = ws[...].T
        wt_o[...] = turned[: 3 * cols, :]
        wo_o[...] = turned[3 * cols :, :]

    for j, ref in enumerate((t0, t1, t2, t3)):

        @pl.when(step == j)
        def _(ref=ref):
            xs[...] = ref[...]

    x = xs[...].astype(F32)
    scale = lax.rsqrt(jnp.mean(x * x, axis=-1, keepdims=True) + eps_norm)
    n1 = (x * scale * gain[...]).astype(BF16)
    n1_o[...] = n1
    qkvt_o[...] = nt(wt_o[...], n1).astype(BF16)
    kn_o[...] = nn(n1, ws[:, 0:cols]).astype(BF16)
    vn_o[...] = nn(n1, ws[:, 2 * cols : 3 * cols]).astype(BF16)


def qkv(sc, shards, gain, pieces, cols):
    rows, width = shards[0].shape
    total = rows * len(shards)
    return pl.pallas_call(
        functools.partial(qkv_kernel, len(pieces)),
        grid=(len(shards),),
        in_specs=[SMEM]
        + [whole((rows, width))] * 4
        + [whole((1, width))]
        + [whole(p.shape) for p in pieces],
        out_specs=[
            pl.BlockSpec((rows, width), lambda i: (i, 0)),
            pl.BlockSpec((3 * cols, rows), lambda i: (0, i)),
            pl.BlockSpec((rows, cols), lambda i: (i, 0)),
            pl.BlockSpec((rows, cols), lambda i: (i, 0)),
            whole((3 * cols, width)),
            whole((cols, width)),
        ],
        out_shape=[
            shape((total, width), BF16),
            shape((3 * cols, total), BF16),
            shape((total, cols), BF16),
            shape((total, cols), BF16),
            shape((3 * cols, width), BF16),
            shape((cols, width), BF16),
        ],
        scratch_shapes=[pltpu.VMEM((rows, width), BF16), pltpu.VMEM((width, 4 * cols), BF16)],
        name="qkv",
        cost_estimate=cost(0.01),
    )(sc, *shards, gain, *pieces)


def spread(rows, z_ref):
    heads = rows.shape[0] // HEAD
    z_ref[...] = jnp.zeros(z_ref.shape, z_ref.dtype)
    for h in range(heads):
        z_ref[h, h * HEAD : (h + 1) * HEAD, :] = rows[h * HEAD : (h + 1) * HEAD, :]


def cost(us):
    return pl.CostEstimate(flops=int(us * 1e9), transcendentals=0, bytes_accessed=1024)


def span(sc, half, per, blocks):
    me = sc[0]
    stored = half * blocks + pl.program_id(0)
    shard = (stored // per) ^ me
    place = shard * per + lax.rem(stored, per)
    low, high = sc[8 + place] // per, (sc[16 + place] + per - 1) // per
    has_own = jnp.logical_and(low <= shard, shard < high)
    count = jnp.maximum(high - low, 0) - has_own.astype(jnp.int32)

    def at(t):
        other = low + t - 1
        other = jnp.where(t == 0, shard, other + (other >= shard).astype(jnp.int32))
        return other, other ^ me

    return place, count + 1, at


def allowed(gkv, queries, place, shard, size, own=True):
    keys = gkv[pl.ds(pl.multiple_of(shard * size, size), size), :]
    mask = jnp.concatenate([keys] * (BLK // 128), axis=1) == queries
    if not own:
        return mask
    key_at = lax.broadcasted_iota(jnp.int32, mask.shape, 0)
    query_at = lax.broadcasted_iota(jnp.int32, mask.shape, 1) + (place * BLK - shard * size)
    return mask | (key_at == query_at)


def forward_kernel(half, per, sc, qt, kn, vt, gq, gkv, ot, lse, zq):
    heads = qt.shape[0] // HEAD
    size = per * BLK
    place, count, at = span(sc, half, per, pl.num_programs(0))
    spread(qt, zq)
    queries = gq[:, pl.ds(pl.multiple_of(place * BLK, BLK), BLK)]

    def scores(t, own):
        shard, stored = at(t)
        mask = allowed(gkv, queries, place, shard, size, own)
        where = pl.ds(pl.multiple_of(stored * size, size), size)
        keys = kn[where, :]
        return where, [jnp.where(mask, nn(keys, zq[h]), neg_large) for h in range(heads)]

    def mixed(h, where, p):
        return nn(vt[h * HEAD : (h + 1) * HEAD, where], p.astype(BF16))

    carry = []
    where, first = scores(0, True)
    for h, s in enumerate(first):
        top = jnp.max(s, axis=0, keepdims=True)
        p = jnp.exp(s - top)
        carry.append((top, jnp.sum(p, axis=0, keepdims=True), mixed(h, where, p)))

    def body(t, carry):
        where, more = scores(t, False)
        out = []
        for h, s in enumerate(more):
            top, total, acc = carry[h]
            higher = jnp.maximum(top, jnp.max(s, axis=0, keepdims=True))
            p = jnp.exp(s - higher)
            fade = jnp.exp(top - higher)
            out.append(
                (
                    higher,
                    fade * total + jnp.sum(p, axis=0, keepdims=True),
                    fade * acc + mixed(h, where, p),
                )
            )
        return tuple(out)

    carry = lax.fori_loop(1, count, body, tuple(carry))
    for h, (top, total, acc) in enumerate(carry):
        ot[h * HEAD : (h + 1) * HEAD, :] = (acc / total).astype(BF16)
        lse[h : h + 1, :] = top + jnp.log(total)


def attention(half, sc, qkvt, kn, gq, gkv):
    cols3, total = qkvt.shape
    cols = cols3 // 3
    blocks = total // BLK // 2
    per = total // 4 // BLK
    return pl.pallas_call(
        functools.partial(forward_kernel, half, per),
        grid=(blocks,),
        in_specs=[
            SMEM,
            pl.BlockSpec((cols, BLK), lambda i: (1, half * blocks + i)),
            whole((total, cols)),
            pl.BlockSpec((cols, total), lambda i: (2, 0)),
            whole((1, total)),
            whole((total, 128)),
        ],
        out_specs=[
            pl.BlockSpec((cols, BLK), lambda i: (0, i)),
            pl.BlockSpec((8, BLK), lambda i: (0, i)),
        ],
        out_shape=[shape((cols, blocks * BLK), BF16), shape((8, blocks * BLK), F32)],
        scratch_shapes=[pltpu.VMEM((cols // HEAD, cols, BLK), BF16)],
        compiler_params=room(32),
        name="attention",
        cost_estimate=cost(12),
    )(sc, qkvt, kn, qkvt, gq, gkv)


def backward_block(
    half, per, sc, qt, kn, kt, vn, dot_, ot, lse, gq, gkv, dk, dv, zq, zd
):
    heads = qt.shape[0] // HEAD
    size = per * BLK
    place, count, at = span(sc, half, per, pl.num_programs(0))
    queries = gq[:, pl.ds(pl.multiple_of(place * BLK, BLK), BLK)]
    spread(qt, zq)
    spread(dot_, zd)
    deltas = []
    for h in range(heads):
        part = slice(h * HEAD, (h + 1) * HEAD)
        deltas.append(
            jnp.sum(dot_[part, :].astype(F32) * ot[part, :].astype(F32), axis=0, keepdims=True)
        )

    def body(t, carry):
        shard, stored = at(t)
        mask = allowed(gkv, queries, place, shard, size)
        at_keys = pl.ds(pl.multiple_of(stored * size, size), size)
        keys, values = kn[at_keys, :], vn[at_keys, :]
        out = []
        for h in range(heads):
            part = slice(h * HEAD, (h + 1) * HEAD)
            s = jnp.where(mask, nn(keys, zq[h]), neg_large)
            p = jnp.exp(s - lse[h : h + 1, :])
            ds = (p * (nn(values, zd[h]) - deltas[h])).astype(BF16)
            dv[part, at_keys] += nt(dot_[part, :], p.astype(BF16))
            dk[part, at_keys] += nt(qt[part, :], ds)
            out.append(carry[h] + nn(kt[part, at_keys], ds))
        return tuple(out)

    zero = jnp.zeros((HEAD, BLK), F32)
    return lax.fori_loop(0, count, body, (zero,) * heads)


def first_back_kernel(per, sc, qt, kn, kt, vn, dot_, ot, lse, gq, gkv, dqt, dk_o, dv_o, dk, dv, zq, zd):
    step = pl.program_id(0)

    @pl.when(step == 0)
    def _():
        dk[...] = jnp.zeros(dk.shape, F32)
        dv[...] = jnp.zeros(dv.shape, F32)

    dq = backward_block(0, per, sc, qt, kn, kt, vn, dot_, ot, lse, gq, gkv, dk, dv, zq, zd)
    for h, part in enumerate(dq):
        dqt[h * HEAD : (h + 1) * HEAD, :] = part.astype(BF16)

    @pl.when(step == pl.num_programs(0) - 1)
    def _():
        dk_o[...] = dk[...]
        dv_o[...] = dv[...]


def folded(v):
    return sum(v[at : at + FOLD, :] for at in range(0, v.shape[0], FOLD))


def halves(row):
    high = row.astype(BF16)
    return [high, (row - high.astype(F32)).astype(BF16)]


def second_back_kernel(
    per, pieces, sc, qt, kn, kt, vn, dot_, ot, lse, gq, gkv,
    dk_i, dv_i, dqa, go, gox, gain, gain_m, n1_h, wt_h, *rest
):
    r2, r3, dk_o, dv_o = rest[:4]
    outs = rest[4 : 4 + pieces]
    dk, dv, dqb, zq, zd, n1, wt, gs, sems = rest[4 + pieces :]
    step = pl.program_id(0)
    cols = dk.shape[0]
    copies = [
        pltpu.make_async_copy(n1_h, n1, sems.at[0]),
        pltpu.make_async_copy(wt_h, wt, sems.at[1]),
    ]

    @pl.when(step == 0)
    def _():
        for copy in copies:
            copy.start()
        dk[...] = dk_i[...]
        dv[...] = dv_i[...]

    dq = backward_block(1, per, sc, qt, kn, kt, vn, dot_, ot, lse, gq, gkv, dk, dv, zq, zd)
    at = pl.multiple_of(step * BLK, BLK)
    for h, part in enumerate(dq):
        dqb[h * HEAD : (h + 1) * HEAD, pl.ds(at, BLK)] = part.astype(BF16)

    @pl.when(step == pl.num_programs(0) - 1)
    def _():
        for copy in copies:
            copy.wait()
        both = dqb.shape[1]
        dkb, dvb = dk[...].astype(BF16), dv[...].astype(BF16)
        dk_o[...] = dkb[:, :both]
        dv_o[...] = dvb[:, :both]
        grads = jnp.concatenate([dkb[:, both:], dqb[...], dvb[:, both:]], axis=0)
        part = nn(grads.T, wt[0 : 3 * cols, :]).astype(BF16)
        r2[...] = part[: both // 2]
        r3[...] = part[both // 2 :]
        gt = [
            nn(dkb, n1[...]),
            nn(dqa[...], n1[:both, :]) + nn(dqb[...], n1[both:, :]),
            nn(dvb, n1[...]),
        ]
        total = jnp.zeros((FOLD, gain.shape[1]), F32)
        for j in range(3):
            total += folded(gt[j] * wt[j * cols : (j + 1) * cols, :].astype(F32))
        gain_a = jnp.sum(total, axis=0, keepdims=True) / gain[...]
        gt.append(go[...] + gox[...].astype(F32))
        gs[...] = jnp.concatenate(gt, axis=0).T.astype(BF16)
        depth = gs.shape[0] // pieces
        extra = halves(gain_a) + halves(jnp.sum(gain_m[...], axis=0, keepdims=True))
        extra.append(jnp.zeros((EXTRA - len(extra), gain.shape[1]), BF16))
        extra = jnp.concatenate(extra, axis=0)
        for j, out in enumerate(outs):
            start = pl.multiple_of((sc[1] ^ j) * depth, 16) if pieces > 1 else 0
            out[0:depth, :] = gs[pl.ds(start, depth), :]
            out[depth : depth + EXTRA, :] = extra


def back_specs(half, total, cols):
    blocks = total // BLK // 2
    return [
        SMEM,
        pl.BlockSpec((cols, BLK), lambda i: (1, half * blocks + i)),
        whole((total, cols)),
        pl.BlockSpec((cols, total), lambda i: (0, 0)),
        whole((total, cols)),
        pl.BlockSpec((cols, BLK), lambda i: (0, i)),
        pl.BlockSpec((cols, BLK), lambda i: (0, i)),
        pl.BlockSpec((8, BLK), lambda i: (0, i)),
        whole((1, total)),
        whole((total, 128)),
    ]


def spread_scratch(cols):
    return [pltpu.VMEM((cols // HEAD, cols, BLK), BF16)] * 2


def first_back(sc, qkvt, kn, vn, dout, out, lse, gq, gkv):
    total, cols = kn.shape
    blocks = total // BLK // 2
    return pl.pallas_call(
        functools.partial(first_back_kernel, total // 4 // BLK),
        grid=(blocks,),
        in_specs=back_specs(0, total, cols),
        out_specs=[
            pl.BlockSpec((cols, BLK), lambda i: (0, i)),
            whole((cols, total)),
            whole((cols, total)),
        ],
        out_shape=[
            shape((cols, blocks * BLK), BF16),
            shape((cols, total), F32),
            shape((cols, total), F32),
        ],
        scratch_shapes=[pltpu.VMEM((cols, total), F32)] * 2 + spread_scratch(cols),
        name="attention_back",
        cost_estimate=cost(20),
    )(sc, qkvt, kn, qkvt, vn, dout, out, lse, gq, gkv)


def second_back(pieces, sc, qkvt, kn, vn, dout, out, lse, gq, gkv, dk, dv, dqa, go, gox, gain, gain_m, n1, wt):
    total, cols = kn.shape
    blocks = total // BLK // 2
    both = blocks * BLK
    width = n1.shape[1]
    piece = (width // pieces + EXTRA, 4 * cols)
    return pl.pallas_call(
        functools.partial(second_back_kernel, total // 4 // BLK, pieces),
        grid=(blocks,),
        in_specs=back_specs(1, total, cols)
        + [whole((cols, total))] * 2
        + [whole((cols, both))]
        + [whole((cols, width))] * 2
        + [whole((1, width)), whole(gain_m.shape)]
        + [HBM] * 2,
        out_specs=[whole((both // 2, width))] * 2
        + [whole((cols, both))] * 2
        + [whole(piece)] * pieces,
        out_shape=[shape((both // 2, width), BF16)] * 2
        + [shape((cols, both), BF16)] * 2
        + [shape(piece, BF16)] * pieces,
        scratch_shapes=[pltpu.VMEM((cols, total), F32)] * 2
        + [pltpu.VMEM((cols, both), BF16)]
        + spread_scratch(cols)
        + [
            pltpu.VMEM(n1.shape, BF16),
            pltpu.VMEM(wt.shape, BF16),
            pltpu.VMEM((width, 4 * cols), BF16),
            pltpu.SemaphoreType.DMA((2,)),
        ],
        compiler_params=room(48),
        name="attention_back_end",
        cost_estimate=cost(0.01),
    )(sc, qkvt, kn, qkvt, vn, dout, out, lse, gq, gkv, dk, dv, dqa, go, gox, gain, gain_m, n1, wt)


def rows_kernel(fn, counts, n_const, n_out, chunks, split, *refs):
    ins = []
    for count in counts:
        ins.append(refs[:count])
        refs = refs[count:]
    n_in = len(ins)
    consts, refs = refs[:n_const], refs[n_const:]
    outs, refs = refs[:n_out], refs[n_out:]
    pieces, refs = refs[:split], refs[split:]
    sums, refs = refs[: len(refs) - n_in - n_out - 2], refs[len(refs) - n_in - n_out - 2 :]
    held, made, (in_sem, out_sem) = refs[:n_in], refs[n_in:-2], refs[-2:]
    size = held[0].shape[0] // chunks

    def part(c):
        return pl.ds(pl.multiple_of(c * size, size), size)

    def arrival(i, c):
        src = ins[i][c] if len(ins[i]) > 1 else ins[i][0].at[part(c)]
        return pltpu.make_async_copy(src, held[i].at[part(c)], in_sem.at[i, c])

    def departure(i, c):
        return pltpu.make_async_copy(made[i].at[part(c)], outs[i].at[part(c)], out_sem.at[i, c])

    def apart(c):
        return pltpu.make_async_copy(made[-1].at[part(c)], pieces[c], out_sem.at[n_out, c])

    for c in range(chunks):
        for i in range(n_in):
            arrival(i, c).start()
    def each(c, of_chunk, many):
        if not many:
            of_chunk(c)
            return
        for known in range(chunks):

            @pl.when(c == known)
            def _(known=known):
                of_chunk(known)

    def body(c, totals):
        for i in range(n_in):
            each(c, lambda c, i=i: arrival(i, c).wait(), len(ins[i]) > 1)
        where = pl.ds(pl.multiple_of(c * size, size), size)
        results, adds = fn([r[where, :] for r in held], [r[...] for r in consts])
        for i, value in enumerate(results):
            made[i][where, :] = value
        if split:
            each(c, lambda c: apart(c).start(), True)
        for i in range(n_out):
            departure(i, c).start()
        return tuple(t + a for t, a in zip(totals, adds))

    totals = lax.fori_loop(0, chunks, body, tuple(jnp.zeros(r.shape, F32) for r in sums))
    for ref, t in zip(sums, totals):
        ref[...] = t
    for c in range(chunks):
        if split:
            apart(c).wait()
        for i in range(n_out):
            departure(i, c).wait()


def by_rows(name, fn, ins, arrived, consts, kinds, sums=(), chunks=2, split=0):
    near = len(ins)
    ins = (*ins, *arrived)
    dims = ins[0].shape
    flat = [v if isinstance(v, tuple) else (v,) for v in ins]
    return pl.pallas_call(
        functools.partial(
            rows_kernel, fn, [len(v) for v in flat], len(consts), len(kinds), chunks, split
        ),
        in_specs=[HBM] * near
        + [ANY] * sum(len(v) for v in flat[near:])
        + [VMEM] * len(consts),
        out_specs=[HBM] * (len(kinds) + split) + [VMEM] * len(sums),
        out_shape=[shape(dims, k) for k in kinds]
        + [shape((dims[0] // chunks, dims[1]), kinds[-1])] * split
        + [shape(d, F32) for d in sums],
        scratch_shapes=[pltpu.VMEM(dims, v[0].dtype) for v in flat]
        + [pltpu.VMEM(dims, k) for k in kinds]
        + [
            pltpu.SemaphoreType.DMA((len(ins), chunks)),
            pltpu.SemaphoreType.DMA((len(kinds) + 1, chunks)),
        ],
        compiler_params=room(24),
        name=name,
        cost_estimate=cost(0.01),
    )(*[part for v in flat for part in v], *consts)


def out_kernel(om, ox, wm, wx, own, other, omv, oxv, wmv, wxv, ownv, otherv, sems):
    rows = own.shape[0]
    copies = [
        pltpu.make_async_copy(src, dst, sems.at[i])
        for i, (src, dst) in enumerate(((om, omv), (ox, oxv), (wm, wmv), (wx, wxv)))
    ]
    for copy in copies:
        copy.start()
    for copy in copies:
        copy.wait()
    leave = [
        pltpu.make_async_copy(made, out, sems.at[4 + i])
        for i, (made, out) in enumerate(((otherv, other), (ownv, own)))
    ]

    def body(i, carry):
        where = pl.ds(pl.multiple_of((1 - i) * rows, rows), rows)
        part = (nn(omv[:, where].T, wmv[...]) + nn(oxv[:, where].T, wxv[...])).astype(BF16)
        for c, (made, copy) in enumerate(zip((otherv, ownv), leave)):

            @pl.when(i == c)
            def _(made=made, copy=copy):
                made[...] = part
                copy.start()

        return carry

    lax.fori_loop(0, 2, body, 0)
    for copy in leave:
        copy.wait()


def out_projection(om, ox, wm, wx):
    cols, both = om.shape
    width = wm.shape[1]
    made = (both // 2, width)
    return pl.pallas_call(
        out_kernel,
        in_specs=[HBM, ANY, HBM, ANY],
        out_specs=[HBM] * 2,
        out_shape=[shape(made, BF16)] * 2,
        scratch_shapes=[pltpu.VMEM(v.shape, BF16) for v in (om, ox, wm, wx)]
        + [pltpu.VMEM(made, BF16)] * 2
        + [pltpu.SemaphoreType.DMA((6,))],
        compiler_params=room(24),
        name="out_projection",
        cost_estimate=cost(0.01),
    )(om, ox, wm, wx)


def middle_rows(held, consts):
    tokens, own, got = (v.astype(F32) for v in held)
    h1 = tokens + (own + got)
    scale = lax.rsqrt(jnp.mean(h1 * h1, axis=-1, keepdims=True) + eps_norm)
    return (h1, (h1 * scale * consts[0]).astype(BF16)), ()


def middle(tokens, own, got, gain):
    return by_rows("middle", middle_rows, (tokens, own), (got,), (gain,), (F32, BF16), split=2)


def mlp_kernel(at, aliased, na, nb, ya, yb, w, *refs):
    ma, mb, da, db, hid_o, dgu_o, nv, yv, wv, mv, dv, hv, gv, in_sem, w_sem, out_sem = refs[aliased:]
    rows, units = na.shape[0], hv.shape[1]
    arrivals, departures = [], []
    for c, (n, y, m, d) in enumerate(((na, ya, ma, da), (nb, yb, mb, db))):
        part, place = pl.ds(c * rows, rows), pl.ds(at, rows)
        arrivals += [
            pltpu.make_async_copy(n, nv.at[part], in_sem.at[0, c]),
            pltpu.make_async_copy(y.at[place], yv.at[part], in_sem.at[1, c]),
        ]
        departures.append(
            [
                pltpu.make_async_copy(dv.at[part], d, out_sem.at[0, c]),
                pltpu.make_async_copy(mv.at[part], m.at[place], out_sem.at[1, c]),
                pltpu.make_async_copy(hv.at[part], hid_o.at[part], out_sem.at[2, c]),
                pltpu.make_async_copy(gv.at[part], dgu_o.at[part], out_sem.at[3, c]),
            ]
        )
    weights = [
        pltpu.make_async_copy(
            w.at[:, pl.ds(j * units, units)], wv.at[:, pl.ds(j * units, units)], w_sem.at[j]
        )
        for j in range(3)
    ]
    for copy in weights + arrivals:
        copy.start()
    for copy in weights + arrivals:
        copy.wait()
    wg, wu, wd = (wv.at[:, pl.ds(j * units, units)] for j in range(3))
    tile = rows if rows < 512 else 512

    def body(i, carry):
        part = pl.ds(pl.multiple_of(i * tile, tile), tile)
        n2 = nv[part, :]
        gate, up = nn(n2, wg[...]), nn(n2, wu[...])
        dhid = nn(yv[part, :], wd[...])
        square = gate * gate
        share = 0.5 * jnp.tanh(gate * (ROOT + ROOT * 0.044715 * square)) + 0.5
        value = gate * share
        slope = share + value * (1.0 - share) * (2.0 * ROOT + 6.0 * ROOT * 0.044715 * square)
        dgate = (dhid * up * slope).astype(BF16)
        dup = (dhid * value).astype(BF16)
        hidden = (value * up).astype(BF16)
        dv[part, :] = (nt(dgate, wg[...]) + nt(dup, wu[...])).astype(BF16)
        hv[part, :] = hidden
        gv[part, 0:units] = dgate
        gv[part, units : 2 * units] = dup
        mv[part, :] = nt(hidden, wd[...]).astype(BF16)
        for c, copies in enumerate(departures):

            @pl.when(i == c * rows // tile)
            def _(copies=copies):
                for copy in copies:
                    copy.start()

        return carry

    lax.fori_loop(0, 2 * rows // tile, body, 0)
    for copies in departures:
        for copy in copies:
            copy.wait()


def mlp_both(na, nb, ya, yb, weights, at=0, into=(), mib=32):
    rows, width = na.shape
    units = weights.shape[1] // 3
    both = 2 * rows
    return pl.pallas_call(
        functools.partial(mlp_kernel, at, len(into)),
        in_specs=[ANY] * 4 + [HBM] * (1 + len(into)),
        out_specs=[HBM] * 6,
        out_shape=[shape(ya.shape, BF16)] * 2
        + [shape((rows, width), BF16)] * 2
        + [shape((both, units), BF16), shape((both, 2 * units), BF16)],
        scratch_shapes=[
            pltpu.VMEM((both, width), BF16),
            pltpu.VMEM((both, width), BF16),
            pltpu.VMEM(weights.shape, BF16),
            pltpu.VMEM((both, width), BF16),
            pltpu.VMEM((both, width), BF16),
            pltpu.VMEM((both, units), BF16),
            pltpu.VMEM((both, 2 * units), BF16),
            pltpu.SemaphoreType.DMA((2, 2)),
            pltpu.SemaphoreType.DMA((3,)),
            pltpu.SemaphoreType.DMA((4, 2)),
        ],
        input_output_aliases={5 + i: i for i in range(len(into))},
        compiler_params=room(mib),
        name="mlp",
        cost_estimate=cost(8),
    )(na, nb, ya, yb, weights, *into)


def mlp_weights_kernel(order, n_in, *refs):
    ins, (out, *held, total, made, sems, sem) = refs[:n_in], refs[n_in:]
    copies = []
    for group, moves in enumerate(order):
        for which, start, rows, at in moves:
            copy = pltpu.make_async_copy(
                ins[which].at[pl.ds(start, rows)], held[group].at[pl.ds(at, rows)], sems.at[len(copies)]
            )
            copies.append((at + rows, copy))
    size = held[0].shape[0] // 2
    copies.sort(key=lambda v: v[0])
    for _, copy in copies:
        copy.start()
    wide = held[2].shape[1]

    def body(i, carry):
        for c in range(2):

            @pl.when(i == c)
            def _(c=c):
                for end, copy in copies:
                    if c * size < end <= (c + 1) * size:
                        copy.wait()

        rows = pl.ds(pl.multiple_of(i * size, size), size)
        n2, dy, dgu, hidden = (r[rows, :] for r in held)
        for at, left, right in ((0, n2, dgu), (wide, dy, hidden)):
            cols = pl.ds(at, right.shape[1])
            new = nn(left.T, right) + total[:, cols]
            total[:, cols] = new
            made[:, cols] = new.astype(BF16)
        return carry

    total[...] = jnp.zeros(total.shape, F32)
    lax.fori_loop(0, 2, body, 0)
    leave = pltpu.make_async_copy(made, out, sem)
    leave.start()
    leave.wait()


def mlp_weights(n2, dy, dgu, hidden):
    ins = (*n2, *dy, *dgu, *hidden)
    rows = n2[0].shape[0]
    half = rows // 2
    first = [(0, 0, rows, 0), (1, 0, rows, rows)]
    order = [
        first + [(2, 0, half, 2 * rows), (4, 0, half, 2 * rows + half), (3, 0, half, 3 * rows), (5, 0, half, 3 * rows + half)],
        [(6 + j, 0, rows, j * rows) for j in range(4)],
    ]
    for base in (10, 13):
        order.append(
            [
                (base, 0, 2 * rows, 0),
                (base + 1, 0, half, 2 * rows),
                (base + 2, 0, half, 2 * rows + half),
                (base + 1, half, half, 3 * rows),
                (base + 2, half, half, 3 * rows + half),
            ]
        )
    width = n2[0].shape[1]
    dims = (width, dgu[0].shape[1] + hidden[0].shape[1])
    return pl.pallas_call(
        functools.partial(mlp_weights_kernel, order, len(ins)),
        in_specs=[HBM] * len(ins),
        out_specs=HBM,
        out_shape=shape(dims, BF16),
        scratch_shapes=[
            pltpu.VMEM((4 * rows, v.shape[1]), BF16) for v in (n2[0], dy[0], dgu[0], hidden[0])
        ]
        + [
            pltpu.VMEM(dims, F32),
            pltpu.VMEM(dims, BF16),
            pltpu.SemaphoreType.DMA((sum(len(v) for v in order),)),
            pltpu.SemaphoreType.DMA,
        ],
        compiler_params=room(48),
        name="mlp_weights",
        cost_estimate=cost(10),
    )(*ins)


def middle_back_rows(held, consts):
    dy, h1, *shares = (v.astype(F32) for v in held)
    dn2 = sum(shares[1:], shares[0])
    scale = lax.rsqrt(jnp.mean(h1 * h1, axis=-1, keepdims=True) + eps_norm)
    hat = dn2 * consts[0]
    dh1 = (
        dy
        + scale * hat
        - h1 * (scale * scale * scale) * jnp.mean(hat * h1, axis=-1, keepdims=True)
    )
    return (dh1, dh1.astype(BF16)), (folded(dn2 * h1 * scale),)


def middle_back(dy, h1, a, b, c, gain):
    return by_rows(
        "middle_back",
        middle_back_rows,
        (dy, h1, a),
        (b, c),
        (gain,),
        (F32, BF16),
        sums=((FOLD, dy.shape[1]),),
    )


def out_back_kernel(own, other, wm, wx, om, ox, dm_o, dx_o, gm_o, gx_o, *scratch):
    refs = (own, other, wm, wx, om, ox)
    held, made, sems = scratch[:6], scratch[6:10], scratch[10]
    copies = [pltpu.make_async_copy(src, dst, sems.at[i]) for i, (src, dst) in enumerate(zip(refs, held))]
    for copy in copies:
        copy.start()
    ownv, otherv, wmv, wxv, omv, oxv = held
    dm, dx, gm, gx = made
    rows = own.shape[0]
    for copy in copies:
        copy.wait()
    leave = [
        pltpu.make_async_copy(src, dst, sems.at[6 + i])
        for i, (src, dst) in enumerate(((dx, dx_o), (dm, dm_o), (gx, gx_o), (gm, gm_o)))
    ]
    for i, (w, out) in enumerate(((wxv, dx), (wmv, dm))):
        for at, ref in ((0, ownv), (rows, otherv)):
            out[:, at : at + rows] = nt(w[...], ref[...]).astype(BF16)
        leave[i].start()
    gx[...] = (nn(oxv[:, :rows], ownv[...]) + nn(oxv[:, rows:], otherv[...])).astype(BF16)
    leave[2].start()
    gm[...] = nn(omv[:, :rows], ownv[...]) + nn(omv[:, rows:], otherv[...])
    leave[3].start()
    for copy in leave:
        copy.wait()


def out_back(own, other, wm, wx, om, ox):
    cols, both = om.shape
    width = own.shape[1]
    ins = (own, other, wm, wx, om, ox)
    outs = [
        ((cols, both), BF16),
        ((cols, both), BF16),
        ((cols, width), F32),
        ((cols, width), BF16),
    ]
    return pl.pallas_call(
        out_back_kernel,
        in_specs=[HBM, ANY, HBM, ANY, HBM, ANY],
        out_specs=[HBM] * 4,
        out_shape=[shape(*v) for v in outs],
        scratch_shapes=[pltpu.VMEM(v.shape, BF16) for v in ins]
        + [pltpu.VMEM(*v) for v in outs]
        + [pltpu.SemaphoreType.DMA((10,))],
        compiler_params=room(24),
        name="out_back",
        cost_estimate=cost(0.01),
    )(*ins)


def rows_back_kernel(dk, dq, dv, wt, a_o, b_o):
    rows = a_o.shape[0]

    def body(i, carry):
        where = pl.ds(pl.multiple_of(i * rows, rows), rows)
        grads = jnp.concatenate([dk[:, where], dq[:, where], dv[:, where]], axis=0)
        part = nn(grads.T, wt[...]).astype(BF16)
        for c, ref in enumerate((a_o, b_o)):

            @pl.when(i == c)
            def _(ref=ref):
                ref[...] = part

        return carry

    lax.fori_loop(0, 2, body, 0)


def rows_back(dk, dq, dv, wt):
    cols, both = dq.shape
    width = wt.shape[1]
    return pl.pallas_call(
        rows_back_kernel,
        out_shape=[shape((both // 2, width), BF16)] * 2,
        compiler_params=room(24),
        name="rows_back",
        cost_estimate=cost(0.01),
    )(dk, dq, dv, wt)


def last_rows(held, consts):
    x, dh1, *shares = (v.astype(F32) for v in held)
    dn1 = sum(shares[1:], shares[0])
    scale = lax.rsqrt(jnp.mean(x * x, axis=-1, keepdims=True) + eps_norm)
    hat = dn1 * consts[0]
    out = (
        dh1
        + scale * hat
        - x * (scale * scale * scale) * jnp.mean(hat * x, axis=-1, keepdims=True)
    )
    return (out.astype(BF16),), ()


def last(tokens, dh1, a, b, c, gain):
    return by_rows("last", last_rows, (tokens, dh1, a), (b, c), (gain,), (BF16,))[0]


def grads_sum_kernel(count, *refs):
    ins, outs, gains_o = refs[:count], refs[count:-1], refs[-1]
    rows, cols = outs[0].shape
    total = ins[0][0:rows, :].astype(F32)
    for ref in ins[1:]:
        total = total + ref[0:rows, :].astype(F32)
    for j, ref in enumerate(outs):
        ref[...] = total[:, j * cols : (j + 1) * cols]
    tail = [ref[rows : rows + EXTRA, :].astype(F32) for ref in ins]
    gains = tail[0]
    for part in tail[1:]:
        gains = gains + part
    gains = gains[0:4, :] + gains[4:8, :]
    gains_o[...] = jnp.concatenate(
        [gains[0:1, :] + gains[1:2, :], gains[2:3, :] + gains[3:4, :]], axis=0
    )


def grads_sum(parts):
    rows, width = parts[0].shape
    rows -= EXTRA
    return pl.pallas_call(
        functools.partial(grads_sum_kernel, len(parts)),
        out_shape=[shape((rows, width // 4), F32)] * 4 + [shape((2, width), F32)],
        compiler_params=room(16),
        name="grads_sum",
        cost_estimate=cost(0.01),
    )(*parts)


def local(
    dp,
    mp,
    tokens,
    w_query,
    w_key,
    w_value,
    w_out,
    w_gate,
    w_up,
    w_down,
    norm_attn,
    norm_mlp,
    valid_counts,
    group_ids,
    cotangent,
):
    me, row = lax.axis_index("mp"), lax.axis_index("dp")
    cols = w_query.shape[1]
    length = group_ids.shape[1]

    def core(v):
        return lax.ppermute(v, "mp", [(i, i ^ 1) for i in range(mp)])

    def across(v):
        return lax.ppermute(v, "mp", [(i, i ^ 2) for i in range(mp)])

    def core_across(v):
        return lax.ppermute(v, "mp", [(i, i ^ 3) for i in range(mp)])

    def far(v, k):
        return lax.ppermute(v, "dp", [(i, i ^ k) for i in range(dp)])

    def after(v, *others):
        return lax.optimization_barrier((v, *others))[0]

    def summed(a, b):
        return (a.astype(F32) + b.astype(F32)).astype(BF16)

    direct = dp <= DIRECT
    gain_a, gain_m = norm_attn[None], norm_mlp[None]

    gq = group_ids
    flat = group_ids[0]
    valid = valid_counts[0]
    tiles = flat.reshape(length // BLK, BLK)
    low = jnp.sum(flat[None, :] < tiles[:, :1], axis=1) // BLK
    high = jnp.minimum(jnp.sum(flat[None, :] <= tiles[:, -1:], axis=1), valid)
    high = (high + BLK - 1) // BLK
    head = jnp.stack([me, row, valid, valid, valid, valid, valid, valid])
    sc = jnp.concatenate([head, low, high]).astype(jnp.int32)
    keyed = jnp.where(jnp.arange(length, dtype=jnp.int32) < valid, flat, -1)
    gkv = jnp.broadcast_to(keyed[:, None], (length, 128))

    tok2 = across(tokens)
    w_attn = jnp.concatenate([w_key, w_query, w_value, w_out], axis=1)
    w_mlp = jnp.concatenate([w_gate, w_up, w_down], axis=1)
    if direct:
        near = [w_attn] + [far(w_attn, k) for k in range(2, dp, 2)]
        middle_way = len(near) // 2
        near[middle_way] = after(near[middle_way], sc, gkv, w_mlp)
        w_pieces = [p for v in near for p in (v, far(v, 1))]
        tok1 = core(after(tokens, w_pieces[1]))
    else:
        w_pieces = [lax.all_gather(w_attn, "dp", axis=0, tiled=True)]
        tok1 = core(tokens)
    w_mlp = lax.all_gather(w_mlp, "dp", axis=0, tiled=True)
    tok3 = core(after(tok2, *w_pieces[1::2]))

    n1, qkvt, kn, vn, wt, wo = qkv(sc, (tokens, tok1, tok2, tok3), gain_a, w_pieces, cols)
    wo_x = across(wo)
    dy0 = cotangent
    dy2 = across(after(cotangent, tok2))
    dy1 = core(after(cotangent, tok3))

    o_far, lse_far = attention(1, sc, qkvt, kn, gq, gkv)
    o_x = across(after(o_far, dy2, wo_x))
    dy3 = core(after(dy2, o_far))
    o_own, lse_own = attention(0, after(sc, o_far), qkvt, kn, gq, gkv)
    p_own, p_other = out_projection(o_own, o_x, wo, wo_x)
    h1, n2, n2_a, n2_b = middle(tokens, p_own, core(p_other), gain_m)

    half = n2.shape[0] // 2
    n2_1 = core(n2)
    far_a = across(n2_a)
    far_b = across(n2_b)
    m0, m1, d0, d1, hid_o, dgu_o = mlp_both(n2, n2_1, dy0, dy1, w_mlp, mib=60)
    side_a = core(after(far_a, d0))
    m2, m3, d2a, d3a, hid_a, dgu_a = mlp_both(far_a, side_a, dy2, dy3, w_mlp)
    dsum_a = summed(d2a, core(d3a))
    dx_a = across(dsum_a)
    side_b = core(after(far_b, d2a))
    far_b = after(far_b, dsum_a)
    m2, m3, d2b, d3b, hid_b, dgu_b = mlp_both(far_b, side_b, dy2, dy3, w_mlp, half, (m2, m3))

    d_sum = summed(d2b, core(after(d3b, dx_a)))
    dx_b = across(d_sum)
    mlp_all = mlp_weights(
        (n2, n2_1, far_a, side_a, far_b, side_b),
        (dy0, dy1, dy2, dy3),
        (dgu_o, dgu_a, dgu_b),
        (after(hid_o, d_sum), hid_a, hid_b),
    )
    mlp_grads = lax.psum_scatter(mlp_all, "dp", scatter_dimension=0, tiled=True)
    m_other, m_core = core(m3), core(after(m1, d_sum))
    dh1, da, gain_m_part = middle_back(
        dy0,
        h1,
        d0,
        core(after(d1, d_sum)),
        (dx_a, after(dx_b, mlp_all, m_other, m_core)),
        gain_m,
    )

    do_own, do_send, go, go_send = out_back(da, core(da), wo, wo_x, o_own, o_x)
    do_far = across(do_send)
    go_x = across(go_send)
    m_x = across(after(summed(after(m2, da), m_other), do_send))
    dq_own, dk, dv = first_back(sc, qkvt, kn, vn, do_own, o_own, lse_own, gq, gkv)
    r2, r3, dk_own, dv_own, *grads = second_back(
        dp if direct else 1,
        sc, qkvt, kn, vn, do_far, o_far, lse_far, gq, gkv,
        dk, dv, dq_own, go, go_x, gain_a, gain_m_part, n1, wt,
    )
    r_sum = summed(r2, core(after(r3, m_x)))
    r_x = across(r_sum)
    depth = w_query.shape[0]
    parts = []
    if direct:
        for k in range(dp - 2, 0, -2):
            sent = grads[k + 1]
            if k < dp // 2 and parts:
                sent = after(sent, parts[-1])
            near, other = grads[k], after(far(sent, 1), r_sum)
            both = summed(near[:depth], other[:depth])
            part = jnp.concatenate([both, near[depth : depth + 4], other[depth : depth + 4]], axis=0)
            parts.insert(0, part)
        last_sent = after(grads[1], parts[0]) if parts else grads[1]
        parts = [far(part, 2 * k + 2) for k, part in enumerate(parts)]
        parts = [grads[0], far(last_sent, 1)] + parts
    r0, r1 = rows_back(after(dk_own, r_sum), dq_own, dv_own, wt)
    output = (
        h1 + (m0.astype(F32) + m_core.astype(F32) + after(m_x, r_sum).astype(F32))
    ).astype(BF16)
    units = w_gate.shape[1]
    grad_gate, grad_up, grad_down = (
        mlp_grads[:, j * units : (j + 1) * units].astype(F32) for j in range(3)
    )
    grad_tokens = last(tokens, after(dh1, output, grad_gate), r0, core(r1), r_x, gain_a)
    if direct:
        parts[0] = after(parts[0], grad_tokens)
        grad_k, grad_q, grad_v, grad_o, gains = grads_sum(parts)
        gains = gains + core(gains) + across(gains) + core_across(gains)
    else:
        width = tokens.shape[1]
        attn_grads = lax.psum_scatter(
            grads[0][:width], "dp", scatter_dimension=0, tiled=True
        ).astype(F32)
        grad_k, grad_q, grad_v, grad_o = jnp.split(attn_grads, 4, axis=1)
        extra = grads[0][width : width + 4].astype(F32)
        gains = lax.psum(extra[0::2] + extra[1::2], ("dp", "mp"))

    return (
        output,
        grad_tokens,
        grad_q,
        grad_k,
        grad_v,
        grad_o,
        grad_gate,
        grad_up,
        grad_down,
        gains[0],
        gains[1],
    )


def solution(mesh):
    rows, weight = P(("dp", "mp"), None), P("dp", "mp")
    return jax.shard_map(
        functools.partial(local, mesh.shape["dp"], mesh.shape["mp"]),
        mesh=mesh,
        in_specs=(rows,) + (weight,) * 7 + (P(), P(), P("dp"), P("dp", None), rows),
        out_specs=(rows, rows) + (weight,) * 7 + (P(), P()),
        check_vma=False,
    )
```
